128 devices in a mesh: rows: 32 (over x, z, core), lev: 4 (over y).
Axes of the slice: x: 4, y: 4, z: 4, core: 2. Of those that a mesh axis runs over, the one named last changes fastest.
Arguments:
- source: float32 [2048, 16, 2048], P('rows', 'lev'), may hold values from -40 to 40
- solid: int32 [256, 16, 32], P('rows', 'lev'), may hold values 0 or 1
- couplings: float32 [17], replicated, may hold values from 2 to 8
Outputs:
- pressure: float32 [2048, 16, 2048], P('rows', 'lev')
The draws below stay inside these ranges and needn't reach their ends.
Inputs may be any that keep to these rules, and one draw needn't show every extreme that they name: Each entry is 0 or 1; 1 marks a block of 8 x 64 cells of one level inside a solid.
All inputs are finite; a program needn't handle non-finite values.
Results may differ from the reference program's by a relative error of at most 0.0001.
Values sent between devices are 32-bit elements; how exact they have to be, the bound alone decides.
No kernel may reach another device: no remote copies, remote signals or barrier semaphores. Data moves between devices by JAX's collectives and lax.ppermute only.
A program may use at most 128 MiB of HBM per device.

```python
import math
import jax
import jax.numpy as jnp
from jax import lax

NX = 2048
NY = 2048
BY = 8
BX = 64
NZ = 16


def touch_ends(values, key, low, largest):
    extent = values.shape
    place = [jax.random.randint(jax.random.fold_in(key, axis), (), 0, extent[axis]) for axis in range(len(extent))]
    values = values.at[tuple(place)].set(low)
    longest = extent.index(max(extent))
    place[longest] = (place[longest] + 1) % extent[longest]
    return values.at[tuple(place)].set(largest)


def steps_of(own_key, dims, split, smallest, largest):
    level, own = 1.0, jax.random.fold_in(own_key, 6)
    for axis_at, shards_of in split:
        steps = jnp.exp(jax.random.uniform(jax.random.fold_in(own, axis_at), (shards_of,), jnp.float32, smallest / len(split), largest / len(split)))
        level = level * jnp.repeat(steps, dims[axis_at] // shards_of).reshape([-1 if axis == axis_at else 1 for axis in range(len(dims))])
    return level


def normal_values(key, extent, spread, limit, cuts=(), kind=jnp.bfloat16):
    entries = jax.random.normal(key, extent, jnp.float32) * spread
    if len(cuts) > 0:
        entries = steps_of(key, extent, cuts, -0.22, 0.18) * entries
    return jnp.clip(entries, min=-limit, max=limit).astype(kind)


def setup_inputs(seed: int = 0) -> dict:
    key_of = jax.random.split(jax.random.key(seed), 4)
    return {
        "source": normal_values(key_of[0], (NY, NZ, NX), 8.0, 40.0, ((0, 32), (1, 4)), jnp.float32),
        "solid": touch_ends((jax.random.randint(key_of[1], (NY // BY, NZ, NX // BX), 0, 4) < 1).astype(jnp.int32), jax.random.fold_in(key_of[1], 1), 0, 1),
        "couplings": jnp.clip(jnp.exp(jax.random.uniform(key_of[2], (NZ + 1,), jnp.float32, math.log(2.0), math.log(8.0))), 2.0, 8.0),
    }


full_turn = 2.0 * math.pi

def eigenvalue(length):
    slots = jnp.arange(length, dtype=jnp.int32)
    frequency = jnp.where(slots <= length // 2, slots, slots - length // 2)
    return 2.0 - 2.0 * jnp.cos(frequency.astype(jnp.float32) * (full_turn / length))

def weights_for(length):
    slots = jnp.arange(length, dtype=jnp.int32)
    edge = (slots == 0) | (slots == length // 2)
    return jnp.where(edge, math.sqrt(1.0 / length), math.sqrt(2.0 / length)).astype(jnp.float32)

def forward_last(values):
    length = values.shape[-1]
    half_len = length // 2
    spectral = jnp.fft.rfft(values, axis=-1)
    real_part = jnp.real(spectral)
    imag_part = jnp.imag(spectral)
    packed = jnp.concatenate([real_part[..., :half_len + 1], -imag_part[..., 1:half_len]], -1)
    return (packed * weights_for(length)).astype(jnp.float32)

def inverse_last(packed):
    length = packed.shape[-1]
    half_len = length // 2
    scaled = packed / weights_for(length)
    real_part = scaled[..., :half_len + 1]
    blank = jnp.zeros(packed.shape[:-1] + (1,), jnp.float32)
    imag_part = jnp.concatenate([blank, -scaled[..., half_len + 1:], blank], -1)
    return jnp.fft.irfft(lax.complex(real_part, imag_part), n=length, axis=-1).astype(jnp.float32)

def reference(source, solid, couplings):
    keep_cells = (1 - solid).astype(jnp.float32)
    horizontal = eigenvalue(NY)[:, None] + eigenvalue(NX)[None, :]
    zero_plane = jnp.zeros((NY, NX), jnp.float32)

    def forward(carry, level):
        ratio_prev, partial_prev = carry
        cells = lax.dynamic_index_in_dim(source, level, 1, keepdims=False)
        keep_level = lax.dynamic_index_in_dim(keep_cells, level, 1, keepdims=False)
        cells = (cells.reshape(NY // BY, BY, NX // BX, BX) * keep_level[:, None, :, None]).reshape(NY, NX)
        spectral = forward_last(forward_last(cells).T).T
        lower_w = couplings[level]
        upper_w = couplings[level + 1]
        inverse = 1.0 / (horizontal + lower_w + upper_w - lower_w * ratio_prev)
        ratio = upper_w * inverse
        partial_value = (spectral + lower_w * partial_prev) * inverse
        return ((ratio, partial_value), (ratio, partial_value))
    unused, (ratios, partials) = lax.scan(forward, (zero_plane, zero_plane), jnp.arange(NZ, dtype=jnp.int32))

    def backward(upper_values, slices):
        ratio, partial_value = slices
        current = partial_value + ratio * upper_values
        cells = inverse_last(inverse_last(current.T).T)
        return (current, cells)
    unused, levels = lax.scan(backward, zero_plane, (ratios, partials), reverse=True)
    return jnp.moveaxis(levels, 0, 1)
```

```python
import math

import jax
import jax.numpy as jnp
import ml_dtypes
import numpy as np
from jax import lax
from jax.experimental import pallas as pl
from jax.experimental.pallas import tpu as pltpu
from jax.sharding import PartitionSpec as P

F32 = jnp.float32
BF16 = jnp.bfloat16
BY = 8
BX = 64
N = 2048
LANES = 128
NZ = 16
TURN = 2.0 * math.pi
RESIDUES = (1, 5, 9, 13, 2, 10, 4)
SWEEPS = 7


def split_host(table):
    table = np.asarray(table, np.float32)
    high = table.astype(ml_dtypes.bfloat16)
    low = (table - high.astype(np.float32)).astype(ml_dtypes.bfloat16)
    return high, low


def host_tables():
    b = np.arange(LANES)
    m = np.arange(LANES)
    angle = TURN * np.mod(np.outer(b, m), LANES) / LANES
    scale = math.sqrt(2.0 / N)
    cos, sin = scale * np.cos(angle), scale * np.sin(angle)
    full = np.block([[cos, -sin], [sin, cos]])
    edge = np.zeros((2 * LANES, 2 * LANES))
    freq0 = np.concatenate([np.arange(65), np.arange(1, 64)])
    angle0 = TURN * np.mod(np.outer(b, freq0), LANES) / LANES
    part = np.where(np.arange(LANES)[None, :] < 65, np.cos(angle0), -np.sin(angle0)) * scale
    part[:, 0] *= math.sqrt(0.5)
    part[:, 64] *= math.sqrt(0.5)
    edge[:LANES, :LANES] = part
    freq8 = 16 * np.arange(64) + 8
    angle8 = TURN * np.mod(np.outer(b, freq8), N) / N
    edge[LANES:, LANES:] = scale * np.concatenate([np.cos(angle8), -np.sin(angle8)], 1)
    q = np.array(RESIDUES)
    twist = TURN * np.outer(q, b) / N
    twiddle = np.zeros((16, LANES), np.float32)
    twiddle[:7] = np.cos(twist)
    twiddle[8:15] = np.sin(twist)
    freqs = [np.concatenate([16 * freq0, freq8, freq8])]
    for residue in RESIDUES:
        freqs.append(np.tile(16 * m + residue, 2))
    freqs = np.concatenate(freqs)
    eigen = (4.0 * np.sin(np.pi * freqs / N) ** 2).astype(np.float32).reshape(8, 256)
    spread = (np.arange(32)[:, None] == np.arange(N)[None, :] // BX).astype(ml_dtypes.bfloat16)
    return full, edge, twiddle, eigen, spread


def halves(value):
    high = value.astype(BF16)
    return high, (value - high.astype(F32)).astype(BF16)


def mm(left, right):
    return jnp.dot(left, right, preferred_element_type=F32)


def mm3(left, right):
    return mm(left[0], right[0]) + (mm(left[1], right[0]) + mm(left[0], right[1]))


def cmul(value, cos, sin):
    re, im = value
    return re * cos + im * sin, im * cos - re * sin


def cadd(left, right):
    return left[0] + right[0], left[1] + right[1]


def csub(left, right):
    return left[0] - right[0], left[1] - right[1]


def phase(steps):
    return math.cos(TURN * steps / 16), math.sin(TURN * steps / 16)


def real16(v):
    s = [v[a] + v[a + 8] for a in range(8)]
    d = [v[a] - v[a + 8] for a in range(8)]
    u = [(d[0], -d[4])]
    for a in range(1, 4):
        u.append(cmul((d[a], -d[a + 4]), *phase(a)))
    p02, m02 = cadd(u[0], u[2]), csub(u[0], u[2])
    p13, m13 = cadd(u[1], u[3]), csub(u[1], u[3])
    y1, y9 = cadd(p02, p13), csub(p02, p13)
    y5 = (m02[0] + m13[1], m02[1] - m13[0])
    y13 = (m02[0] - m13[1], m02[1] + m13[0])
    t = [s[a] + s[a + 4] for a in range(4)]
    e = [s[a] - s[a + 4] for a in range(4)]
    z1 = cmul((e[1], -e[3]), *phase(2))
    z0 = (e[0], -e[2])
    y2, y10 = cadd(z0, z1), csub(z0, z1)
    a0, a1 = t[0] + t[2], t[1] + t[3]
    y4 = (t[0] - t[2], t[3] - t[1])
    return (a0 + a1, a0 - a1), (y1, y5, y9, y13, y2, y10, y4)


def real16_back(real, comps):
    g1, g5, g9, g13, g2, g10, g4 = comps
    a0, a1 = real[0] + real[1], real[0] - real[1]
    t = [a0 + g4[0], a1 - g4[1], a0 - g4[0], a1 + g4[1]]
    z0 = cadd(g2, g10)
    cos, sin = phase(2)
    z1 = cmul(csub(g2, g10), cos, -sin)
    e = [z0[0], z1[0], -z0[1], -z1[1]]
    s = [t[a] + e[a] for a in range(4)] + [t[a] - e[a] for a in range(4)]
    p19, m19 = cadd(g1, g9), csub(g1, g9)
    p513, m513 = cadd(g5, g13), csub(g5, g13)
    u = [cadd(p19, p513), None, csub(p19, p513), None]
    u[1] = (m19[0] - m513[1], m19[1] + m513[0])
    u[3] = (m19[0] + m513[1], m19[1] - m513[0])
    d = [None] * 8
    for a in range(4):
        cos, sin = phase(a)
        z = u[a] if a == 0 else cmul(u[a], cos, -sin)
        d[a], d[a + 4] = z[0], -z[1]
    return [s[a] + d[a] for a in range(8)] + [s[a] - d[a] for a in range(8)]


YB = 16


def forward_x_kernel(src, keep, spread, twiddle, fh, fl, eh, el, out, hi, lo):
    masks = mm(keep[...].reshape(keep.shape[0] * keep.shape[1], keep.shape[2]).astype(BF16), spread[...])
    levels = src.shape[1]
    for z in range(levels):
        rows = []
        for a in range(16):
            piece = src[:, z, a * LANES : (a + 1) * LANES]
            mask = masks[:, a * LANES : (a + 1) * LANES]
            pieces = [
                piece[8 * i : 8 * i + 8] * mask[i * levels + z : i * levels + z + 1]
                for i in range(YB // 8)
            ]
            rows.append(jnp.concatenate(pieces, 0))
        real, comps = real16(rows)
        blocks = [real]
        for i in range(7):
            blocks.append(cmul(comps[i], twiddle[i : i + 1, :], twiddle[8 + i : 9 + i, :]))
        for i in range(8):
            for part in range(2):
                high, low = halves(blocks[i][part])
                at = pl.ds((i * levels + z) * YB, YB)
                cols = pl.ds(part * LANES, LANES)
                hi[at, cols] = high
                lo[at, cols] = low
    rows = levels * YB
    first = mm3((hi[:rows, :], lo[:rows, :]), (eh[...], el[...]))
    rest = mm3((hi[rows:, :], lo[rows:, :]), (fh[...], fl[...]))
    for i in range(8):
        value = first if i == 0 else rest[(i - 1) * rows : i * rows]
        out[i // 2, :, :, (i % 2) * 256 : (i % 2) * 256 + 256] = value.reshape(levels, YB, 256)


def forward_x(source, keep, consts):
    rows, levels, cells = source.shape
    spread, twiddle, fh, fl, eh, el = consts
    full2 = lambda shape: pl.BlockSpec(shape, lambda i: (0, 0))
    return pl.pallas_call(
        forward_x_kernel,
        grid=(rows // YB,),
        in_specs=[
            pl.BlockSpec((YB, levels, cells), lambda i: (i, 0, 0)),
            pl.BlockSpec((YB // BY, levels, cells // BX), lambda i: (i, 0, 0)),
            full2(spread.shape),
            full2(twiddle.shape),
        ]
        + [full2((256, 256))] * 4,
        out_specs=pl.BlockSpec((4, levels, YB, 512), lambda i: (0, 0, i, 0)),
        out_shape=jax.ShapeDtypeStruct((4, levels, rows, 512), F32),
        scratch_shapes=[pltpu.VMEM((8 * levels * YB, 256), BF16)] * 2,
        name="forward_x",
    )(source, keep, spread, twiddle, fh, fl, eh, el)


def inverse_x_kernel(spec, twiddle, fh, fl, eh, el, out, hi, lo):
    levels = spec.shape[1]
    rows = levels * YB
    for i in range(8):
        value = spec[i // 2, :, :, (i % 2) * 256 : (i % 2) * 256 + 256].reshape(rows, 256)
        high, low = halves(value)
        hi[i * rows : (i + 1) * rows, :] = high
        lo[i * rows : (i + 1) * rows, :] = low
    first = mm3((hi[:rows, :], lo[:rows, :]), (eh[...], el[...]))
    rest = mm3((hi[rows:, :], lo[rows:, :]), (fh[...], fl[...]))
    for z in range(levels):
        real = (first[z * YB : (z + 1) * YB, :LANES], first[z * YB : (z + 1) * YB, LANES:])
        comps = []
        for i in range(7):
            at = i * rows + z * YB
            value = (rest[at : at + YB, :LANES], rest[at : at + YB, LANES:])
            comps.append(cmul(value, twiddle[i : i + 1, :], -twiddle[8 + i : 9 + i, :]))
        cells = real16_back(real, comps)
        for a in range(16):
            out[:, z, a * LANES : (a + 1) * LANES] = cells[a]


def inverse_x(spec, consts):
    sections, levels, rows, _ = spec.shape
    twiddle, fh, fl, eh, el = consts
    full2 = lambda shape: pl.BlockSpec(shape, lambda i: (0, 0))
    return pl.pallas_call(
        inverse_x_kernel,
        grid=(rows // YB,),
        in_specs=[
            pl.BlockSpec((4, levels, YB, 512), lambda i: (0, 0, i, 0)),
            full2(twiddle.shape),
        ]
        + [full2((256, 256))] * 4,
        out_specs=pl.BlockSpec((YB, levels, N), lambda i: (i, 0, 0)),
        out_shape=jax.ShapeDtypeStruct((rows, levels, N), F32),
        scratch_shapes=[pltpu.VMEM((8 * levels * YB, 256), BF16)] * 2,
        name="inverse_x",
    )(spec, twiddle, fh, fl, eh, el)


def eigen_kernel(coup, lam, w2h, w2l, w4h, w4l):
    sub = lax.broadcasted_iota(jnp.int32, (8, LANES), 0)
    lane = lax.broadcasted_iota(jnp.int32, (8, LANES), 1)
    top = jnp.zeros((8, LANES), F32)
    bottom = jnp.zeros((8, LANES), F32)
    for i in range(NZ):
        row = jnp.where(lane == i, coup[i] + coup[i + 1], 0.0)
        if i > 0:
            row = row - jnp.where(lane == i - 1, coup[i], 0.0)
        if i < NZ - 1:
            row = row - jnp.where(lane == i + 1, coup[i + 1], 0.0)
        row = row + jnp.where(lane == NZ + i, 1.0, 0.0)
        if i < 8:
            top = jnp.where(sub == i, row, top)
        else:
            bottom = jnp.where(sub == i - 8, row, bottom)
    near, far = lane == sub, lane == sub + 8
    both = jnp.logical_or(near, far)
    low_half = lane < 8
    square = lane < NZ

    def pick(mask, value):
        return jnp.where(mask, value, 0.0)

    def angle(p, q, a):
        d = q - p
        root = jnp.sqrt(d * d + 4.0 * a * a)
        t = 2.0 * a / (jnp.abs(d) + root + 1e-30)
        t = jnp.where(d >= 0.0, t, -t)
        w = 1.0 + t * t
        c = lax.rsqrt(w)
        c = c * (1.5 - 0.5 * w * c * c)
        return c, t * c

    def partner(value):
        return jnp.where(low_half, pltpu.roll(value, LANES - 8, 1), pltpu.roll(value, 8, 1))

    def shuffle(value):
        right = pltpu.roll(value, 1, 1)
        left = pltpu.roll(value, LANES - 1, 1)
        out = jnp.where(lane < 8, right, left)
        out = jnp.where(lane == 1, pltpu.roll(value, LANES - 7, 1), out)
        out = jnp.where(lane == 15, pltpu.roll(value, 8, 1), out)
        return jnp.where(jnp.logical_or(lane == 0, lane >= NZ), value, out)

    def step(_, carry):
        top, bottom = carry
        c_s, s_s = angle(
            jnp.sum(pick(near, top), 1, keepdims=True),
            jnp.sum(pick(far, bottom), 1, keepdims=True),
            jnp.sum(pick(far, top), 1, keepdims=True),
        )
        one = jnp.broadcast_to(jnp.sum(pick(both, top), 0, keepdims=True), (8, LANES))
        two = jnp.broadcast_to(jnp.sum(pick(both, bottom), 0, keepdims=True), (8, LANES))
        p = jnp.where(low_half, one, pltpu.roll(one, 8, 1))
        q = jnp.where(low_half, pltpu.roll(two, LANES - 8, 1), two)
        a = jnp.where(low_half, pltpu.roll(one, LANES - 8, 1), one)
        c_l, s_l = angle(p, q, a)
        c_l = jnp.where(square, c_l, 1.0)
        s_l = jnp.where(low_half, -s_l, jnp.where(square, s_l, 0.0))
        t1 = top * c_l + partner(top) * s_l
        b1 = bottom * c_l + partner(bottom) * s_l
        t1, b1 = shuffle(t1), shuffle(b1)
        t2 = c_s * t1 - s_s * b1
        b2 = s_s * t1 + c_s * b1
        new_top = jnp.where(
            sub == 0, t2, jnp.where(sub == 1, pltpu.roll(b2, 1, 0), pltpu.roll(t2, 1, 0))
        )
        new_bottom = jnp.where(sub == 7, t2, pltpu.roll(b2, 7, 0))
        return new_top, new_bottom

    top, bottom = lax.fori_loop(0, 15 * SWEEPS, step, (top, bottom))
    lam[...] = jnp.concatenate(
        [
            jnp.broadcast_to(jnp.sum(pick(near, top), 1, keepdims=True), (8, LANES)),
            jnp.broadcast_to(jnp.sum(pick(far, bottom), 1, keepdims=True), (8, LANES)),
        ],
        0,
    )
    rows = jnp.concatenate([top, bottom], 0)
    rows = jnp.concatenate([rows] * 8, 0)
    src = lax.broadcasted_iota(jnp.int32, (LANES, LANES), 0)
    dst = lax.broadcasted_iota(jnp.int32, (LANES, LANES), 1)
    expand = (src == dst // 8 + NZ).astype(F32)
    wide = jnp.dot(rows, expand, precision=lax.Precision.HIGHEST, preferred_element_type=F32)
    w2 = jnp.where(src // NZ == dst % 8, wide, 0.0)
    w2h[...], w2l[...] = halves(w2)
    w4h[...], w4l[...] = halves(w2.T)


def eigen(couplings):
    matrix = jax.ShapeDtypeStruct((LANES, LANES), BF16)
    return pl.pallas_call(
        eigen_kernel,
        in_specs=[pl.BlockSpec(memory_space=pltpu.SMEM)],
        out_shape=[jax.ShapeDtypeStruct((NZ, LANES), F32), matrix, matrix, matrix, matrix],
        name="level_modes",
    )(couplings)


def decay(lam, e):
    half = 0.5 * (lam + e)
    root = jnp.sqrt(half * (2.0 + half))
    return 1.0 / (1.0 + half + root), 0.5 / root


def level_kernel(at, x, wh, wl, lam, eig, f, ends):
    h = pl.program_id(0)
    rows = x.shape[1]
    w = (wh[...], wl[...])
    e = eig[pl.ds(at[0] * 2 + h, 1), :]
    r, _ = decay(lam[:, 0:1], e)
    for o in range(rows // 8):
        block = x[:, 8 * o : 8 * o + 8, :].reshape(LANES, 256)
        value = mm3(w, halves(block))
        f[8 * o : 8 * o + 8, :, :] = value.reshape(8, NZ, 256)
    up = jnp.zeros((NZ, 256), F32)
    down = jnp.zeros((NZ, 256), F32)
    for y in range(rows):
        up = f[y] + r * up
        down = f[rows - 1 - y] + r * down
    ends[:, 0, :] = up[:, :LANES]
    ends[:, 1, :] = up[:, LANES:]
    ends[:, 2, :] = down[:, :LANES]
    ends[:, 3, :] = down[:, LANES:]


def level_transform(at, x, wh, wl, lam, eig):
    _, rows, width = x.shape
    whole = lambda shape: pl.BlockSpec(shape, lambda h, at: (0,) * len(shape))
    return pl.pallas_call(
        level_kernel,
        grid_spec=pltpu.PrefetchScalarGridSpec(
            num_scalar_prefetch=1,
            grid=(width // 256,),
            in_specs=[
                pl.BlockSpec((NZ, rows, 256), lambda h, at: (0, 0, h)),
                whole((LANES, LANES)),
                whole((LANES, LANES)),
                whole((NZ, LANES)),
                whole((8, 256)),
            ],
            out_specs=[
                pl.BlockSpec((rows, NZ, 256), lambda h, at: (0, 0, h)),
                pl.BlockSpec((NZ, 4, LANES), lambda h, at: (h, 0, 0)),
            ],
        ),
        out_shape=[
            jax.ShapeDtypeStruct((rows, NZ, width), F32),
            jax.ShapeDtypeStruct((2 * NZ, 4, LANES), F32),
        ],
        name="level_transform",
    )(at, x, wh, wl, lam, eig)


def carry_kernel(at, ends, lam, eig, out):
    sections = ends.shape[0]
    j = at[1]
    k = lax.rem(j, NZ)
    h = lax.div(j, NZ)
    e = eig[pl.ds(at[0] * 2 + h, 1), :]
    r, _ = decay(lam[pl.ds(k, 1), 0:1], e)
    for _ in range(6):
        r = r * r
    row = lax.broadcasted_iota(jnp.int32, (4, LANES), 0)
    ratio = jnp.where(lax.rem(row, 2) == 0, r[:, :LANES], r[:, LANES:])
    whole = ratio
    for _ in range(5):
        whole = whole * whole
    scale = 1.0 / (1.0 - whole)
    up = jnp.zeros((4, LANES), F32)
    down = jnp.zeros((4, LANES), F32)
    for s in range(sections):
        up = ends[s] + ratio * up
        down = ends[sections - 1 - s] + ratio * down
    up = up * scale
    down = down * scale
    first = row < 2
    ups = []
    for s in range(sections):
        ups.append(up)
        up = ends[s] + ratio * up
    for s in reversed(range(sections)):
        out[s] = jnp.where(first, ups[s], down)
        down = ends[s] + ratio * down


def carries(at, ends, lam, eig):
    return pl.pallas_call(
        carry_kernel,
        in_specs=[pl.BlockSpec(memory_space=pltpu.SMEM)] + [pl.BlockSpec(memory_space=pltpu.VMEM)] * 3,
        out_shape=jax.ShapeDtypeStruct(ends.shape, F32),
        name="section_carries",
    )(at, ends, lam, eig)


def solve_kernel(at, f, ends, wh, wl, lam, eig, out, work):
    h = pl.program_id(0)
    rows = f.shape[0]
    w = (wh[...], wl[...])
    e = eig[pl.ds(at[0] * 2 + h, 1), :]
    r, gain = decay(lam[:, 0:1], e)
    up = jnp.concatenate([ends[:, 0, :], ends[:, 1, :]], 1)
    down = jnp.concatenate([ends[:, 2, :], ends[:, 3, :]], 1)
    for y in range(rows):
        up = r * up
        work[y] = up
        up = up + f[y]
    for y in reversed(range(rows)):
        down = f[y] + r * down
        work[y] = (work[y] + down) * gain
    for o in range(rows // 8):
        block = work[8 * o : 8 * o + 8].reshape(LANES, 256)
        value = mm3(w, halves(block))
        out[:, 8 * o : 8 * o + 8, :] = value.reshape(NZ, 8, 256)


def solve(at, f, ends, wh, wl, lam, eig):
    rows, _, width = f.shape
    whole = lambda shape: pl.BlockSpec(shape, lambda h, at: (0,) * len(shape))
    return pl.pallas_call(
        solve_kernel,
        grid_spec=pltpu.PrefetchScalarGridSpec(
            num_scalar_prefetch=1,
            grid=(width // 256,),
            in_specs=[
                pl.BlockSpec((rows, NZ, 256), lambda h, at: (0, 0, h)),
                pl.BlockSpec((NZ, 4, LANES), lambda h, at: (h, 0, 0)),
                whole((LANES, LANES)),
                whole((LANES, LANES)),
                whole((NZ, LANES)),
                whole((8, 256)),
            ],
            out_specs=pl.BlockSpec((NZ, rows, 256), lambda h, at: (0, 0, h)),
            scratch_shapes=[pltpu.VMEM((rows, NZ, 256), F32)],
        ),
        out_shape=jax.ShapeDtypeStruct((NZ, rows, width), F32),
        name="solve_columns",
    )(at, f, ends, wh, wl, lam, eig)


def body(source, solid, couplings):
    rows, levels, _ = source.shape
    full, edge, twiddle, eig, spread = host_tables()
    fh, fl = split_host(full)
    eh, el = split_host(edge)
    fth, ftl = split_host(full.T)
    eth, etl = split_host(edge.T)
    keep = (1 - solid).astype(F32)
    at = jnp.stack([lax.axis_index("lev"), lax.axis_index("rows")]).astype(jnp.int32)
    lam, w2h, w2l, w4h, w4l = eigen(couplings)
    spectral = forward_x(source, keep, (spread, twiddle, fh, fl, eh, el))
    gathered = lax.all_to_all(spectral, "lev", 0, 0, tiled=True)
    f, ends = level_transform(at, gathered.reshape(NZ, rows, 512), w2h, w2l, lam, eig)
    ends = lax.all_to_all(ends, "rows", 0, 0, tiled=True)
    ends = carries(at, ends, lam, eig)
    ends = lax.all_to_all(ends, "rows", 0, 0, tiled=True)
    pressure = solve(at, f, ends, w4h, w4l, lam, eig)
    back = lax.all_to_all(pressure.reshape(4, levels, rows, 512), "lev", 0, 0, tiled=True)
    return inverse_x(back, (twiddle, fth, ftl, eth, etl))


def solution(mesh):
    return jax.shard_map(
        body,
        mesh=mesh,
        in_specs=(P("rows", "lev", None), P("rows", "lev", None), P()),
        out_specs=P("rows", "lev", None),
        check_vma=False,
    )
```

```python
import math

import jax
import jax.numpy as jnp
import ml_dtypes
import numpy as np
from jax import lax
from jax.experimental import pallas as pl
from jax.experimental.pallas import tpu as pltpu
from jax.sharding import PartitionSpec as P

F32 = jnp.float32
BF16 = jnp.bfloat16
BY = 8
BX = 64
N = 2048
LANES = 128
NZ = 16
TURN = 2.0 * math.pi
RESIDUES = (1, 5, 9, 13, 2, 10, 4)
SWEEPS = 7


def split_host(table):
    table = np.asarray(table, np.float32)
    high = table.astype(ml_dtypes.bfloat16)
    low = (table - high.astype(np.float32)).astype(ml_dtypes.bfloat16)
    return high, low


def host_tables():
    b = np.arange(LANES)
    m = np.arange(LANES)
    angle = TURN * np.mod(np.outer(b, m), LANES) / LANES
    scale = math.sqrt(2.0 / N)
    cos, sin = scale * np.cos(angle), scale * np.sin(angle)
    full = np.block([[cos, -sin], [sin, cos]])
    edge = np.zeros((2 * LANES, 2 * LANES))
    freq0 = np.concatenate([np.arange(65), np.arange(1, 64)])
    angle0 = TURN * np.mod(np.outer(b, freq0), LANES) / LANES
    part = np.where(np.arange(LANES)[None, :] < 65, np.cos(angle0), -np.sin(angle0)) * scale
    part[:, 0] *= math.sqrt(0.5)
    part[:, 64] *= math.sqrt(0.5)
    edge[:LANES, :LANES] = part
    freq8 = 16 * np.arange(64) + 8
    angle8 = TURN * np.mod(np.outer(b, freq8), N) / N
    edge[LANES:, LANES:] = scale * np.concatenate([np.cos(angle8), -np.sin(angle8)], 1)
    q = np.array(RESIDUES)
    twist = TURN * np.outer(q, b) / N
    twiddle = np.zeros((16, LANES), np.float32)
    twiddle[:7] = np.cos(twist)
    twiddle[8:15] = np.sin(twist)
    freqs = [np.concatenate([16 * freq0, freq8, freq8])]
    for residue in RESIDUES:
        freqs.append(np.tile(16 * m + residue, 2))
    freqs = np.concatenate(freqs)
    eigen = (4.0 * np.sin(np.pi * freqs / N) ** 2).astype(np.float32).reshape(8, 256)
    spread = (np.arange(32)[:, None] == np.arange(N)[None, :] // BX).astype(ml_dtypes.bfloat16)
    return full, edge, twiddle, eigen, spread


def halves(value):
    high = value.astype(BF16)
    return high, (value - high.astype(F32)).astype(BF16)


def mm(left, right):
    return jnp.dot(left, right, preferred_element_type=F32)


def mm3(left, right):
    return mm(left[0], right[0]) + (mm(left[1], right[0]) + mm(left[0], right[1]))


def cmul(value, cos, sin):
    re, im = value
    return re * cos + im * sin, im * cos - re * sin


def cadd(left, right):
    return left[0] + right[0], left[1] + right[1]


def csub(left, right):
    return left[0] - right[0], left[1] - right[1]


def phase(steps):
    return math.cos(TURN * steps / 16), math.sin(TURN * steps / 16)


def real16(v):
    s = [v[a] + v[a + 8] for a in range(8)]
    d = [v[a] - v[a + 8] for a in range(8)]
    u = [(d[0], -d[4])]
    for a in range(1, 4):
        u.append(cmul((d[a], -d[a + 4]), *phase(a)))
    p02, m02 = cadd(u[0], u[2]), csub(u[0], u[2])
    p13, m13 = cadd(u[1], u[3]), csub(u[1], u[3])
    y1, y9 = cadd(p02, p13), csub(p02, p13)
    y5 = (m02[0] + m13[1], m02[1] - m13[0])
    y13 = (m02[0] - m13[1], m02[1] + m13[0])
    t = [s[a] + s[a + 4] for a in range(4)]
    e = [s[a] - s[a + 4] for a in range(4)]
    z1 = cmul((e[1], -e[3]), *phase(2))
    z0 = (e[0], -e[2])
    y2, y10 = cadd(z0, z1), csub(z0, z1)
    a0, a1 = t[0] + t[2], t[1] + t[3]
    y4 = (t[0] - t[2], t[3] - t[1])
    return (a0 + a1, a0 - a1), (y1, y5, y9, y13, y2, y10, y4)


def real16_back(real, comps):
    g1, g5, g9, g13, g2, g10, g4 = comps
    a0, a1 = real[0] + real[1], real[0] - real[1]
    t = [a0 + g4[0], a1 - g4[1], a0 - g4[0], a1 + g4[1]]
    z0 = cadd(g2, g10)
    cos, sin = phase(2)
    z1 = cmul(csub(g2, g10), cos, -sin)
    e = [z0[0], z1[0], -z0[1], -z1[1]]
    s = [t[a] + e[a] for a in range(4)] + [t[a] - e[a] for a in range(4)]
    p19, m19 = cadd(g1, g9), csub(g1, g9)
    p513, m513 = cadd(g5, g13), csub(g5, g13)
    u = [cadd(p19, p513), None, csub(p19, p513), None]
    u[1] = (m19[0] - m513[1], m19[1] + m513[0])
    u[3] = (m19[0] + m513[1], m19[1] - m513[0])
    d = [None] * 8
    for a in range(4):
        cos, sin = phase(a)
        z = u[a] if a == 0 else cmul(u[a], cos, -sin)
        d[a], d[a + 4] = z[0], -z[1]
    return [s[a] + d[a] for a in range(8)] + [s[a] - d[a] for a in range(8)]


YB = 16


def forward_x_kernel(src, keep, spread, twiddle, fh, fl, eh, el, out, hi, lo):
    open_cells = (1 - keep[...]).astype(F32).astype(BF16)
    masks = mm(open_cells.reshape(keep.shape[0] * keep.shape[1], keep.shape[2]), spread[...])
    levels = src.shape[1]
    for z in range(levels):
        rows = []
        for a in range(16):
            piece = src[:, z, a * LANES : (a + 1) * LANES]
            mask = masks[:, a * LANES : (a + 1) * LANES]
            pieces = [
                piece[8 * i : 8 * i + 8] * mask[i * levels + z : i * levels + z + 1]
                for i in range(YB // 8)
            ]
            rows.append(jnp.concatenate(pieces, 0))
        real, comps = real16(rows)
        blocks = [real]
        for i in range(7):
            blocks.append(cmul(comps[i], twiddle[i : i + 1, :], twiddle[8 + i : 9 + i, :]))
        for i in range(8):
            for part in range(2):
                high, low = halves(blocks[i][part])
                at = pl.ds((i * levels + z) * YB, YB)
                cols = pl.ds(part * LANES, LANES)
                hi[at, cols] = high
                lo[at, cols] = low
    rows = levels * YB
    first = mm3((hi[:rows, :], lo[:rows, :]), (eh[...], el[...]))
    rest = mm3((hi[rows:, :], lo[rows:, :]), (fh[...], fl[...]))
    for i in range(8):
        value = first if i == 0 else rest[(i - 1) * rows : i * rows]
        out[i // 2, :, :, (i % 2) * 256 : (i % 2) * 256 + 256] = value.reshape(levels, YB, 256)


def forward_x(source, keep, consts):
    rows, levels, cells = source.shape
    spread, twiddle, fh, fl, eh, el = consts
    full2 = lambda shape: pl.BlockSpec(shape, lambda i: (0, 0))
    return pl.pallas_call(
        forward_x_kernel,
        grid=(rows // YB,),
        in_specs=[
            pl.BlockSpec((YB, levels, cells), lambda i: (i, 0, 0)),
            pl.BlockSpec((YB // BY, levels, cells // BX), lambda i: (i, 0, 0)),
            full2(spread.shape),
            full2(twiddle.shape),
        ]
        + [full2((256, 256))] * 4,
        out_specs=pl.BlockSpec((4, levels, YB, 512), lambda i: (0, 0, i, 0)),
        out_shape=jax.ShapeDtypeStruct((4, levels, rows, 512), F32),
        scratch_shapes=[pltpu.VMEM((8 * levels * YB, 256), BF16)] * 2,
        name="forward_x",
    )(source, keep, spread, twiddle, fh, fl, eh, el)


def eigen_kernel(coup, lam, modes, w2h, w2l, w4h, w4l):
    sub = lax.broadcasted_iota(jnp.int32, (8, LANES), 0)
    lane = lax.broadcasted_iota(jnp.int32, (8, LANES), 1)
    top = jnp.zeros((8, LANES), F32)
    bottom = jnp.zeros((8, LANES), F32)
    for i in range(NZ):
        row = jnp.where(lane == i, coup[i] + coup[i + 1], 0.0)
        if i > 0:
            row = row - jnp.where(lane == i - 1, coup[i], 0.0)
        if i < NZ - 1:
            row = row - jnp.where(lane == i + 1, coup[i + 1], 0.0)
        row = row + jnp.where(lane == NZ + i, 1.0, 0.0)
        if i < 8:
            top = jnp.where(sub == i, row, top)
        else:
            bottom = jnp.where(sub == i - 8, row, bottom)
    near, far = lane == sub, lane == sub + 8
    both = jnp.logical_or(near, far)
    low_half = lane < 8
    square = lane < NZ

    def pick(mask, value):
        return jnp.where(mask, value, 0.0)

    def angle(p, q, a):
        d = q - p
        root = jnp.sqrt(d * d + 4.0 * a * a)
        t = 2.0 * a / (jnp.abs(d) + root + 1e-30)
        t = jnp.where(d >= 0.0, t, -t)
        w = 1.0 + t * t
        c = lax.rsqrt(w)
        c = c * (1.5 - 0.5 * w * c * c)
        return c, t * c

    def partner(value):
        return jnp.where(low_half, pltpu.roll(value, LANES - 8, 1), pltpu.roll(value, 8, 1))

    def shuffle(value):
        right = pltpu.roll(value, 1, 1)
        left = pltpu.roll(value, LANES - 1, 1)
        out = jnp.where(lane < 8, right, left)
        out = jnp.where(lane == 1, pltpu.roll(value, LANES - 7, 1), out)
        out = jnp.where(lane == 15, pltpu.roll(value, 8, 1), out)
        return jnp.where(jnp.logical_or(lane == 0, lane >= NZ), value, out)

    def step(_, carry):
        top, bottom = carry
        c_s, s_s = angle(
            jnp.sum(pick(near, top), 1, keepdims=True),
            jnp.sum(pick(far, bottom), 1, keepdims=True),
            jnp.sum(pick(far, top), 1, keepdims=True),
        )
        one = jnp.broadcast_to(jnp.sum(pick(both, top), 0, keepdims=True), (8, LANES))
        two = jnp.broadcast_to(jnp.sum(pick(both, bottom), 0, keepdims=True), (8, LANES))
        p = jnp.where(low_half, one, pltpu.roll(one, 8, 1))
        q = jnp.where(low_half, pltpu.roll(two, LANES - 8, 1), two)
        a = jnp.where(low_half, pltpu.roll(one, LANES - 8, 1), one)
        c_l, s_l = angle(p, q, a)
        c_l = jnp.where(square, c_l, 1.0)
        s_l = jnp.where(low_half, -s_l, jnp.where(square, s_l, 0.0))
        t1 = top * c_l + partner(top) * s_l
        b1 = bottom * c_l + partner(bottom) * s_l
        t1, b1 = shuffle(t1), shuffle(b1)
        t2 = c_s * t1 - s_s * b1
        b2 = s_s * t1 + c_s * b1
        new_top = jnp.where(
            sub == 0, t2, jnp.where(sub == 1, pltpu.roll(b2, 1, 0), pltpu.roll(t2, 1, 0))
        )
        new_bottom = jnp.where(sub == 7, t2, pltpu.roll(b2, 7, 0))
        return new_top, new_bottom

    top, bottom = lax.fori_loop(0, 15 * SWEEPS, step, (top, bottom))
    lam[...] = jnp.concatenate(
        [
            jnp.broadcast_to(jnp.sum(pick(near, top), 1, keepdims=True), (8, LANES)),
            jnp.broadcast_to(jnp.sum(pick(far, bottom), 1, keepdims=True), (8, LANES)),
        ],
        0,
    )
    rows = jnp.concatenate([top, bottom], 0)
    modes[...] = pltpu.roll(rows, LANES - NZ, 1)
    rows = jnp.concatenate([rows] * 8, 0)
    src = lax.broadcasted_iota(jnp.int32, (LANES, LANES), 0)
    dst = lax.broadcasted_iota(jnp.int32, (LANES, LANES), 1)
    expand = (src == dst // 8 + NZ).astype(F32)
    wide = jnp.dot(rows, expand, precision=lax.Precision.HIGHEST, preferred_element_type=F32)
    w2 = jnp.where(src // NZ == dst % 8, wide, 0.0)
    w2h[...], w2l[...] = halves(w2)
    w4 = w2.T
    w4h[...], w4l[...] = halves(jnp.concatenate([w4, w4], 0))


def eigen(couplings):
    matrix = jax.ShapeDtypeStruct((LANES, LANES), BF16)
    return pl.pallas_call(
        eigen_kernel,
        in_specs=[pl.BlockSpec(memory_space=pltpu.SMEM)],
        out_shape=[jax.ShapeDtypeStruct((NZ, LANES), F32)] * 2
        + [matrix] * 2
        + [jax.ShapeDtypeStruct((2 * LANES, LANES), BF16)] * 2,
        name="level_modes",
    )(couplings)


def decay(lam, e):
    half = 0.5 * (lam + e)
    root = jnp.sqrt(half * (2.0 + half))
    return 1.0 / (1.0 + half + root), 0.5 / root


def powers(base, count):
    square = base * base
    value = jnp.where((count & 1) != 0, base, 1.0)
    value = value * jnp.where((count & 2) != 0, square, 1.0)
    return value * jnp.where((count & 4) != 0, square * square, 1.0)


def inverse_x_kernel(
    at, spec0, spec1, spec2, spec3, ends, modes, lam, eig, twiddle, fh, fl, eh, el,
    out, hi, lo, above, below, eighth, steps,
):
    levels = spec0.shape[0]
    rows = levels * YB
    i = pl.program_id(0)
    blocks = 2 * pl.num_programs(0)

    @pl.when(i == 0)
    def _():
        b = lax.broadcasted_iota(jnp.int32, (8, LANES), 0)
        for t in range(16):
            l, h, p = t // 4, (t // 2) % 2, t % 2
            e = eig[t // 2 : t // 2 + 1, p * LANES : (p + 1) * LANES]
            r, gain = decay(lam[:, 0:1], e)
            gain = gain * r
            up = ends[h, :, l, p, :] * gain
            down = ends[h, :, l, 2 + p, :] * gain
            r2 = r * r
            r4 = r2 * r2
            eighth[t] = r4 * r4
            for k in range(NZ):
                base = jnp.broadcast_to(r[k : k + 1], (8, LANES))
                above[t, k] = powers(base, b) * up[k : k + 1]
                below[t, k] = powers(base, 7 - b) * down[k : k + 1]

    r8 = eighth[...]
    for o in range(2):
        steps[o] = powers(r8, 2 * i + o)
        steps[2 + o] = powers(r8, blocks - 1 - 2 * i - o)
    first_level = at[0] * levels
    for step, spec in enumerate((spec0, spec1, spec2, spec3)):
        l = (at[0] - step) & 3
        for part in range(4):
            t = 4 * l + part
            acc = [[None, None] for _ in range(levels)]
            for k in range(NZ):
                u, d = above[t, k], below[t, k]
                for o in range(2):
                    value = u * steps[o, t, k : k + 1, :] + d * steps[2 + o, t, k : k + 1, :]
                    for z in range(levels):
                        term = value * modes[k, first_level + z]
                        acc[z][o] = term if k == 0 else acc[z][o] + term
            for z in range(levels):
                value = spec[z, :, part * LANES : (part + 1) * LANES] + jnp.concatenate(acc[z], 0)
                high, low = halves(value)
                place = pl.multiple_of((2 * l + part // 2) * rows + z * YB, YB)
                half = pl.ds((part % 2) * LANES, LANES)
                hi[pl.ds(place, YB), half] = high
                lo[pl.ds(place, YB), half] = low
    first = mm3((hi[:rows, :], lo[:rows, :]), (eh[...], el[...]))
    rest = mm3((hi[rows:, :], lo[rows:, :]), (fh[...], fl[...]))
    for z in range(levels):
        real = (first[z * YB : (z + 1) * YB, :LANES], first[z * YB : (z + 1) * YB, LANES:])
        comps = []
        for i in range(7):
            place = i * rows + z * YB
            value = (rest[place : place + YB, :LANES], rest[place : place + YB, LANES:])
            comps.append(cmul(value, twiddle[i : i + 1, :], -twiddle[8 + i : 9 + i, :]))
        cells = real16_back(real, comps)
        for a in range(16):
            out[:, z, a * LANES : (a + 1) * LANES] = cells[a]


def inverse_x(at, specs, ends, modes, lam, eig, consts):
    levels, rows, _ = specs[0].shape
    twiddle, fh, fl, eh, el = consts
    whole = lambda value: pl.BlockSpec(value.shape, lambda i, at: (0,) * value.ndim)
    return pl.pallas_call(
        inverse_x_kernel,
        grid_spec=pltpu.PrefetchScalarGridSpec(
            num_scalar_prefetch=1,
            grid=(rows // YB,),
            in_specs=[pl.BlockSpec((levels, YB, 512), lambda i, at: (0, i, 0))] * 4
            + [
                whole(ends),
                pl.BlockSpec(memory_space=pltpu.SMEM),
                whole(lam),
                whole(eig),
                whole(twiddle),
            ]
            + [whole(fh)] * 4,
            out_specs=pl.BlockSpec((YB, levels, N), lambda i, at: (i, 0, 0)),
            scratch_shapes=[pltpu.VMEM((8 * levels * YB, 256), BF16)] * 2
            + [pltpu.VMEM((16, NZ, 8, LANES), F32)] * 2
            + [pltpu.VMEM((16, NZ, LANES), F32), pltpu.VMEM((4, 16, NZ, LANES), F32)],
        ),
        out_shape=jax.ShapeDtypeStruct((rows, levels, N), F32),
        name="inverse_x",
    )(at, *specs, ends, modes, lam, eig, twiddle, fh, fl, eh, el)


def level_kernel(at, x, w2h, w2l, w4h, w4l, lam, eig, out0, out1, out2, out3, ends, f, work):
    h = pl.program_id(0)
    rows = x.shape[1]
    w2 = (w2h[...], w2l[...])
    turned = pl.ds(pl.multiple_of(at[0] * 32, 32), LANES)
    w4 = (w4h[turned, :], w4l[turned, :])
    e = eig[pl.ds(at[0] * 2 + h, 1), :]
    r, gain = decay(lam[:, 0:1], e)
    for o in range(rows // 8):
        block = x[:, 8 * o : 8 * o + 8, :].reshape(LANES, 256)
        value = mm3(w2, halves(block))
        f[8 * o : 8 * o + 8, :, :] = value.reshape(8, NZ, 256)
    up = jnp.zeros((NZ, 256), F32)
    down = jnp.zeros((NZ, 256), F32)
    for y in range(rows):
        up = r * up
        work[y] = up
        up = up + f[y]
    for y in reversed(range(rows)):
        down = f[y] + r * down
        work[y] = (work[y] + down) * gain
    ends[:, 0, :] = up[:, :LANES]
    ends[:, 1, :] = up[:, LANES:]
    ends[:, 2, :] = down[:, :LANES]
    ends[:, 3, :] = down[:, LANES:]
    for o in range(rows // 8):
        block = work[8 * o : 8 * o + 8].reshape(LANES, 256)
        value = mm3(w4, halves(block))
        for step, out in enumerate((out0, out1, out2, out3)):
            out[:, 8 * o : 8 * o + 8, :] = value[32 * step : 32 * step + 32].reshape(4, 8, 256)


def level_solve(at, x, weights, lam, eig):
    _, rows, width = x.shape
    whole = lambda shape: pl.BlockSpec(shape, lambda h, at: (0,) * len(shape))
    field = pl.BlockSpec((NZ, rows, 256), lambda h, at: (0, 0, h))
    return pl.pallas_call(
        level_kernel,
        grid_spec=pltpu.PrefetchScalarGridSpec(
            num_scalar_prefetch=1,
            grid=(width // 256,),
            in_specs=[field]
            + [whole((LANES, LANES))] * 2
            + [whole((2 * LANES, LANES))] * 2
            + [whole((NZ, LANES)), whole((8, 256))],
            out_specs=[pl.BlockSpec((4, rows, 256), lambda h, at: (0, 0, h))] * 4
            + [pl.BlockSpec((NZ, 4, LANES), lambda h, at: (h, 0, 0))],
            scratch_shapes=[pltpu.VMEM((rows, NZ, 256), F32)] * 2,
        ),
        out_shape=[jax.ShapeDtypeStruct((4, rows, width), F32)] * 4
        + [jax.ShapeDtypeStruct((2 * NZ, 4, LANES), F32)],
        name="level_solve",
    )(at, x, *weights, lam, eig)


def carry_kernel(at, ends, lam, eig, out):
    sections = ends.shape[0]
    j = at[1]
    k = lax.rem(j, NZ)
    h = lax.div(j, NZ)
    e = eig[pl.ds(at[0] * 2 + h, 1), :]
    r, _ = decay(lam[pl.ds(k, 1), 0:1], e)
    for _ in range(6):
        r = r * r
    row = lax.broadcasted_iota(jnp.int32, (4, LANES), 0)
    ratio = jnp.where(lax.rem(row, 2) == 0, r[:, :LANES], r[:, LANES:])
    whole = ratio
    for _ in range(5):
        whole = whole * whole
    scale = 1.0 / (1.0 - whole)
    up = jnp.zeros((4, LANES), F32)
    down = jnp.zeros((4, LANES), F32)
    for s in range(sections):
        up = ends[s] + ratio * up
        down = ends[sections - 1 - s] + ratio * down
    up = up * scale
    down = down * scale
    first = row < 2
    ups = []
    for s in range(sections):
        ups.append(up)
        up = ends[s] + ratio * up
    for s in reversed(range(sections)):
        value = jnp.where(first, ups[s], down)
        for section in range(4):
            out[s, section] = value
        down = ends[s] + ratio * down


def carries(at, ends, lam, eig):
    return pl.pallas_call(
        carry_kernel,
        in_specs=[pl.BlockSpec(memory_space=pltpu.SMEM)] + [pl.BlockSpec(memory_space=pltpu.VMEM)] * 3,
        out_shape=jax.ShapeDtypeStruct((ends.shape[0], 4) + ends.shape[1:], F32),
        name="section_carries",
    )(at, ends, lam, eig)


def body(source, solid, couplings):
    rows, levels, _ = source.shape
    full, edge, twiddle, eig, spread = host_tables()
    fh, fl = split_host(full)
    eh, el = split_host(edge)
    fth, ftl = split_host(full.T)
    eth, etl = split_host(edge.T)
    at = jnp.stack([lax.axis_index("lev"), lax.axis_index("rows")]).astype(jnp.int32)
    lam, modes, w2h, w2l, w4h, w4l = eigen(couplings)
    spectral = forward_x(source, solid, (spread, twiddle, fh, fl, eh, el))
    gathered = lax.all_to_all(spectral, "lev", 0, 0, tiled=True)
    *parts, ends = level_solve(at, gathered.reshape(NZ, rows, 512), (w2h, w2l, w4h, w4l), lam, eig)
    specs = [parts[0]]
    for step in range(1, 4):
        specs.append(lax.ppermute(parts[step], "lev", [(i, (i + step) % 4) for i in range(4)]))
    ends = lax.all_to_all(ends, "rows", 0, 0, tiled=True)
    ends = carries(at, ends, lam, eig).reshape(128, 4, LANES)
    ends = lax.all_to_all(ends, ("rows", "lev"), 0, 0, tiled=True).reshape(2, NZ, 4, 4, LANES)
    return inverse_x(at, specs, ends, modes, lam, eig, (twiddle, fth, ftl, eth, etl))


def solution(mesh):
    return jax.shard_map(
        body,
        mesh=mesh,
        in_specs=(P("rows", "lev", None), P("rows", "lev", None), P()),
        out_specs=P("rows", "lev", None),
        check_vma=False,
    )
```

```python
import math

import jax
import jax.numpy as jnp
import ml_dtypes
import numpy as np
from jax import lax
from jax.experimental import pallas as pl
from jax.experimental.pallas import tpu as pltpu
from jax.sharding import PartitionSpec as P


F32 = jnp.float32
BF16 = jnp.bfloat16
BY = 8
BX = 64
N = 2048
LANES = 128
NZ = 16
TURN = 2.0 * math.pi
RESIDUES = (1, 5, 9, 13, 2, 10, 4)
SWEEPS = 12


def split_host(table):
    table = np.asarray(table, np.float32)
    high = table.astype(ml_dtypes.bfloat16)
    low = (table - high.astype(np.float32)).astype(ml_dtypes.bfloat16)
    return high, low


def host_tables():
    b = np.arange(LANES)
    m = np.arange(LANES)
    angle = TURN * np.mod(np.outer(b, m), LANES) / LANES
    scale = math.sqrt(2.0 / N)
    cos, sin = scale * np.cos(angle), scale * np.sin(angle)
    full = np.block([[cos, -sin], [sin, cos]])
    edge = np.zeros((2 * LANES, 2 * LANES))
    freq0 = np.concatenate([np.arange(65), np.arange(1, 64)])
    angle0 = TURN * np.mod(np.outer(b, freq0), LANES) / LANES
    part = np.where(np.arange(LANES)[None, :] < 65, np.cos(angle0), -np.sin(angle0)) * scale
    part[:, 0] *= math.sqrt(0.5)
    part[:, 64] *= math.sqrt(0.5)
    edge[:LANES, :LANES] = part
    freq8 = 16 * np.arange(64) + 8
    angle8 = TURN * np.mod(np.outer(b, freq8), N) / N
    edge[LANES:, LANES:] = scale * np.concatenate([np.cos(angle8), -np.sin(angle8)], 1)
    q = np.array(RESIDUES)
    twist = TURN * np.outer(q, b) / N
    twiddle = np.zeros((16, LANES), np.float32)
    twiddle[:7] = np.cos(twist)
    twiddle[8:15] = np.sin(twist)
    freqs = [np.concatenate([16 * freq0, freq8, freq8])]
    for residue in RESIDUES:
        freqs.append(np.tile(16 * m + residue, 2))
    freqs = np.concatenate(freqs)
    eigen = (4.0 * np.sin(np.pi * freqs / N) ** 2).astype(np.float32).reshape(8, 256)
    spread = (np.arange(32)[:, None] == np.arange(N)[None, :] // BX).astype(ml_dtypes.bfloat16)
    return full, edge, twiddle, eigen, spread


def halves(value):
    high = value.astype(BF16)
    return high, (value - high.astype(F32)).astype(BF16)


def mm(left, right):
    return jnp.dot(left, right, preferred_element_type=F32)


def mm3(left, right):
    return mm(left[0], right[0]) + (mm(left[1], right[0]) + mm(left[0], right[1]))


def cmul(value, cos, sin):
    re, im = value
    return re * cos + im * sin, im * cos - re * sin


def cadd(left, right):
    return left[0] + right[0], left[1] + right[1]


def csub(left, right):
    return left[0] - right[0], left[1] - right[1]


def phase(steps):
    return math.cos(TURN * steps / 16), math.sin(TURN * steps / 16)


def real16(v):
    s = [v[a] + v[a + 8] for a in range(8)]
    d = [v[a] - v[a + 8] for a in range(8)]
    u = [(d[0], -d[4])]
    for a in range(1, 4):
        u.append(cmul((d[a], -d[a + 4]), *phase(a)))
    p02, m02 = cadd(u[0], u[2]), csub(u[0], u[2])
    p13, m13 = cadd(u[1], u[3]), csub(u[1], u[3])
    y1, y9 = cadd(p02, p13), csub(p02, p13)
    y5 = (m02[0] + m13[1], m02[1] - m13[0])
    y13 = (m02[0] - m13[1], m02[1] + m13[0])
    t = [s[a] + s[a + 4] for a in range(4)]
    e = [s[a] - s[a + 4] for a in range(4)]
    z1 = cmul((e[1], -e[3]), *phase(2))
    z0 = (e[0], -e[2])
    y2, y10 = cadd(z0, z1), csub(z0, z1)
    a0, a1 = t[0] + t[2], t[1] + t[3]
    y4 = (t[0] - t[2], t[3] - t[1])
    return (a0 + a1, a0 - a1), (y1, y5, y9, y13, y2, y10, y4)


def real16_back(real, comps):
    g1, g5, g9, g13, g2, g10, g4 = comps
    a0, a1 = real[0] + real[1], real[0] - real[1]
    t = [a0 + g4[0], a1 - g4[1], a0 - g4[0], a1 + g4[1]]
    z0 = cadd(g2, g10)
    cos, sin = phase(2)
    z1 = cmul(csub(g2, g10), cos, -sin)
    e = [z0[0], z1[0], -z0[1], -z1[1]]
    s = [t[a] + e[a] for a in range(4)] + [t[a] - e[a] for a in range(4)]
    p19, m19 = cadd(g1, g9), csub(g1, g9)
    p513, m513 = cadd(g5, g13), csub(g5, g13)
    u = [cadd(p19, p513), None, csub(p19, p513), None]
    u[1] = (m19[0] - m513[1], m19[1] + m513[0])
    u[3] = (m19[0] + m513[1], m19[1] - m513[0])
    d = [None] * 8
    for a in range(4):
        cos, sin = phase(a)
        z = u[a] if a == 0 else cmul(u[a], cos, -sin)
        d[a], d[a + 4] = z[0], -z[1]
    return [s[a] + d[a] for a in range(8)] + [s[a] - d[a] for a in range(8)]


YB = 16


def forward_x_kernel(
    at, src, solid, spread, twiddle, fh, fl, eh, el, out0, out1, out2, out3, hi, lo, hi0, lo0
):
    levels = src.shape[1]
    rows = levels * YB
    open_cells = (1 - solid[...]).astype(F32).astype(BF16)
    masks = mm(open_cells.reshape(solid.shape[0] * levels, solid.shape[2]), spread[...])
    for z in range(levels):
        cells = []
        for a in range(16):
            piece = src[:, z, a * LANES : (a + 1) * LANES]
            mask = masks[:, a * LANES : (a + 1) * LANES]
            pieces = [
                piece[8 * i : 8 * i + 8] * mask[i * levels + z : i * levels + z + 1]
                for i in range(YB // 8)
            ]
            cells.append(jnp.concatenate(pieces, 0))
        real, comps = real16(cells)
        for part in range(2):
            high, low = halves(real[part])
            hi0[z * YB : (z + 1) * YB, part * LANES : (part + 1) * LANES] = high
            lo0[z * YB : (z + 1) * YB, part * LANES : (part + 1) * LANES] = low
        for i in range(1, 8):
            block = cmul(comps[i - 1], twiddle[i - 1 : i, :], twiddle[7 + i : 8 + i, :])
            slot = 2 * ((at[0] - i // 2) & 3) + i % 2
            place = pl.multiple_of(slot * rows + z * YB, YB)
            for part in range(2):
                high, low = halves(block[part])
                hi[pl.ds(place, YB), part * LANES : (part + 1) * LANES] = high
                lo[pl.ds(place, YB), part * LANES : (part + 1) * LANES] = low
    outs = (out0, out1, out2, out3)
    rest = mm3((hi[...], lo[...]), (fh[...], fl[...]))
    for step in range(4):
        for h in range(2):
            value = rest[(2 * step + h) * rows : (2 * step + h + 1) * rows]
            outs[step][:, :, h * 256 : h * 256 + 256] = value.reshape(levels, YB, 256)
    first = mm3((hi0[...], lo0[...]), (eh[...], el[...])).reshape(levels, YB, 256)
    for step in range(4):

        @pl.when(at[0] == step)
        def _(step=step):
            outs[step][:, :, 0:256] = first


def forward_x(at, source, solid, consts):
    rows, levels, cells = source.shape
    spread, twiddle, fh, fl, eh, el = consts
    whole = lambda value: pl.BlockSpec(value.shape, lambda i, at: (0,) * value.ndim)
    return pl.pallas_call(
        forward_x_kernel,
        grid_spec=pltpu.PrefetchScalarGridSpec(
            num_scalar_prefetch=1,
            grid=(rows // YB,),
            in_specs=[
                pl.BlockSpec((YB, levels, cells), lambda i, at: (i, 0, 0)),
                pl.BlockSpec((YB // BY, levels, cells // BX), lambda i, at: (i, 0, 0)),
            ]
            + [whole(value) for value in (spread, twiddle, fh, fl, eh, el)],
            out_specs=[pl.BlockSpec((levels, YB, 512), lambda i, at: (0, i, 0))] * 4,
            scratch_shapes=[pltpu.VMEM((8 * levels * YB, 256), BF16)] * 2
            + [pltpu.VMEM((levels * YB, 256), BF16)] * 2,
        ),
        out_shape=[jax.ShapeDtypeStruct((levels, rows, 512), F32)] * 4,
        name="forward_x",
    )(at, source, solid, spread, twiddle, fh, fl, eh, el)


def rsqrt(value):
    root = lax.rsqrt(value)
    return root * (1.5 - 0.5 * value * root * root)


def eigen_kernel(coup, lam, modes, w2h, w2l, w4h, w4l):
    sub = lax.broadcasted_iota(jnp.int32, (8, LANES), 0)
    lane = lax.broadcasted_iota(jnp.int32, (8, LANES), 1) & (NZ - 1)
    low = lane < 8
    g = [jnp.zeros((8, LANES), F32), jnp.zeros((8, LANES), F32)]
    link = jnp.zeros((8, LANES), F32)
    for k in range(NZ):
        pivot = coup[k] + coup[k + 1] - link * link
        inverse = rsqrt(pivot)
        here = lane == (k // 2 + 8 * (k % 2))
        g[k // 8] = jnp.where(here & (sub == k % 8), pivot * inverse, g[k // 8])
        link = -coup[k + 1] * inverse
        if k < NZ - 1:
            below = (k + 1) // 8
            g[below] = jnp.where(here & (sub == (k + 1) % 8), link, g[below])
    partners = [pltpu.roll(value, 8, 1) for value in g]

    def total(first, second):
        value = first + second
        for shift in (4, 2, 1):
            value = value + pltpu.roll(value, shift, 0)
        return value

    def right(value):
        return pltpu.roll(value, 1, 1)

    def left(value):
        return pltpu.roll(value, LANES - 1, 1)

    def step(_, carry):
        g0, g1, p0, p1, worst = carry
        own = total(g0 * g0, g1 * g1)
        other = total(p0 * p0, p1 * p1)
        a = total(g0 * p0, g1 * p1)
        d = other - own
        w = d * d + 4.0 * a * a
        h = rsqrt(w)
        x = 0.5 + 0.5 * jnp.abs(d) * h
        y = rsqrt(x)
        positive = (d > 0.0) | ((d == 0.0) & low)
        turn = a * h * y
        still = w == 0.0
        c = jnp.where(still, 1.0, x * y)
        turn = jnp.where(still, 0.0, jnp.where(positive, turn, -turn))
        worst = jnp.maximum(worst, jnp.where(still, 0.0, a * a / (own * other)))
        out = []
        for value, partner in ((g0, p0), (g1, p1)):
            mine = c * value - turn * partner
            theirs = c * partner + turn * value
            rising = right(jnp.where(lane == 0, theirs, mine))
            new = jnp.where(low, rising, jnp.where(lane == 15, theirs, left(mine)))
            new = jnp.where(lane == 0, mine, new)
            falling = right(jnp.where(lane == 8, mine, theirs))
            new_partner = jnp.where(low, jnp.where(lane == 7, mine, left(theirs)), falling)
            new_partner = jnp.where(lane == 8, theirs, new_partner)
            out.append((new, new_partner))
        return out[0][0], out[1][0], out[0][1], out[1][1], worst

    def sweep(carry):
        count, _, *state = carry
        state = lax.fori_loop(0, 15, step, (*state, jnp.zeros((8, LANES), F32)))
        return (count + 1, jnp.max(state[4]), *state[:4])

    def unfinished(carry):
        return (carry[0] < SWEEPS) & (carry[1] > 1e-7)

    state = (jnp.int32(0), jnp.float32(1.0), g[0], g[1], partners[0], partners[1])
    _, _, g0, g1, _, _ = lax.while_loop(unfinished, sweep, state)
    square = total(g0 * g0, g1 * g1)
    inverse = rsqrt(square)
    vectors = jnp.concatenate([g0 * inverse, g1 * inverse], 0)
    lam[...] = jnp.concatenate([square] * NZ, 0).T[:NZ]
    modes[...] = jnp.concatenate([vectors] * 8, 0).T[:NZ]
    wide = [jnp.broadcast_to(vectors[z : z + 1], (8, LANES)) for z in range(NZ)]
    row = lax.broadcasted_iota(jnp.int32, (LANES, LANES), 0)
    col = lax.broadcasted_iota(jnp.int32, (LANES, LANES), 1)
    for section in range(4):
        order = [wide[(z + 4 * section) % NZ] for z in range(NZ)]
        w4 = jnp.where(row % 8 == col // NZ, jnp.concatenate(order, 0), 0.0)
        w4h[section], w4l[section] = halves(w4)
        w2h[section], w2l[section] = halves(w4.T)


def eigen(couplings):
    table = jax.ShapeDtypeStruct((NZ, LANES), F32)
    matrix = jax.ShapeDtypeStruct((4, LANES, LANES), BF16)
    return pl.pallas_call(
        eigen_kernel,
        in_specs=[pl.BlockSpec(memory_space=pltpu.SMEM)],
        out_shape=[table, table, matrix, matrix, matrix, matrix],
        name="level_modes",
    )(couplings)


def decay(lam, e):
    half = 0.5 * (lam + e)
    root = jnp.sqrt(half * (2.0 + half))
    return 1.0 / (1.0 + half + root), 0.5 / root


def powers(base, count):
    square = base * base
    value = jnp.where((count & 1) != 0, base, 1.0)
    value = value * jnp.where((count & 2) != 0, square, 1.0)
    return value * jnp.where((count & 4) != 0, square * square, 1.0)


def inverse_x_kernel(
    at, spec0, spec1, spec2, spec3, ends, modes, lam, eig, twiddle, fh, fl, eh, el,
    out, hi, lo, above, below, eighth, steps,
):
    levels = spec0.shape[0]
    rows = levels * YB
    i = pl.program_id(0)
    blocks = 2 * pl.num_programs(0)

    @pl.when(i == 0)
    def _():
        b = lax.broadcasted_iota(jnp.int32, (8, LANES), 0)
        for t in range(16):
            l, h, p = t // 4, (t // 2) % 2, t % 2
            e = eig[t // 2 : t // 2 + 1, p * LANES : (p + 1) * LANES]
            r, gain = decay(lam[:, 0:1], e)
            gain = gain * r
            up = ends[h, :, l, p, :] * gain
            down = ends[h, :, l, 2 + p, :] * gain
            r2 = r * r
            r4 = r2 * r2
            eighth[t] = r4 * r4
            for k in range(NZ):
                base = jnp.broadcast_to(r[k : k + 1], (8, LANES))
                above[t, k] = powers(base, b) * up[k : k + 1]
                below[t, k] = powers(base, 7 - b) * down[k : k + 1]

    r8 = eighth[...]
    for o in range(2):
        steps[o] = powers(r8, 2 * i + o)
        steps[2 + o] = powers(r8, blocks - 1 - 2 * i - o)
    first_level = at[0] * levels
    for step, spec in enumerate((spec0, spec1, spec2, spec3)):
        l = (at[0] - step) & 3
        for part in range(4):
            t = 4 * l + part
            acc = [[None, None] for _ in range(levels)]
            for k in range(NZ):
                u, d = above[t, k], below[t, k]
                for o in range(2):
                    value = u * steps[o, t, k : k + 1, :] + d * steps[2 + o, t, k : k + 1, :]
                    for z in range(levels):
                        term = value * modes[k, first_level + z]
                        acc[z][o] = term if k == 0 else acc[z][o] + term
            for z in range(levels):
                value = spec[z, :, part * LANES : (part + 1) * LANES] + jnp.concatenate(acc[z], 0)
                high, low = halves(value)
                place = pl.multiple_of((2 * l + part // 2) * rows + z * YB, YB)
                half = pl.ds((part % 2) * LANES, LANES)
                hi[pl.ds(place, YB), half] = high
                lo[pl.ds(place, YB), half] = low
    first = mm3((hi[:rows, :], lo[:rows, :]), (eh[...], el[...]))
    rest = mm3((hi[rows:, :], lo[rows:, :]), (fh[...], fl[...]))
    for z in range(levels):
        real = (first[z * YB : (z + 1) * YB, :LANES], first[z * YB : (z + 1) * YB, LANES:])
        comps = []
        for i in range(7):
            place = i * rows + z * YB
            value = (rest[place : place + YB, :LANES], rest[place : place + YB, LANES:])
            comps.append(cmul(value, twiddle[i : i + 1, :], -twiddle[8 + i : 9 + i, :]))
        cells = real16_back(real, comps)
        for a in range(16):
            out[:, z, a * LANES : (a + 1) * LANES] = cells[a]


def inverse_x(at, specs, ends, modes, lam, eig, consts):
    levels, rows, _ = specs[0].shape
    twiddle, fh, fl, eh, el = consts
    whole = lambda value: pl.BlockSpec(value.shape, lambda i, at: (0,) * value.ndim)
    return pl.pallas_call(
        inverse_x_kernel,
        grid_spec=pltpu.PrefetchScalarGridSpec(
            num_scalar_prefetch=1,
            grid=(rows // YB,),
            in_specs=[pl.BlockSpec((levels, YB, 512), lambda i, at: (0, i, 0))] * 4
            + [
                whole(ends),
                pl.BlockSpec(memory_space=pltpu.SMEM),
                whole(lam),
                whole(eig),
                whole(twiddle),
            ]
            + [whole(fh)] * 4,
            out_specs=pl.BlockSpec((YB, levels, N), lambda i, at: (i, 0, 0)),
            scratch_shapes=[pltpu.VMEM((8 * levels * YB, 256), BF16)] * 2
            + [pltpu.VMEM((16, NZ, 8, LANES), F32)] * 2
            + [pltpu.VMEM((16, NZ, LANES), F32), pltpu.VMEM((4, 16, NZ, LANES), F32)],
        ),
        out_shape=jax.ShapeDtypeStruct((rows, levels, N), F32),
        name="inverse_x",
    )(at, *specs, ends, modes, lam, eig, twiddle, fh, fl, eh, el)


def ends_kernel(at, x0, x1, x2, x3, wh, wl, lam, eig, f, ends):
    h = pl.program_id(0)
    rows = x0.shape[1]
    w = (wh[at[0]], wl[at[0]])
    e = eig[pl.ds(at[0] * 2 + h, 1), :]
    r, _ = decay(lam[:, 0:1], e)
    for o in range(rows // 8):
        block = [x[:, 8 * o : 8 * o + 8, :].reshape(32, 256) for x in (x0, x1, x2, x3)]
        value = mm3(w, halves(jnp.concatenate(block, 0)))
        f[8 * o : 8 * o + 8, :, :] = value.reshape(8, NZ, 256)
    up = jnp.zeros((NZ, 256), F32)
    down = jnp.zeros((NZ, 256), F32)
    for y in range(rows):
        up = f[y] + r * up
        down = f[rows - 1 - y] + r * down
    ends[:, 0, :] = up[:, :LANES]
    ends[:, 1, :] = up[:, LANES:]
    ends[:, 2, :] = down[:, :LANES]
    ends[:, 3, :] = down[:, LANES:]


def solve_kernel(at, f, wh, wl, lam, eig, out0, out1, out2, out3, work):
    h = pl.program_id(0)
    rows = f.shape[0]
    w = (wh[at[0]], wl[at[0]])
    e = eig[pl.ds(at[0] * 2 + h, 1), :]
    r, gain = decay(lam[:, 0:1], e)
    up = jnp.zeros((NZ, 256), F32)
    down = jnp.zeros((NZ, 256), F32)
    for y in range(rows):
        up = r * up
        work[y] = up
        up = up + f[y]
    for y in reversed(range(rows)):
        down = f[y] + r * down
        work[y] = (work[y] + down) * gain
    for o in range(rows // 8):
        block = work[8 * o : 8 * o + 8].reshape(LANES, 256)
        value = mm3(w, halves(block))
        for step, out in enumerate((out0, out1, out2, out3)):
            out[:, 8 * o : 8 * o + 8, :] = value[32 * step : 32 * step + 32].reshape(4, 8, 256)


def level_ends(at, xs, wh, wl, lam, eig):
    _, rows, width = xs[0].shape
    whole = lambda value: pl.BlockSpec(value.shape, lambda h, at: (0,) * value.ndim)
    return pl.pallas_call(
        ends_kernel,
        grid_spec=pltpu.PrefetchScalarGridSpec(
            num_scalar_prefetch=1,
            grid=(width // 256,),
            in_specs=[pl.BlockSpec((4, rows, 256), lambda h, at: (0, 0, h))] * 4
            + [whole(value) for value in (wh, wl, lam, eig)],
            out_specs=[
                pl.BlockSpec((rows, NZ, 256), lambda h, at: (0, 0, h)),
                pl.BlockSpec((NZ, 4, LANES), lambda h, at: (h, 0, 0)),
            ],
        ),
        out_shape=[
            jax.ShapeDtypeStruct((rows, NZ, width), F32),
            jax.ShapeDtypeStruct((2 * NZ, 4, LANES), F32),
        ],
        name="level_ends",
    )(at, *xs, wh, wl, lam, eig)


def level_solve(at, f, wh, wl, lam, eig):
    rows, _, width = f.shape
    whole = lambda value: pl.BlockSpec(value.shape, lambda h, at: (0,) * value.ndim)
    return pl.pallas_call(
        solve_kernel,
        grid_spec=pltpu.PrefetchScalarGridSpec(
            num_scalar_prefetch=1,
            grid=(width // 256,),
            in_specs=[pl.BlockSpec((rows, NZ, 256), lambda h, at: (0, 0, h))]
            + [whole(value) for value in (wh, wl, lam, eig)],
            out_specs=[pl.BlockSpec((4, rows, 256), lambda h, at: (0, 0, h))] * 4,
            scratch_shapes=[pltpu.VMEM((rows, NZ, 256), F32)],
        ),
        out_shape=[jax.ShapeDtypeStruct((4, rows, width), F32)] * 4,
        name="level_solve",
    )(at, f, wh, wl, lam, eig)


def carry_kernel(at, ends, lam, eig, out):
    sections = ends.shape[0]
    j = at[1]
    k = lax.rem(j, NZ)
    h = lax.div(j, NZ)
    e = eig[pl.ds(at[0] * 2 + h, 1), :]
    r, _ = decay(lam[pl.ds(k, 1), 0:1], e)
    for _ in range(6):
        r = r * r
    row = lax.broadcasted_iota(jnp.int32, (4, LANES), 0)
    ratio = jnp.where(lax.rem(row, 2) == 0, r[:, :LANES], r[:, LANES:])
    whole = ratio
    for _ in range(5):
        whole = whole * whole
    scale = 1.0 / (1.0 - whole)
    up = jnp.zeros((4, LANES), F32)
    down = jnp.zeros((4, LANES), F32)
    for s in range(sections):
        up = ends[s] + ratio * up
        down = ends[sections - 1 - s] + ratio * down
    up = up * scale
    down = down * scale
    first = row < 2
    ups = []
    for s in range(sections):
        ups.append(up)
        up = ends[s] + ratio * up
    for s in reversed(range(sections)):
        value = jnp.where(first, ups[s], down)
        for section in range(4):
            out[s, section] = value
        down = ends[s] + ratio * down


def carries(at, ends, lam, eig):
    return pl.pallas_call(
        carry_kernel,
        in_specs=[pl.BlockSpec(memory_space=pltpu.SMEM)] + [pl.BlockSpec(memory_space=pltpu.VMEM)] * 3,
        out_shape=jax.ShapeDtypeStruct((ends.shape[0], 4) + ends.shape[1:], F32),
        name="section_carries",
    )(at, ends, lam, eig)


def shift(value, step):
    return lax.ppermute(value, "lev", [(i, (i + step) % 4) for i in range(4)])


def body(source, solid, couplings):
    full, edge, twiddle, eig, spread = host_tables()
    fh, fl = split_host(full)
    eh, el = split_host(edge)
    fth, ftl = split_host(full.T)
    eth, etl = split_host(edge.T)
    at = jnp.stack([lax.axis_index("lev"), lax.axis_index("rows")]).astype(jnp.int32)
    lam, modes, w2h, w2l, w4h, w4l = eigen(couplings)
    parts = forward_x(at, source, solid, (spread, twiddle, fh, fl, eh, el))
    xs = [parts[0]] + [shift(parts[step], -step) for step in (1, 2, 3)]
    f, ends = level_ends(at, xs, w2h, w2l, lam, eig)
    ends = lax.all_to_all(ends, "rows", 0, 0, tiled=True)
    parts = level_solve(at, f, w4h, w4l, lam, eig)
    specs = [parts[0]] + [shift(parts[step], step) for step in (1, 2, 3)]
    ends = carries(at, ends, lam, eig).reshape(128, 4, LANES)
    ends = lax.all_to_all(ends, ("rows", "lev"), 0, 0, tiled=True).reshape(2, NZ, 4, 4, LANES)
    return inverse_x(at, specs, ends, modes, lam, eig, (twiddle, fth, ftl, eth, etl))


def solution(mesh):
    return jax.shard_map(
        body,
        mesh=mesh,
        in_specs=(P("rows", "lev", None), P("rows", "lev", None), P()),
        out_specs=P("rows", "lev", None),
        check_vma=False,
    )
```

```python
import math

import jax
import jax.numpy as jnp
import ml_dtypes
import numpy as np
from jax import lax
from jax.experimental import pallas as pl
from jax.experimental.pallas import tpu as pltpu
from jax.sharding import PartitionSpec as P

F32 = jnp.float32
BF16 = jnp.bfloat16
BY = 8
BX = 64
N = 2048
LANES = 128
NZ = 16
TURN = 2.0 * math.pi
RESIDUES = (1, 5, 9, 13, 2, 10, 4)
SWEEPS = 12


VMEM = pl.BlockSpec(memory_space=pltpu.VMEM)


def grant(mebibytes):
    return pltpu.CompilerParams(vmem_limit_bytes=mebibytes << 20)


def split_host(table):
    table = np.asarray(table, np.float32)
    high = table.astype(ml_dtypes.bfloat16)
    low = (table - high.astype(np.float32)).astype(ml_dtypes.bfloat16)
    return high, low


def host_tables():
    b = np.arange(LANES)
    m = np.arange(LANES)
    angle = TURN * np.mod(np.outer(b, m), LANES) / LANES
    scale = math.sqrt(2.0 / N)
    cos, sin = scale * np.cos(angle), scale * np.sin(angle)
    full = np.block([[cos, -sin], [sin, cos]])
    edge = np.zeros((2 * LANES, 2 * LANES))
    freq0 = np.concatenate([np.arange(65), np.arange(1, 64)])
    angle0 = TURN * np.mod(np.outer(b, freq0), LANES) / LANES
    part = np.where(np.arange(LANES)[None, :] < 65, np.cos(angle0), -np.sin(angle0)) * scale
    part[:, 0] *= math.sqrt(0.5)
    part[:, 64] *= math.sqrt(0.5)
    edge[:LANES, :LANES] = part
    freq8 = 16 * np.arange(64) + 8
    angle8 = TURN * np.mod(np.outer(b, freq8), N) / N
    edge[LANES:, LANES:] = scale * np.concatenate([np.cos(angle8), -np.sin(angle8)], 1)
    q = np.array(RESIDUES)
    twist = TURN * np.outer(q, b) / N
    twiddle = np.zeros((16, LANES), np.float32)
    twiddle[:7] = np.cos(twist)
    twiddle[8:15] = np.sin(twist)
    freqs = [np.concatenate([16 * freq0, freq8, freq8])]
    for residue in RESIDUES:
        freqs.append(np.tile(16 * m + residue, 2))
    freqs = np.concatenate(freqs)
    eigen = (4.0 * np.sin(np.pi * freqs / N) ** 2).astype(np.float32).reshape(8, 256)
    spread = (np.arange(32)[:, None] == np.arange(N)[None, :] // BX).astype(ml_dtypes.bfloat16)
    return full, edge, twiddle, eigen, spread


def halves(value):
    high = value.astype(BF16)
    return high, (value - high.astype(F32)).astype(BF16)


def mm(left, right):
    return jnp.dot(left, right, preferred_element_type=F32)


def mm3(left, right):
    return mm(left[0], right[0]) + (mm(left[1], right[0]) + mm(left[0], right[1]))


def cmul(value, cos, sin):
    re, im = value
    return re * cos + im * sin, im * cos - re * sin


def cadd(left, right):
    return left[0] + right[0], left[1] + right[1]


def csub(left, right):
    return left[0] - right[0], left[1] - right[1]


def phase(steps):
    return math.cos(TURN * steps / 16), math.sin(TURN * steps / 16)


def real16(v):
    s = [v[a] + v[a + 8] for a in range(8)]
    d = [v[a] - v[a + 8] for a in range(8)]
    u = [(d[0], -d[4])]
    for a in range(1, 4):
        u.append(cmul((d[a], -d[a + 4]), *phase(a)))
    p02, m02 = cadd(u[0], u[2]), csub(u[0], u[2])
    p13, m13 = cadd(u[1], u[3]), csub(u[1], u[3])
    y1, y9 = cadd(p02, p13), csub(p02, p13)
    y5 = (m02[0] + m13[1], m02[1] - m13[0])
    y13 = (m02[0] - m13[1], m02[1] + m13[0])
    t = [s[a] + s[a + 4] for a in range(4)]
    e = [s[a] - s[a + 4] for a in range(4)]
    z1 = cmul((e[1], -e[3]), *phase(2))
    z0 = (e[0], -e[2])
    y2, y10 = cadd(z0, z1), csub(z0, z1)
    a0, a1 = t[0] + t[2], t[1] + t[3]
    y4 = (t[0] - t[2], t[3] - t[1])
    return (a0 + a1, a0 - a1), (y1, y5, y9, y13, y2, y10, y4)


def real16_back(real, comps):
    g1, g5, g9, g13, g2, g10, g4 = comps
    a0, a1 = real[0] + real[1], real[0] - real[1]
    t = [a0 + g4[0], a1 - g4[1], a0 - g4[0], a1 + g4[1]]
    z0 = cadd(g2, g10)
    cos, sin = phase(2)
    z1 = cmul(csub(g2, g10), cos, -sin)
    e = [z0[0], z1[0], -z0[1], -z1[1]]
    s = [t[a] + e[a] for a in range(4)] + [t[a] - e[a] for a in range(4)]
    p19, m19 = cadd(g1, g9), csub(g1, g9)
    p513, m513 = cadd(g5, g13), csub(g5, g13)
    u = [cadd(p19, p513), None, csub(p19, p513), None]
    u[1] = (m19[0] - m513[1], m19[1] + m513[0])
    u[3] = (m19[0] + m513[1], m19[1] - m513[0])
    d = [None] * 8
    for a in range(4):
        cos, sin = phase(a)
        z = u[a] if a == 0 else cmul(u[a], cos, -sin)
        d[a], d[a + 4] = z[0], -z[1]
    return [s[a] + d[a] for a in range(8)] + [s[a] - d[a] for a in range(8)]


YB = 16


def forward_x_kernel(
    src, solid, spread, twiddle, fh, fl, eh, el, out0, out1, out2, out3, hi, lo, hi0, lo0
):
    lev = lax.axis_index("lev")
    band = pl.ds(pl.multiple_of(pl.program_id(0) * YB, YB), YB)
    levels = src.shape[1]
    rows = levels * YB
    open_cells = (1 - solid[...]).astype(F32).astype(BF16)
    masks = mm(open_cells.reshape(solid.shape[0] * levels, solid.shape[2]), spread[...])
    for z in range(levels):
        cells = []
        for a in range(16):
            piece = src[:, z, a * LANES : (a + 1) * LANES]
            mask = masks[:, a * LANES : (a + 1) * LANES]
            pieces = [
                piece[8 * i : 8 * i + 8] * mask[i * levels + z : i * levels + z + 1]
                for i in range(YB // 8)
            ]
            cells.append(jnp.concatenate(pieces, 0))
        real, comps = real16(cells)
        for part in range(2):
            high, low = halves(real[part])
            hi0[z * YB : (z + 1) * YB, part * LANES : (part + 1) * LANES] = high
            lo0[z * YB : (z + 1) * YB, part * LANES : (part + 1) * LANES] = low
        for i in range(1, 8):
            block = cmul(comps[i - 1], twiddle[i - 1 : i, :], twiddle[7 + i : 8 + i, :])
            slot = 2 * ((lev - i // 2) & 3) + i % 2
            place = pl.multiple_of(slot * rows + z * YB, YB)
            for part in range(2):
                high, low = halves(block[part])
                hi[pl.ds(place, YB), part * LANES : (part + 1) * LANES] = high
                lo[pl.ds(place, YB), part * LANES : (part + 1) * LANES] = low
    outs = (out0, out1, out2, out3)
    rest = mm3((hi[...], lo[...]), (fh[...], fl[...]))
    for step in range(4):
        for h in range(2):
            value = rest[(2 * step + h) * rows : (2 * step + h + 1) * rows]
            outs[step][:, band, h * 256 : h * 256 + 256] = value.reshape(levels, YB, 256)
    first = mm3((hi0[...], lo0[...]), (eh[...], el[...])).reshape(levels, YB, 256)
    for step in range(4):

        @pl.when(lev == step)
        def _(step=step):
            outs[step][:, band, 0:256] = first


def forward_x(source, solid, consts):
    rows, levels, cells = source.shape
    return pl.pallas_call(
        forward_x_kernel,
        grid=(rows // YB,),
        in_specs=[
            pl.BlockSpec((YB, levels, cells), lambda i: (i, 0, 0)),
            pl.BlockSpec((YB // BY, levels, cells // BX), lambda i: (i, 0, 0)),
        ]
        + [VMEM] * 6,
        out_specs=[VMEM] * 4,
        out_shape=[jax.ShapeDtypeStruct((levels, rows, 512), F32)] * 4,
        scratch_shapes=[pltpu.VMEM((8 * levels * YB, 256), BF16)] * 2
        + [pltpu.VMEM((levels * YB, 256), BF16)] * 2,
        compiler_params=grant(12),
        name="forward_x",
    )(source, solid, *consts)


def rsqrt(value):
    root = lax.rsqrt(value)
    return root * (1.5 - 0.5 * value * root * root)


def eigen_kernel(coup, lam, modes, w2h, w2l, w4h, w4l):
    sub = lax.broadcasted_iota(jnp.int32, (8, LANES), 0)
    lane = lax.broadcasted_iota(jnp.int32, (8, LANES), 1) & (NZ - 1)
    low = lane < 8
    g = [jnp.zeros((8, LANES), F32), jnp.zeros((8, LANES), F32)]
    link = jnp.zeros((8, LANES), F32)
    for k in range(NZ):
        pivot = coup[k] + coup[k + 1] - link * link
        inverse = rsqrt(pivot)
        here = lane == (k // 2 + 8 * (k % 2))
        g[k // 8] = jnp.where(here & (sub == k % 8), pivot * inverse, g[k // 8])
        link = -coup[k + 1] * inverse
        if k < NZ - 1:
            below = (k + 1) // 8
            g[below] = jnp.where(here & (sub == (k + 1) % 8), link, g[below])
    partners = [pltpu.roll(value, 8, 1) for value in g]

    def total(first, second):
        value = first + second
        for shift in (4, 2, 1):
            value = value + pltpu.roll(value, shift, 0)
        return value

    def right(value):
        return pltpu.roll(value, 1, 1)

    def left(value):
        return pltpu.roll(value, LANES - 1, 1)

    def step(_, carry):
        g0, g1, p0, p1, worst = carry
        own = total(g0 * g0, g1 * g1)
        other = total(p0 * p0, p1 * p1)
        a = total(g0 * p0, g1 * p1)
        d = other - own
        w = d * d + 4.0 * a * a
        h = rsqrt(w)
        x = 0.5 + 0.5 * jnp.abs(d) * h
        y = rsqrt(x)
        positive = (d > 0.0) | ((d == 0.0) & low)
        turn = a * h * y
        still = w == 0.0
        c = jnp.where(still, 1.0, x * y)
        turn = jnp.where(still, 0.0, jnp.where(positive, turn, -turn))
        worst = jnp.maximum(worst, jnp.where(still, 0.0, a * a / (own * other)))
        out = []
        for value, partner in ((g0, p0), (g1, p1)):
            mine = c * value - turn * partner
            theirs = c * partner + turn * value
            rising = right(jnp.where(lane == 0, theirs, mine))
            new = jnp.where(low, rising, jnp.where(lane == 15, theirs, left(mine)))
            new = jnp.where(lane == 0, mine, new)
            falling = right(jnp.where(lane == 8, mine, theirs))
            new_partner = jnp.where(low, jnp.where(lane == 7, mine, left(theirs)), falling)
            new_partner = jnp.where(lane == 8, theirs, new_partner)
            out.append((new, new_partner))
        return out[0][0], out[1][0], out[0][1], out[1][1], worst

    def sweep(carry):
        count, _, *state = carry
        state = lax.fori_loop(0, 15, step, (*state, jnp.zeros((8, LANES), F32)))
        return (count + 1, jnp.max(state[4]), *state[:4])

    def unfinished(carry):
        return (carry[0] < SWEEPS) & (carry[1] > 1e-7)

    state = (jnp.int32(0), jnp.float32(1.0), g[0], g[1], partners[0], partners[1])
    _, _, g0, g1, _, _ = lax.while_loop(unfinished, sweep, state)
    square = total(g0 * g0, g1 * g1)
    inverse = rsqrt(square)
    vectors = jnp.concatenate([g0 * inverse, g1 * inverse], 0)
    lam[...] = jnp.concatenate([square] * NZ, 0).T[:NZ]
    modes[...] = jnp.concatenate([vectors] * 8, 0).T[:NZ]
    wide = [jnp.broadcast_to(vectors[z : z + 1], (8, LANES)) for z in range(NZ)]
    row = lax.broadcasted_iota(jnp.int32, (LANES, LANES), 0)
    col = lax.broadcasted_iota(jnp.int32, (LANES, LANES), 1)
    for section in range(4):
        order = [wide[(z + 4 * section) % NZ] for z in range(NZ)]
        w4 = jnp.where(row % 8 == col // NZ, jnp.concatenate(order, 0), 0.0)
        w4h[section], w4l[section] = halves(w4)
        w2h[section], w2l[section] = halves(w4.T)


def eigen(couplings):
    table = jax.ShapeDtypeStruct((NZ, LANES), F32)
    matrix = jax.ShapeDtypeStruct((4, LANES, LANES), BF16)
    return pl.pallas_call(
        eigen_kernel,
        in_specs=[pl.BlockSpec(memory_space=pltpu.SMEM)],
        out_specs=[VMEM] * 6,
        out_shape=[table, table, matrix, matrix, matrix, matrix],
        compiler_params=grant(4),
        name="level_modes",
    )(couplings)


def decay(lam, e):
    half = 0.5 * (lam + e)
    root = jnp.sqrt(half * (2.0 + half))
    return 1.0 / (1.0 + half + root), 0.5 / root


def powers(base, count):
    square = base * base
    value = jnp.where((count & 1) != 0, base, 1.0)
    value = value * jnp.where((count & 2) != 0, square, 1.0)
    return value * jnp.where((count & 4) != 0, square * square, 1.0)


def inverse_x_kernel(
    spec0, spec1, spec2, spec3, ends, modes, lam, eig, twiddle, fh, fl, eh, el,
    out, hi, lo, above, below, eighth, steps,
):
    levels = spec0.shape[0]
    rows = levels * YB
    lev = lax.axis_index("lev")
    i = pl.program_id(0)
    band = pl.ds(pl.multiple_of(i * YB, YB), YB)
    blocks = 2 * pl.num_programs(0)

    @pl.when(i == 0)
    def _():
        b = lax.broadcasted_iota(jnp.int32, (8, LANES), 0)
        for t in range(16):
            l, h, p = t // 4, (t // 2) % 2, t % 2
            e = eig[t // 2 : t // 2 + 1, p * LANES : (p + 1) * LANES]
            r, gain = decay(lam[:, 0:1], e)
            gain = gain * r
            up = ends[h, :, l, p, :] * gain
            down = ends[h, :, l, 2 + p, :] * gain
            r2 = r * r
            r4 = r2 * r2
            eighth[t] = r4 * r4
            for k in range(NZ):
                base = jnp.broadcast_to(r[k : k + 1], (8, LANES))
                above[t, k] = powers(base, b) * up[k : k + 1]
                below[t, k] = powers(base, 7 - b) * down[k : k + 1]

    r8 = eighth[...]
    for o in range(2):
        steps[o] = powers(r8, 2 * i + o)
        steps[2 + o] = powers(r8, blocks - 1 - 2 * i - o)
    first_level = lev * levels
    for step, spec in enumerate((spec0, spec1, spec2, spec3)):
        l = (lev - step) & 3
        for part in range(4):
            t = 4 * l + part
            acc = [[None, None] for _ in range(levels)]
            for k in range(NZ):
                u, d = above[t, k], below[t, k]
                for o in range(2):
                    value = u * steps[o, t, k : k + 1, :] + d * steps[2 + o, t, k : k + 1, :]
                    for z in range(levels):
                        term = value * modes[k, first_level + z]
                        acc[z][o] = term if k == 0 else acc[z][o] + term
            for z in range(levels):
                value = spec[z, band, part * LANES : (part + 1) * LANES] + jnp.concatenate(acc[z], 0)
                high, low = halves(value)
                place = pl.multiple_of((2 * l + part // 2) * rows + z * YB, YB)
                half = pl.ds((part % 2) * LANES, LANES)
                hi[pl.ds(place, YB), half] = high
                lo[pl.ds(place, YB), half] = low
    first = mm3((hi[:rows, :], lo[:rows, :]), (eh[...], el[...]))
    rest = mm3((hi[rows:, :], lo[rows:, :]), (fh[...], fl[...]))
    for z in range(levels):
        real = (first[z * YB : (z + 1) * YB, :LANES], first[z * YB : (z + 1) * YB, LANES:])
        comps = []
        for i in range(7):
            place = i * rows + z * YB
            value = (rest[place : place + YB, :LANES], rest[place : place + YB, LANES:])
            comps.append(cmul(value, twiddle[i : i + 1, :], -twiddle[8 + i : 9 + i, :]))
        cells = real16_back(real, comps)
        for a in range(16):
            out[:, z, a * LANES : (a + 1) * LANES] = cells[a]


def inverse_x(specs, ends, modes, lam, eig, consts):
    levels, rows, _ = specs[0].shape
    return pl.pallas_call(
        inverse_x_kernel,
        grid=(rows // YB,),
        in_specs=[VMEM] * 5 + [pl.BlockSpec(memory_space=pltpu.SMEM)] + [VMEM] * 7,
        out_specs=pl.BlockSpec((YB, levels, N), lambda i: (i, 0, 0)),
        out_shape=jax.ShapeDtypeStruct((rows, levels, N), F32),
        scratch_shapes=[pltpu.VMEM((8 * levels * YB, 256), BF16)] * 2
        + [pltpu.VMEM((16, NZ, 8, LANES), F32)] * 2
        + [pltpu.VMEM((16, NZ, LANES), F32), pltpu.VMEM((4, 16, NZ, LANES), F32)],
        compiler_params=grant(16),
        name="inverse_x",
    )(*specs, ends, modes, lam, eig, *consts)


def level_kernel(
    x0, x1, x2, x3, w2h, w2l, w4h, w4l, lam, eig, out0, out1, out2, out3, ends, f, work
):
    lev = lax.axis_index("lev")
    rows = x0.shape[1]
    w2 = (w2h[lev], w2l[lev])
    w4 = (w4h[lev], w4l[lev])
    for h in range(x0.shape[2] // 256):
        cols = pl.ds(h * 256, 256)
        e = eig[pl.ds(lev * 2 + h, 1), :]
        r, gain = decay(lam[:, 0:1], e)
        for o in range(rows // 8):
            block = [x[:, 8 * o : 8 * o + 8, cols].reshape(32, 256) for x in (x0, x1, x2, x3)]
            value = mm3(w2, halves(jnp.concatenate(block, 0)))
            f[8 * o : 8 * o + 8] = value.reshape(8, NZ, 256)
        up = jnp.zeros((NZ, 256), F32)
        down = jnp.zeros((NZ, 256), F32)
        for y in range(rows):
            up = r * up
            work[y] = up
            up = up + f[y]
        for y in reversed(range(rows)):
            down = f[y] + r * down
            work[y] = (work[y] + down) * gain
        place = pl.ds(h * NZ, NZ)
        ends[place, 0, :] = up[:, :LANES]
        ends[place, 1, :] = up[:, LANES:]
        ends[place, 2, :] = down[:, :LANES]
        ends[place, 3, :] = down[:, LANES:]
        for o in range(rows // 8):
            block = work[8 * o : 8 * o + 8].reshape(LANES, 256)
            value = mm3(w4, halves(block))
            for step, out in enumerate((out0, out1, out2, out3)):
                out[:, 8 * o : 8 * o + 8, cols] = value[32 * step : 32 * step + 32].reshape(4, 8, 256)


def level_solve(xs, weights, lam, eig):
    _, rows, width = xs[0].shape
    return pl.pallas_call(
        level_kernel,
        in_specs=[VMEM] * 10,
        out_specs=[VMEM] * 5,
        out_shape=[jax.ShapeDtypeStruct((4, rows, width), F32)] * 4
        + [jax.ShapeDtypeStruct((2 * NZ, 4, LANES), F32)],
        scratch_shapes=[pltpu.VMEM((rows, NZ, 256), F32)] * 2,
        compiler_params=grant(12),
        name="level_solve",
    )(*xs, *weights, lam, eig)


def carry_kernel(ends, lam, eig, out):
    sections = ends.shape[0]
    j = lax.axis_index("rows")
    k = lax.rem(j, NZ)
    h = lax.div(j, NZ)
    e = eig[pl.ds(lax.axis_index("lev") * 2 + h, 1), :]
    r, _ = decay(lam[pl.ds(k, 1), 0:1], e)
    for _ in range(6):
        r = r * r
    row = lax.broadcasted_iota(jnp.int32, (4, LANES), 0)
    ratio = jnp.where(lax.rem(row, 2) == 0, r[:, :LANES], r[:, LANES:])
    whole = ratio
    for _ in range(5):
        whole = whole * whole
    scale = 1.0 / (1.0 - whole)
    up = jnp.zeros((4, LANES), F32)
    down = jnp.zeros((4, LANES), F32)
    for s in range(sections):
        up = ends[s] + ratio * up
        down = ends[sections - 1 - s] + ratio * down
    up = up * scale
    down = down * scale
    first = row < 2
    ups = []
    for s in range(sections):
        ups.append(up)
        up = ends[s] + ratio * up
    for s in reversed(range(sections)):
        value = jnp.where(first, ups[s], down)
        for section in range(4):
            out[s, section] = value
        down = ends[s] + ratio * down


def carries(ends, lam, eig):
    return pl.pallas_call(
        carry_kernel,
        in_specs=[VMEM] * 3,
        out_specs=VMEM,
        out_shape=jax.ShapeDtypeStruct((ends.shape[0], 4) + ends.shape[1:], F32),
        compiler_params=grant(4),
        name="section_carries",
    )(ends, lam, eig)


def shift(value, step):
    return lax.ppermute(value, "lev", [(i, (i + step) % 4) for i in range(4)])


def body(source, solid, couplings):
    full, edge, twiddle, eig, spread = host_tables()
    fh, fl = split_host(full)
    eh, el = split_host(edge)
    fth, ftl = split_host(full.T)
    eth, etl = split_host(edge.T)
    lam, modes, w2h, w2l, w4h, w4l = eigen(couplings)
    parts = forward_x(source, solid, (spread, twiddle, fh, fl, eh, el))
    xs = [parts[0]] + [shift(parts[step], -step) for step in (1, 2, 3)]
    *parts, ends = level_solve(xs, (w2h, w2l, w4h, w4l), lam, eig)
    specs = [parts[0]] + [shift(parts[step], step) for step in (1, 2, 3)]
    ends = lax.all_to_all(ends, "rows", 0, 0, tiled=True)
    ends = carries(ends, lam, eig).reshape(128, 4, LANES)
    ends = lax.all_to_all(ends, ("rows", "lev"), 0, 0, tiled=True).reshape(2, NZ, 4, 4, LANES)
    return inverse_x(specs, ends, modes, lam, eig, (twiddle, fth, ftl, eth, etl))


def solution(mesh):
    return jax.shard_map(
        body,
        mesh=mesh,
        in_specs=(P("rows", "lev", None), P("rows", "lev", None), P()),
        out_specs=P("rows", "lev", None),
        check_vma=False,
    )
```

```python
import math

import jax
import jax.numpy as jnp
import ml_dtypes
import numpy as np
from jax import lax
from jax.experimental import pallas as pl
from jax.experimental.pallas import tpu as pltpu
from jax.sharding import PartitionSpec as P

F32 = jnp.float32
BF16 = jnp.bfloat16
BY = 8
BX = 64
N = 2048
LANES = 128
NZ = 16
TURN = 2.0 * math.pi
RESIDUES = (1, 5, 9, 13, 2, 10, 4)
SWEEPS = 12


VMEM = pl.BlockSpec(memory_space=pltpu.VMEM)


def grant(mebibytes):
    return pltpu.CompilerParams(vmem_limit_bytes=mebibytes << 20)


def split_host(table):
    table = np.asarray(table, np.float32)
    high = table.astype(ml_dtypes.bfloat16)
    low = (table - high.astype(np.float32)).astype(ml_dtypes.bfloat16)
    return high, low


def host_tables():
    b = np.arange(LANES)
    m = np.arange(LANES)
    angle = TURN * np.mod(np.outer(b, m), LANES) / LANES
    scale = math.sqrt(2.0 / N)
    cos, sin = scale * np.cos(angle), scale * np.sin(angle)
    full = np.block([[cos, -sin], [sin, cos]])
    edge = np.zeros((2 * LANES, 2 * LANES))
    freq0 = np.concatenate([np.arange(65), np.arange(1, 64)])
    angle0 = TURN * np.mod(np.outer(b, freq0), LANES) / LANES
    part = np.where(np.arange(LANES)[None, :] < 65, np.cos(angle0), -np.sin(angle0)) * scale
    part[:, 0] *= math.sqrt(0.5)
    part[:, 64] *= math.sqrt(0.5)
    edge[:LANES, :LANES] = part
    freq8 = 16 * np.arange(64) + 8
    angle8 = TURN * np.mod(np.outer(b, freq8), N) / N
    edge[LANES:, LANES:] = scale * np.concatenate([np.cos(angle8), -np.sin(angle8)], 1)
    q = np.array(RESIDUES)
    twist = TURN * np.outer(q, b) / N
    twiddle = np.zeros((16, LANES), np.float32)
    twiddle[:7] = np.cos(twist)
    twiddle[8:15] = np.sin(twist)
    freqs = [np.concatenate([16 * freq0, freq8, freq8])]
    for residue in RESIDUES:
        freqs.append(np.tile(16 * m + residue, 2))
    freqs = np.concatenate(freqs)
    eigen = (4.0 * np.sin(np.pi * freqs / N) ** 2).astype(np.float32).reshape(8, 256)
    spread = (np.arange(32)[:, None] == np.arange(N)[None, :] // BX).astype(ml_dtypes.bfloat16)
    return full, edge, twiddle, eigen, spread


def halves(value):
    high = value.astype(BF16)
    return high, (value - high.astype(F32)).astype(BF16)


def mm(left, right):
    return jnp.dot(left, right, preferred_element_type=F32)


def mm3(left, right):
    return mm(left[0], right[0]) + (mm(left[1], right[0]) + mm(left[0], right[1]))


def cmul(value, cos, sin):
    re, im = value
    return re * cos + im * sin, im * cos - re * sin


def cadd(left, right):
    return left[0] + right[0], left[1] + right[1]


def csub(left, right):
    return left[0] - right[0], left[1] - right[1]


def phase(steps):
    return math.cos(TURN * steps / 16), math.sin(TURN * steps / 16)


def real16(v):
    s = [v[a] + v[a + 8] for a in range(8)]
    d = [v[a] - v[a + 8] for a in range(8)]
    u = [(d[0], -d[4])]
    for a in range(1, 4):
        u.append(cmul((d[a], -d[a + 4]), *phase(a)))
    p02, m02 = cadd(u[0], u[2]), csub(u[0], u[2])
    p13, m13 = cadd(u[1], u[3]), csub(u[1], u[3])
    y1, y9 = cadd(p02, p13), csub(p02, p13)
    y5 = (m02[0] + m13[1], m02[1] - m13[0])
    y13 = (m02[0] - m13[1], m02[1] + m13[0])
    t = [s[a] + s[a + 4] for a in range(4)]
    e = [s[a] - s[a + 4] for a in range(4)]
    z1 = cmul((e[1], -e[3]), *phase(2))
    z0 = (e[0], -e[2])
    y2, y10 = cadd(z0, z1), csub(z0, z1)
    a0, a1 = t[0] + t[2], t[1] + t[3]
    y4 = (t[0] - t[2], t[3] - t[1])
    return (a0 + a1, a0 - a1), (y1, y5, y9, y13, y2, y10, y4)


def real16_back(real, comps):
    g1, g5, g9, g13, g2, g10, g4 = comps
    a0, a1 = real[0] + real[1], real[0] - real[1]
    t = [a0 + g4[0], a1 - g4[1], a0 - g4[0], a1 + g4[1]]
    z0 = cadd(g2, g10)
    cos, sin = phase(2)
    z1 = cmul(csub(g2, g10), cos, -sin)
    e = [z0[0], z1[0], -z0[1], -z1[1]]
    s = [t[a] + e[a] for a in range(4)] + [t[a] - e[a] for a in range(4)]
    p19, m19 = cadd(g1, g9), csub(g1, g9)
    p513, m513 = cadd(g5, g13), csub(g5, g13)
    u = [cadd(p19, p513), None, csub(p19, p513), None]
    u[1] = (m19[0] - m513[1], m19[1] + m513[0])
    u[3] = (m19[0] + m513[1], m19[1] - m513[0])
    d = [None] * 8
    for a in range(4):
        cos, sin = phase(a)
        z = u[a] if a == 0 else cmul(u[a], cos, -sin)
        d[a], d[a + 4] = z[0], -z[1]
    return [s[a] + d[a] for a in range(8)] + [s[a] - d[a] for a in range(8)]


YB = 16


def forward_x_kernel(
    src, solid, spread, twiddle, fh, fl, eh, el, out0, out1, out2, out3, hi, lo, hi0, lo0
):
    lev = lax.axis_index("lev")
    band = pl.ds(pl.multiple_of(pl.program_id(0) * YB, YB), YB)
    levels = src.shape[1]
    rows = levels * YB
    open_cells = (1 - solid[...]).astype(F32).astype(BF16)
    masks = mm(open_cells.reshape(solid.shape[0] * levels, solid.shape[2]), spread[...])
    for z in range(levels):
        cells = []
        for a in range(16):
            piece = src[:, z, a * LANES : (a + 1) * LANES]
            mask = masks[:, a * LANES : (a + 1) * LANES]
            pieces = [
                piece[8 * i : 8 * i + 8] * mask[i * levels + z : i * levels + z + 1]
                for i in range(YB // 8)
            ]
            cells.append(jnp.concatenate(pieces, 0))
        real, comps = real16(cells)
        for part in range(2):
            high, low = halves(real[part])
            hi0[z * YB : (z + 1) * YB, part * LANES : (part + 1) * LANES] = high
            lo0[z * YB : (z + 1) * YB, part * LANES : (part + 1) * LANES] = low
        for i in range(1, 8):
            block = cmul(comps[i - 1], twiddle[i - 1 : i, :], twiddle[7 + i : 8 + i, :])
            slot = 2 * ((lev - i // 2) & 3) + i % 2
            place = pl.multiple_of(slot * rows + z * YB, YB)
            for part in range(2):
                high, low = halves(block[part])
                hi[pl.ds(place, YB), part * LANES : (part + 1) * LANES] = high
                lo[pl.ds(place, YB), part * LANES : (part + 1) * LANES] = low
    outs = (out0, out1, out2, out3)
    rest = mm3((hi[...], lo[...]), (fh[...], fl[...]))
    for step in range(4):
        for h in range(2):
            value = rest[(2 * step + h) * rows : (2 * step + h + 1) * rows]
            outs[step][:, band, h * 256 : h * 256 + 256] = value.reshape(levels, YB, 256)
    first = mm3((hi0[...], lo0[...]), (eh[...], el[...])).reshape(levels, YB, 256)
    for step in range(4):

        @pl.when(lev == step)
        def _(step=step):
            outs[step][:, band, 0:256] = first


def forward_x(source, solid, consts):
    rows, levels, cells = source.shape
    return pl.pallas_call(
        forward_x_kernel,
        grid=(rows // YB,),
        in_specs=[
            pl.BlockSpec((YB, levels, cells), lambda i: (i, 0, 0)),
            pl.BlockSpec((YB // BY, levels, cells // BX), lambda i: (i, 0, 0)),
        ]
        + [pl.BlockSpec(value.shape, lambda i: (0, 0)) for value in consts],
        out_specs=[VMEM] * 4,
        out_shape=[jax.ShapeDtypeStruct((levels, rows, 512), F32)] * 4,
        scratch_shapes=[pltpu.VMEM((8 * levels * YB, 256), BF16)] * 2
        + [pltpu.VMEM((levels * YB, 256), BF16)] * 2,
        compiler_params=grant(12),
        name="forward_x",
    )(*[pltpu.with_memory_space_constraint(value, pltpu.HBM) for value in (source, solid, *consts)])


def rsqrt(value):
    root = lax.rsqrt(value)
    return root * (1.5 - 0.5 * value * root * root)


def eigen_kernel(coup, lam, modes, w2h, w2l, w4h, w4l):
    sub = lax.broadcasted_iota(jnp.int32, (8, LANES), 0)
    lane = lax.broadcasted_iota(jnp.int32, (8, LANES), 1) & (NZ - 1)
    low = lane < 8
    g = [jnp.zeros((8, LANES), F32), jnp.zeros((8, LANES), F32)]
    link = jnp.zeros((8, LANES), F32)
    for k in range(NZ):
        pivot = coup[k] + coup[k + 1] - link * link
        inverse = rsqrt(pivot)
        here = lane == (k // 2 + 8 * (k % 2))
        g[k // 8] = jnp.where(here & (sub == k % 8), pivot * inverse, g[k // 8])
        link = -coup[k + 1] * inverse
        if k < NZ - 1:
            below = (k + 1) // 8
            g[below] = jnp.where(here & (sub == (k + 1) % 8), link, g[below])
    partners = [pltpu.roll(value, 8, 1) for value in g]

    def total(first, second):
        value = first + second
        for shift in (4, 2, 1):
            value = value + pltpu.roll(value, shift, 0)
        return value

    def right(value):
        return pltpu.roll(value, 1, 1)

    def left(value):
        return pltpu.roll(value, LANES - 1, 1)

    def step(_, carry):
        g0, g1, p0, p1, worst = carry
        own = total(g0 * g0, g1 * g1)
        other = total(p0 * p0, p1 * p1)
        a = total(g0 * p0, g1 * p1)
        d = other - own
        w = d * d + 4.0 * a * a
        h = rsqrt(w)
        x = 0.5 + 0.5 * jnp.abs(d) * h
        y = rsqrt(x)
        positive = (d > 0.0) | ((d == 0.0) & low)
        turn = a * h * y
        still = w == 0.0
        c = jnp.where(still, 1.0, x * y)
        turn = jnp.where(still, 0.0, jnp.where(positive, turn, -turn))
        worst = jnp.maximum(worst, jnp.where(still, 0.0, a * a / (own * other)))
        out = []
        for value, partner in ((g0, p0), (g1, p1)):
            mine = c * value - turn * partner
            theirs = c * partner + turn * value
            rising = right(jnp.where(lane == 0, theirs, mine))
            new = jnp.where(low, rising, jnp.where(lane == 15, theirs, left(mine)))
            new = jnp.where(lane == 0, mine, new)
            falling = right(jnp.where(lane == 8, mine, theirs))
            new_partner = jnp.where(low, jnp.where(lane == 7, mine, left(theirs)), falling)
            new_partner = jnp.where(lane == 8, theirs, new_partner)
            out.append((new, new_partner))
        return out[0][0], out[1][0], out[0][1], out[1][1], worst

    def sweep(carry):
        count, _, *state = carry
        state = lax.fori_loop(0, 15, step, (*state, jnp.zeros((8, LANES), F32)))
        return (count + 1, jnp.max(state[4]), *state[:4])

    def unfinished(carry):
        return (carry[0] < SWEEPS) & (carry[1] > 1e-7)

    state = (jnp.int32(0), jnp.float32(1.0), g[0], g[1], partners[0], partners[1])
    _, _, g0, g1, _, _ = lax.while_loop(unfinished, sweep, state)
    square = total(g0 * g0, g1 * g1)
    inverse = rsqrt(square)
    vectors = jnp.concatenate([g0 * inverse, g1 * inverse], 0)
    lam[...] = jnp.concatenate([square] * NZ, 0).T[:NZ]
    modes[...] = jnp.concatenate([vectors] * 8, 0).T[:NZ]
    wide = [jnp.broadcast_to(vectors[z : z + 1], (8, LANES)) for z in range(NZ)]
    row = lax.broadcasted_iota(jnp.int32, (LANES, LANES), 0)
    col = lax.broadcasted_iota(jnp.int32, (LANES, LANES), 1)
    for section in range(4):
        order = [wide[(z + 4 * section) % NZ] for z in range(NZ)]
        w4 = jnp.where(row % 8 == col // NZ, jnp.concatenate(order, 0), 0.0)
        w4h[section], w4l[section] = halves(w4)
        w2h[section], w2l[section] = halves(w4.T)


def eigen(couplings):
    table = jax.ShapeDtypeStruct((NZ, LANES), F32)
    matrix = jax.ShapeDtypeStruct((4, LANES, LANES), BF16)
    return pl.pallas_call(
        eigen_kernel,
        in_specs=[pl.BlockSpec(memory_space=pltpu.SMEM)],
        out_specs=[VMEM] * 6,
        out_shape=[table, table, matrix, matrix, matrix, matrix],
        compiler_params=grant(4),
        name="level_modes",
    )(couplings)


def decay(lam, e):
    half = 0.5 * (lam + e)
    root = jnp.sqrt(half * (2.0 + half))
    return 1.0 / (1.0 + half + root), 0.5 / root


def powers(base, count):
    square = base * base
    value = jnp.where((count & 1) != 0, base, 1.0)
    value = value * jnp.where((count & 2) != 0, square, 1.0)
    return value * jnp.where((count & 4) != 0, square * square, 1.0)


def inverse_x_kernel(
    spec0, spec1, spec2, spec3, ends, modes, lam, eig, twiddle, fh, fl, eh, el,
    out, hi, lo, above, below, eighth, steps, shelf,
):
    levels = spec0.shape[0]
    rows = levels * YB
    lev = lax.axis_index("lev")
    i = pl.program_id(0)
    band = pl.ds(pl.multiple_of(i * YB, YB), YB)
    blocks = 2 * pl.num_programs(0)

    @pl.when(i == 0)
    def _():
        b = lax.broadcasted_iota(jnp.int32, (8, LANES), 0)
        odd, half, upper = [(b & bit) != 0 for bit in (1, 2, 4)]

        def choose(mask, factor, start=1.0):
            return jnp.where(mask, factor * start, start)

        for t in range(16):
            l, h, p = t // 4, (t // 2) % 2, t % 2
            e = eig[t // 2 : t // 2 + 1, p * LANES : (p + 1) * LANES]
            r, gain = decay(lam[:, 0:1], e)
            gain = gain * r
            r2 = r * r
            r4 = r2 * r2
            eighth[t] = r4 * r4
            for n, value in enumerate(
                (r, r2, r4, ends[h, :, l, p, :] * gain, ends[h, :, l, 2 + p, :] * gain)
            ):
                shelf[t, n] = value
            for k in range(NZ):
                r1, r2, r4, up, down = [shelf[t, n, k : k + 1, :] for n in range(5)]
                above[t, k] = choose(odd, r1, up) * (choose(half, r2) * choose(upper, r4))
                below[t, k] = choose(~odd, r1, down) * (choose(~half, r2) * choose(~upper, r4))

    r8 = eighth[...]
    for o in range(2):
        steps[o] = powers(r8, 2 * i + o)
        steps[2 + o] = powers(r8, blocks - 1 - 2 * i - o)
    first_level = lev * levels
    for step, spec in enumerate((spec0, spec1, spec2, spec3)):
        l = (lev - step) & 3
        for part in range(4):
            t = 4 * l + part
            acc = [[None, None] for _ in range(levels)]
            for k in range(NZ):
                u, d = above[t, k], below[t, k]
                for o in range(2):
                    value = u * steps[o, t, k : k + 1, :] + d * steps[2 + o, t, k : k + 1, :]
                    for z in range(levels):
                        term = value * modes[k, first_level + z]
                        acc[z][o] = term if k == 0 else acc[z][o] + term
            for z in range(levels):
                value = spec[z, band, part * LANES : (part + 1) * LANES] + jnp.concatenate(acc[z], 0)
                high, low = halves(value)
                place = pl.multiple_of((2 * l + part // 2) * rows + z * YB, YB)
                half = pl.ds((part % 2) * LANES, LANES)
                hi[pl.ds(place, YB), half] = high
                lo[pl.ds(place, YB), half] = low
    first = mm3((hi[:rows, :], lo[:rows, :]), (eh[...], el[...]))
    rest = mm3((hi[rows:, :], lo[rows:, :]), (fh[...], fl[...]))
    for z in range(levels):
        real = (first[z * YB : (z + 1) * YB, :LANES], first[z * YB : (z + 1) * YB, LANES:])
        comps = []
        for i in range(7):
            place = i * rows + z * YB
            value = (rest[place : place + YB, :LANES], rest[place : place + YB, LANES:])
            comps.append(cmul(value, twiddle[i : i + 1, :], -twiddle[8 + i : 9 + i, :]))
        cells = real16_back(real, comps)
        for a in range(16):
            out[:, z, a * LANES : (a + 1) * LANES] = cells[a]


def inverse_x(specs, ends, modes, lam, eig, consts):
    levels, rows, _ = specs[0].shape
    return pl.pallas_call(
        inverse_x_kernel,
        grid=(rows // YB,),
        in_specs=[VMEM] * 5 + [pl.BlockSpec(memory_space=pltpu.SMEM)] + [VMEM] * 7,
        out_specs=pl.BlockSpec((YB, levels, N), lambda i: (i, 0, 0)),
        out_shape=jax.ShapeDtypeStruct((rows, levels, N), F32),
        scratch_shapes=[pltpu.VMEM((8 * levels * YB, 256), BF16)] * 2
        + [pltpu.VMEM((16, NZ, 8, LANES), F32)] * 2
        + [pltpu.VMEM((16, NZ, LANES), F32), pltpu.VMEM((4, 16, NZ, LANES), F32)]
        + [pltpu.VMEM((16, 5, NZ, LANES), F32)],
        compiler_params=grant(16),
        name="inverse_x",
    )(*specs, ends, modes, lam, eig, *consts)


def level_kernel(
    x0, x1, x2, x3, w2h, w2l, w4h, w4l, lam, eig, out0, out1, out2, out3, ends, f, work
):
    lev = lax.axis_index("lev")
    rows = x0.shape[1]
    w2 = (w2h[lev], w2l[lev])
    w4 = (w4h[lev], w4l[lev])
    for h in range(x0.shape[2] // 256):
        cols = pl.ds(h * 256, 256)
        e = eig[pl.ds(lev * 2 + h, 1), :]
        r, gain = decay(lam[:, 0:1], e)
        for o in range(rows // 8):
            block = [x[:, 8 * o : 8 * o + 8, cols].reshape(32, 256) for x in (x0, x1, x2, x3)]
            value = mm3(w2, halves(jnp.concatenate(block, 0)))
            f[8 * o : 8 * o + 8] = value.reshape(8, NZ, 256)
        up = jnp.zeros((NZ, 256), F32)
        down = jnp.zeros((NZ, 256), F32)
        for y in range(rows):
            up = r * up
            work[y] = up
            up = up + f[y]
        for y in reversed(range(rows)):
            down = f[y] + r * down
            work[y] = (work[y] + down) * gain
        place = pl.ds(h * NZ, NZ)
        ends[place, 0, :] = up[:, :LANES]
        ends[place, 1, :] = up[:, LANES:]
        ends[place, 2, :] = down[:, :LANES]
        ends[place, 3, :] = down[:, LANES:]
        for o in range(rows // 8):
            block = work[8 * o : 8 * o + 8].reshape(LANES, 256)
            value = mm3(w4, halves(block))
            for step, out in enumerate((out0, out1, out2, out3)):
                out[:, 8 * o : 8 * o + 8, cols] = value[32 * step : 32 * step + 32].reshape(4, 8, 256)


def level_solve(xs, weights, lam, eig):
    _, rows, width = xs[0].shape
    return pl.pallas_call(
        level_kernel,
        in_specs=[VMEM] * 10,
        out_specs=[VMEM] * 5,
        out_shape=[jax.ShapeDtypeStruct((4, rows, width), F32)] * 4
        + [jax.ShapeDtypeStruct((2 * NZ, 4, LANES), F32)],
        scratch_shapes=[pltpu.VMEM((rows, NZ, 256), F32)] * 2,
        compiler_params=grant(12),
        name="level_solve",
    )(*xs, *weights, lam, eig)


def carry_kernel(ends, lam, eig, out):
    sections = ends.shape[0]
    j = lax.axis_index("rows")
    k = lax.rem(j, NZ)
    h = lax.div(j, NZ)
    e = eig[pl.ds(lax.axis_index("lev") * 2 + h, 1), :]
    r, _ = decay(lam[pl.ds(k, 1), 0:1], e)
    for _ in range(6):
        r = r * r
    row = lax.broadcasted_iota(jnp.int32, (4, LANES), 0)
    ratio = jnp.where(lax.rem(row, 2) == 0, r[:, :LANES], r[:, LANES:])
    whole = ratio
    for _ in range(5):
        whole = whole * whole
    scale = 1.0 / (1.0 - whole)
    up = jnp.zeros((4, LANES), F32)
    down = jnp.zeros((4, LANES), F32)
    for s in range(sections):
        up = ends[s] + ratio * up
        down = ends[sections - 1 - s] + ratio * down
    up = up * scale
    down = down * scale
    first = row < 2
    ups = []
    for s in range(sections):
        ups.append(up)
        up = ends[s] + ratio * up
    for s in reversed(range(sections)):
        value = jnp.where(first, ups[s], down)
        for section in range(4):
            out[s, section] = value
        down = ends[s] + ratio * down


def carries(ends, lam, eig):
    return pl.pallas_call(
        carry_kernel,
        in_specs=[VMEM] * 3,
        out_specs=VMEM,
        out_shape=jax.ShapeDtypeStruct((ends.shape[0], 4) + ends.shape[1:], F32),
        compiler_params=grant(4),
        name="section_carries",
    )(ends, lam, eig)


def shift(value, step):
    return lax.ppermute(value, "lev", [(i, (i + step) % 4) for i in range(4)])


def body(source, solid, couplings):
    full, edge, twiddle, eig, spread = host_tables()
    fh, fl = split_host(full)
    eh, el = split_host(edge)
    fth, ftl = split_host(full.T)
    eth, etl = split_host(edge.T)
    lam, modes, w2h, w2l, w4h, w4l = eigen(couplings)
    parts = forward_x(source, solid, (spread, twiddle, fh, fl, eh, el))
    xs = [parts[0]] + [shift(parts[step], -step) for step in (1, 2, 3)]
    *parts, ends = level_solve(xs, (w2h, w2l, w4h, w4l), lam, eig)
    specs = [parts[0]] + [shift(parts[step], step) for step in (1, 2, 3)]
    ends = lax.all_to_all(ends, "rows", 0, 0, tiled=True)
    ends = carries(ends, lam, eig).reshape(128, 4, LANES)
    ends = lax.all_to_all(ends, ("rows", "lev"), 0, 0, tiled=True).reshape(2, NZ, 4, 4, LANES)
    return inverse_x(specs, ends, modes, lam, eig, (twiddle, fth, ftl, eth, etl))


def solution(mesh):
    return jax.shard_map(
        body,
        mesh=mesh,
        in_specs=(P("rows", "lev", None), P("rows", "lev", None), P()),
        out_specs=P("rows", "lev", None),
        check_vma=False,
    )
```

```python
import functools
import math

import jax
import jax.numpy as jnp
import ml_dtypes
import numpy as np
from jax import lax
from jax.experimental import pallas as pl
from jax.experimental.pallas import tpu as pltpu
from jax.sharding import PartitionSpec as P


F32 = jnp.float32
BF16 = jnp.bfloat16
BY = 8
BX = 64
N = 2048
LANES = 128
NZ = 16
TURN = 2.0 * math.pi
RESIDUES = (1, 5, 9, 13, 2, 10, 4)
SWEEPS = 12


VMEM = pl.BlockSpec(memory_space=pltpu.VMEM)


def grant(mebibytes):
    return pltpu.CompilerParams(vmem_limit_bytes=mebibytes << 20)


def split_host(table):
    table = np.asarray(table, np.float32)
    high = table.astype(ml_dtypes.bfloat16)
    low = (table - high.astype(np.float32)).astype(ml_dtypes.bfloat16)
    return high, low


def host_tables():
    b = np.arange(LANES)
    m = np.arange(LANES)
    angle = TURN * np.mod(np.outer(b, m), LANES) / LANES
    scale = math.sqrt(2.0 / N)
    cos, sin = scale * np.cos(angle), scale * np.sin(angle)
    full = np.block([[cos, -sin], [sin, cos]])
    edge = np.zeros((2 * LANES, 2 * LANES))
    freq0 = np.concatenate([np.arange(65), np.arange(1, 64)])
    angle0 = TURN * np.mod(np.outer(b, freq0), LANES) / LANES
    part = np.where(np.arange(LANES)[None, :] < 65, np.cos(angle0), -np.sin(angle0)) * scale
    part[:, 0] *= math.sqrt(0.5)
    part[:, 64] *= math.sqrt(0.5)
    edge[:LANES, :LANES] = part
    freq8 = 16 * np.arange(64) + 8
    angle8 = TURN * np.mod(np.outer(b, freq8), N) / N
    edge[LANES:, LANES:] = scale * np.concatenate([np.cos(angle8), -np.sin(angle8)], 1)
    q = np.array(RESIDUES)
    twist = TURN * np.outer(q, b) / N
    twiddle = np.zeros((16, LANES), np.float32)
    twiddle[:7] = np.cos(twist)
    twiddle[8:15] = np.sin(twist)
    freqs = [np.concatenate([16 * freq0, freq8, freq8])]
    for residue in RESIDUES:
        freqs.append(np.tile(16 * m + residue, 2))
    freqs = np.concatenate(freqs)
    eigen = (4.0 * np.sin(np.pi * freqs / N) ** 2).astype(np.float32).reshape(8, 256)
    spread = (np.arange(32)[:, None] == np.arange(N)[None, :] // BX).astype(ml_dtypes.bfloat16)
    return full, edge, twiddle, eigen, spread


def halves(value):
    high = value.astype(BF16)
    return high, (value - high.astype(F32)).astype(BF16)


def mm(left, right):
    return jnp.dot(left, right, preferred_element_type=F32)


def mm3(left, right):
    return mm(left[0], right[0]) + (mm(left[1], right[0]) + mm(left[0], right[1]))


def cmul(value, cos, sin):
    re, im = value
    return re * cos + im * sin, im * cos - re * sin


def cadd(left, right):
    return left[0] + right[0], left[1] + right[1]


def csub(left, right):
    return left[0] - right[0], left[1] - right[1]


def phase(steps):
    return math.cos(TURN * steps / 16), math.sin(TURN * steps / 16)


def real16(v):
    s = [v[a] + v[a + 8] for a in range(8)]
    d = [v[a] - v[a + 8] for a in range(8)]
    u = [(d[0], -d[4])]
    for a in range(1, 4):
        u.append(cmul((d[a], -d[a + 4]), *phase(a)))
    p02, m02 = cadd(u[0], u[2]), csub(u[0], u[2])
    p13, m13 = cadd(u[1], u[3]), csub(u[1], u[3])
    y1, y9 = cadd(p02, p13), csub(p02, p13)
    y5 = (m02[0] + m13[1], m02[1] - m13[0])
    y13 = (m02[0] - m13[1], m02[1] + m13[0])
    t = [s[a] + s[a + 4] for a in range(4)]
    e = [s[a] - s[a + 4] for a in range(4)]
    z1 = cmul((e[1], -e[3]), *phase(2))
    z0 = (e[0], -e[2])
    y2, y10 = cadd(z0, z1), csub(z0, z1)
    a0, a1 = t[0] + t[2], t[1] + t[3]
    y4 = (t[0] - t[2], t[3] - t[1])
    return (a0 + a1, a0 - a1), (y1, y5, y9, y13, y2, y10, y4)


def real16_back(real, comps):
    g1, g5, g9, g13, g2, g10, g4 = comps
    a0, a1 = real[0] + real[1], real[0] - real[1]
    t = [a0 + g4[0], a1 - g4[1], a0 - g4[0], a1 + g4[1]]
    z0 = cadd(g2, g10)
    cos, sin = phase(2)
    z1 = cmul(csub(g2, g10), cos, -sin)
    e = [z0[0], z1[0], -z0[1], -z1[1]]
    s = [t[a] + e[a] for a in range(4)] + [t[a] - e[a] for a in range(4)]
    p19, m19 = cadd(g1, g9), csub(g1, g9)
    p513, m513 = cadd(g5, g13), csub(g5, g13)
    u = [cadd(p19, p513), None, csub(p19, p513), None]
    u[1] = (m19[0] - m513[1], m19[1] + m513[0])
    u[3] = (m19[0] + m513[1], m19[1] - m513[0])
    d = [None] * 8
    for a in range(4):
        cos, sin = phase(a)
        z = u[a] if a == 0 else cmul(u[a], cos, -sin)
        d[a], d[a + 4] = z[0], -z[1]
    return [s[a] + d[a] for a in range(8)] + [s[a] - d[a] for a in range(8)]


YB = 16


def forward_x_kernel(
    src, solid, spread, twiddle, fh, fl, eh, el,
    out0, out1, out2, out3, out4, out5, out6, out7, hi, lo, hi0, lo0,
):
    lev = lax.axis_index("lev")
    levels = src.shape[1]
    rows = levels * YB
    band = pl.ds(pl.multiple_of(pl.program_id(0) * rows, rows), rows)
    open_cells = (1 - solid[...]).astype(F32).astype(BF16)
    twice = [open_cells[i] for i in range(YB // BY) for _ in range(2)]
    masks = mm(jnp.concatenate(twice, 0), spread[...])
    for part in range(levels):
        near = slice(4 * part, 4 * part + 4)
        mask_at = 8 * (part // 2)
        cells = []
        for a in range(16):
            cols = slice(a * LANES, (a + 1) * LANES)
            piece = src[near, :, cols].reshape(2, 8, LANES)
            cells.append((piece * masks[None, mask_at : mask_at + 8, cols]).reshape(16, LANES))
        real, comps = real16(cells)
        for half in range(2):
            high, low = halves(real[half])
            hi0[part * 16 : part * 16 + 16, half * LANES : (half + 1) * LANES] = high
            lo0[part * 16 : part * 16 + 16, half * LANES : (half + 1) * LANES] = low
        for i in range(1, 8):
            block = cmul(comps[i - 1], twiddle[i - 1 : i, :], twiddle[7 + i : 8 + i, :])
            slot = 2 * ((lev - i // 2) & 3) + i % 2
            place = pl.multiple_of(slot * rows + part * 16, 16)
            for half in range(2):
                high, low = halves(block[half])
                hi[pl.ds(place, 16), half * LANES : (half + 1) * LANES] = high
                lo[pl.ds(place, 16), half * LANES : (half + 1) * LANES] = low
    outs = (out0, out1, out2, out3, out4, out5, out6, out7)
    rest = mm3((hi[...], lo[...]), (fh[...], fl[...]))
    for slot in range(8):
        outs[slot][band, :] = rest[slot * rows : (slot + 1) * rows]
    first = mm3((hi0[...], lo0[...]), (eh[...], el[...]))
    for step in range(4):

        @pl.when(lev == step)
        def _(step=step):
            outs[2 * step][band, :] = first


def forward_x(source, solid, consts):
    rows, levels, cells = source.shape
    return pl.pallas_call(
        forward_x_kernel,
        grid=(rows // YB,),
        in_specs=[
            pl.BlockSpec((YB, levels, cells), lambda i: (i, 0, 0)),
            pl.BlockSpec((YB // BY, levels, cells // BX), lambda i: (i, 0, 0)),
        ]
        + [pl.BlockSpec(value.shape, lambda i: (0, 0)) for value in consts],
        out_specs=[VMEM] * 8,
        out_shape=[jax.ShapeDtypeStruct((rows * levels, 256), F32)] * 8,
        scratch_shapes=[pltpu.VMEM((8 * levels * YB, 256), BF16)] * 2
        + [pltpu.VMEM((levels * YB, 256), BF16)] * 2,
        compiler_params=grant(12),
        name="forward_x",
    )(*[pltpu.with_memory_space_constraint(value, pltpu.HBM) for value in (source, solid, *consts)])


def rsqrt(value):
    root = lax.rsqrt(value)
    return root * (1.5 - 0.5 * value * root * root)


def eigen_kernel(coup, lam, modes, w2h, w2l, w4h, w4l):
    sub = lax.broadcasted_iota(jnp.int32, (8, LANES), 0)
    lane = lax.broadcasted_iota(jnp.int32, (8, LANES), 1) & (NZ - 1)
    low = lane < 8
    g = [jnp.zeros((8, LANES), F32), jnp.zeros((8, LANES), F32)]
    link = jnp.zeros((8, LANES), F32)
    for k in range(NZ):
        pivot = coup[k] + coup[k + 1] - link * link
        inverse = rsqrt(pivot)
        here = lane == (k // 2 + 8 * (k % 2))
        g[k // 8] = jnp.where(here & (sub == k % 8), pivot * inverse, g[k // 8])
        link = -coup[k + 1] * inverse
        if k < NZ - 1:
            below = (k + 1) // 8
            g[below] = jnp.where(here & (sub == (k + 1) % 8), link, g[below])
    partners = [pltpu.roll(value, 8, 1) for value in g]

    def total(first, second):
        value = first + second
        for shift in (4, 2, 1):
            value = value + pltpu.roll(value, shift, 0)
        return value

    def right(value):
        return pltpu.roll(value, 1, 1)

    def left(value):
        return pltpu.roll(value, LANES - 1, 1)

    def step(_, carry):
        g0, g1, p0, p1, worst = carry
        own = total(g0 * g0, g1 * g1)
        other = total(p0 * p0, p1 * p1)
        a = total(g0 * p0, g1 * p1)
        d = other - own
        w = d * d + 4.0 * a * a
        h = rsqrt(w)
        x = 0.5 + 0.5 * jnp.abs(d) * h
        y = rsqrt(x)
        positive = (d > 0.0) | ((d == 0.0) & low)
        turn = a * h * y
        still = w == 0.0
        c = jnp.where(still, 1.0, x * y)
        turn = jnp.where(still, 0.0, jnp.where(positive, turn, -turn))
        worst = jnp.maximum(worst, jnp.where(still, 0.0, a * a / (own * other)))
        out = []
        for value, partner in ((g0, p0), (g1, p1)):
            mine = c * value - turn * partner
            theirs = c * partner + turn * value
            rising = right(jnp.where(lane == 0, theirs, mine))
            new = jnp.where(low, rising, jnp.where(lane == 15, theirs, left(mine)))
            new = jnp.where(lane == 0, mine, new)
            falling = right(jnp.where(lane == 8, mine, theirs))
            new_partner = jnp.where(low, jnp.where(lane == 7, mine, left(theirs)), falling)
            new_partner = jnp.where(lane == 8, theirs, new_partner)
            out.append((new, new_partner))
        return out[0][0], out[1][0], out[0][1], out[1][1], worst

    def sweep(carry):
        count, _, *state = carry
        state = lax.fori_loop(0, 15, step, (*state, jnp.zeros((8, LANES), F32)))
        return (count + 1, jnp.max(state[4]), *state[:4])

    def unfinished(carry):
        return (carry[0] < SWEEPS) & (carry[1] > 1e-7)

    state = (jnp.int32(0), jnp.float32(1.0), g[0], g[1], partners[0], partners[1])
    _, _, g0, g1, _, _ = lax.while_loop(unfinished, sweep, state)
    square = total(g0 * g0, g1 * g1)
    inverse = rsqrt(square)
    vectors = jnp.concatenate([g0 * inverse, g1 * inverse], 0)
    lam[...] = jnp.concatenate([square] * NZ, 0).T[:NZ]
    modes[...] = jnp.concatenate([vectors] * 8, 0).T[:NZ]
    wide = [jnp.broadcast_to(vectors[z : z + 1], (8, LANES)) for z in range(NZ)]
    row = lax.broadcasted_iota(jnp.int32, (LANES, LANES), 0)
    col = lax.broadcasted_iota(jnp.int32, (LANES, LANES), 1)
    for section in range(4):
        order = [wide[(z + 4 * section) % NZ] for z in range(NZ)]
        group = []
        for s in range(4):
            at = (4 * section + 4 * s) % NZ
            group += [vectors[at : at + 4]] * 8
        w4 = jnp.where(row % 8 == col // NZ, jnp.concatenate(order, 0), 0.0)
        w4h[section], w4l[section] = halves(w4)
        w2t = jnp.where(row % 32 // 4 == col // NZ, jnp.concatenate(group, 0), 0.0)
        w2h[section], w2l[section] = halves(w2t.T)


def eigen(couplings):
    table = jax.ShapeDtypeStruct((NZ, LANES), F32)
    matrix = jax.ShapeDtypeStruct((4, LANES, LANES), BF16)
    return pl.pallas_call(
        eigen_kernel,
        in_specs=[pl.BlockSpec(memory_space=pltpu.SMEM)],
        out_specs=[VMEM] * 6,
        out_shape=[table, table, matrix, matrix, matrix, matrix],
        compiler_params=grant(4),
        name="level_modes",
    )(couplings)


def decay(lam, e):
    half = 0.5 * (lam + e)
    root = jnp.sqrt(half * (2.0 + half))
    return 1.0 / (1.0 + half + root), 0.5 / root


def powers(base, count):
    square = base * base
    value = jnp.where((count & 1) != 0, base, 1.0)
    value = value * jnp.where((count & 2) != 0, square, 1.0)
    return value * jnp.where((count & 4) != 0, square * square, 1.0)


def inverse_x_kernel(
    spec0, spec1, spec2, spec3, spec4, spec5, spec6, spec7, ends, modes, lam, eig, twiddle, fh, fl, eh, el,
    out, hi, lo, above, below, eighth, steps, shelf,
):
    levels = spec0.shape[0]
    rows = levels * YB
    lev = lax.axis_index("lev")
    i = pl.program_id(0)
    band = pl.ds(pl.multiple_of(i * YB, YB), YB)
    blocks = 2 * pl.num_programs(0)

    @pl.when(i == 0)
    def _():
        b = lax.broadcasted_iota(jnp.int32, (8, LANES), 0)
        odd, half, upper = [(b & bit) != 0 for bit in (1, 2, 4)]

        def choose(mask, factor, start=1.0):
            return jnp.where(mask, factor * start, start)

        for t in range(16):
            l, h, p = t // 4, (t // 2) % 2, t % 2
            e = eig[t // 2 : t // 2 + 1, p * LANES : (p + 1) * LANES]
            r, gain = decay(lam[:, 0:1], e)
            gain = gain * r
            r2 = r * r
            r4 = r2 * r2
            eighth[t] = r4 * r4
            for n, value in enumerate(
                (r, r2, r4, ends[h, :, l, p, :] * gain, ends[h, :, l, 2 + p, :] * gain)
            ):
                shelf[t, n] = value
            for k in range(NZ):
                r1, r2, r4, up, down = [shelf[t, n, k : k + 1, :] for n in range(5)]
                above[t, k] = choose(odd, r1, up) * (choose(half, r2) * choose(upper, r4))
                below[t, k] = choose(~odd, r1, down) * (choose(~half, r2) * choose(~upper, r4))

    r8 = eighth[...]
    for o in range(2):
        steps[o] = powers(r8, 2 * i + o)
        steps[2 + o] = powers(r8, blocks - 1 - 2 * i - o)
    first_level = lev * levels
    specs = (spec0, spec1, spec2, spec3, spec4, spec5, spec6, spec7)
    for slot, spec in enumerate(specs):
        block = 2 * ((lev - slot // 2) & 3) + slot % 2
        for part in range(2):
            t = 2 * block + part
            acc = [[None, None] for _ in range(levels)]
            for k in range(NZ):
                u, d = above[t, k], below[t, k]
                for o in range(2):
                    value = u * steps[o, t, k : k + 1, :] + d * steps[2 + o, t, k : k + 1, :]
                    for z in range(levels):
                        term = value * modes[k, first_level + z]
                        acc[z][o] = term if k == 0 else acc[z][o] + term
            for z in range(levels):
                value = spec[z, band, part * LANES : (part + 1) * LANES] + jnp.concatenate(acc[z], 0)
                high, low = halves(value)
                place = pl.multiple_of(block * rows + z * YB, YB)
                half = pl.ds(part * LANES, LANES)
                hi[pl.ds(place, YB), half] = high
                lo[pl.ds(place, YB), half] = low
    first = mm3((hi[:rows, :], lo[:rows, :]), (eh[...], el[...]))
    rest = mm3((hi[rows:, :], lo[rows:, :]), (fh[...], fl[...]))
    for z in range(levels):
        real = (first[z * YB : (z + 1) * YB, :LANES], first[z * YB : (z + 1) * YB, LANES:])
        comps = []
        for i in range(7):
            place = i * rows + z * YB
            value = (rest[place : place + YB, :LANES], rest[place : place + YB, LANES:])
            comps.append(cmul(value, twiddle[i : i + 1, :], -twiddle[8 + i : 9 + i, :]))
        cells = real16_back(real, comps)
        for a in range(16):
            out[:, z, a * LANES : (a + 1) * LANES] = cells[a]


def inverse_x(specs, ends, modes, lam, eig, consts):
    levels, rows, _ = specs[0].shape
    return pl.pallas_call(
        inverse_x_kernel,
        grid=(rows // YB,),
        in_specs=[VMEM] * 9 + [pl.BlockSpec(memory_space=pltpu.SMEM)] + [VMEM] * 7,
        out_specs=pl.BlockSpec((YB, levels, N), lambda i: (i, 0, 0)),
        out_shape=jax.ShapeDtypeStruct((rows, levels, N), F32),
        scratch_shapes=[pltpu.VMEM((8 * levels * YB, 256), BF16)] * 2
        + [pltpu.VMEM((16, NZ, 8, LANES), F32)] * 2
        + [pltpu.VMEM((16, NZ, LANES), F32), pltpu.VMEM((4, 16, NZ, LANES), F32)]
        + [pltpu.VMEM((16, 5, NZ, LANES), F32)],
        compiler_params=grant(16),
        name="inverse_x",
    )(*specs, ends, modes, lam, eig, *consts)


def level_kernel(h, x0, x1, x2, x3, w2h, w2l, w4h, w4l, lam, eig, *refs):
    before = refs[:h]
    out0, out1, out2, out3, ends, f, work = refs[h:]
    lev = lax.axis_index("lev")
    rows = x0.shape[0] // 4
    w2 = (w2h[lev], w2l[lev])
    w4 = (w4h[lev], w4l[lev])
    e = eig[pl.ds(lev * 2 + h, 1), :]
    r, gain = decay(lam[:, 0:1], e)
    for o in range(rows // 8):
        block = [x[32 * o : 32 * o + 32, :] for x in (x0, x1, x2, x3)]
        value = mm3(w2, halves(jnp.concatenate(block, 0)))
        f[8 * o : 8 * o + 8] = value.reshape(8, NZ, 256)
    up = jnp.zeros((NZ, 256), F32)
    down = jnp.zeros((NZ, 256), F32)
    for y in range(rows):
        up = r * up
        work[y] = up
        up = up + f[y]
    for y in reversed(range(rows)):
        down = f[y] + r * down
        work[y] = (work[y] + down) * gain
    for value in before:
        ends[:NZ] = value[...]
    place = pl.ds(h * NZ, NZ)
    ends[place, 0, :] = up[:, :LANES]
    ends[place, 1, :] = up[:, LANES:]
    ends[place, 2, :] = down[:, :LANES]
    ends[place, 3, :] = down[:, LANES:]
    for o in range(rows // 8):
        block = work[8 * o : 8 * o + 8].reshape(LANES, 256)
        value = mm3(w4, halves(block))
        for step, out in enumerate((out0, out1, out2, out3)):
            out[:, 8 * o : 8 * o + 8, :] = value[32 * step : 32 * step + 32].reshape(4, 8, 256)


def level_solve(h, xs, weights, lam, eig, before):
    pairs, width = xs[0].shape
    rows = pairs // 4
    return pl.pallas_call(
        functools.partial(level_kernel, h),
        in_specs=[VMEM] * (10 + h),
        out_specs=[VMEM] * 5,
        out_shape=[jax.ShapeDtypeStruct((4, rows, width), F32)] * 4
        + [jax.ShapeDtypeStruct(((h + 1) * NZ, 4, LANES), F32)],
        scratch_shapes=[pltpu.VMEM((rows, NZ, width), F32)] * 2,
        compiler_params=grant(12),
    )(*xs, *weights, lam, eig, *before)


def carry_kernel(ends, lam, eig, out):
    sections = ends.shape[0]
    j = lax.axis_index("rows")
    k = lax.rem(j, NZ)
    h = lax.div(j, NZ)
    e = eig[pl.ds(lax.axis_index("lev") * 2 + h, 1), :]
    r, _ = decay(lam[pl.ds(k, 1), 0:1], e)
    for _ in range(6):
        r = r * r
    row = lax.broadcasted_iota(jnp.int32, (4, LANES), 0)
    ratio = jnp.where(lax.rem(row, 2) == 0, r[:, :LANES], r[:, LANES:])
    whole = ratio
    for _ in range(5):
        whole = whole * whole
    scale = 1.0 / (1.0 - whole)
    up = jnp.zeros((4, LANES), F32)
    down = jnp.zeros((4, LANES), F32)
    for s in range(sections):
        up = ends[s] + ratio * up
        down = ends[sections - 1 - s] + ratio * down
    up = up * scale
    down = down * scale
    first = row < 2
    ups = []
    for s in range(sections):
        ups.append(up)
        up = ends[s] + ratio * up
    for s in reversed(range(sections)):
        value = jnp.where(first, ups[s], down)
        for section in range(4):
            out[s, section] = value
        down = ends[s] + ratio * down


def carries(ends, lam, eig):
    return pl.pallas_call(
        carry_kernel,
        in_specs=[VMEM] * 3,
        out_specs=VMEM,
        out_shape=jax.ShapeDtypeStruct((ends.shape[0], 4) + ends.shape[1:], F32),
        compiler_params=grant(4),
        name="section_carries",
    )(ends, lam, eig)


def shift(value, step):
    return lax.ppermute(value, "lev", [(i, (i + step) % 4) for i in range(4)])


def body(source, solid, couplings):
    full, edge, twiddle, eig, spread = host_tables()
    fh, fl = split_host(full)
    eh, el = split_host(edge)
    fth, ftl = split_host(full.T)
    eth, etl = split_host(edge.T)
    lam, modes, w2h, w2l, w4h, w4l = eigen(couplings)
    parts = forward_x(source, solid, (spread, twiddle, fh, fl, eh, el))
    weights = (w2h, w2l, w4h, w4l)
    xs = [[parts[h]] + [shift(parts[2 * step + h], -step) for step in (1, 2, 3)] for h in range(2)]
    *parts0, ends0 = level_solve(0, xs[0], weights, lam, eig, ())
    *parts1, ends = level_solve(1, xs[1], weights, lam, eig, (ends0,))
    sent = [parts0[0]]
    for step in (1, 2, 3):
        sent.append(shift(parts0[step], step))
    specs = [sent[0], parts1[0]]
    for step in (1, 2, 3):
        specs += [sent[step], shift(parts1[step], step)]
    ends = lax.all_to_all(ends, "rows", 0, 0, tiled=True)
    ends = carries(ends, lam, eig).reshape(128, 4, LANES)
    ends = lax.all_to_all(ends, ("rows", "lev"), 0, 0, tiled=True).reshape(2, NZ, 4, 4, LANES)
    return inverse_x(specs, ends, modes, lam, eig, (twiddle, fth, ftl, eth, etl))


def solution(mesh):
    return jax.shard_map(
        body,
        mesh=mesh,
        in_specs=(P("rows", "lev", None), P("rows", "lev", None), P()),
        out_specs=P("rows", "lev", None),
        check_vma=False,
    )
```

```python
import math

import jax
import jax.numpy as jnp
import ml_dtypes
import numpy as np
from jax import lax
from jax.experimental import pallas as pl
from jax.experimental.pallas import tpu as pltpu
from jax.sharding import PartitionSpec as P

F32 = jnp.float32
BF16 = jnp.bfloat16
BY = 8
BX = 64
N = 2048
LANES = 128
NZ = 16
TURN = 2.0 * math.pi
RESIDUES = (1, 5, 9, 13, 2, 10, 4)
SWEEPS = 12


VMEM = pl.BlockSpec(memory_space=pltpu.VMEM)


def grant(mebibytes):
    return pltpu.CompilerParams(vmem_limit_bytes=mebibytes << 20)


def split_host(table):
    table = np.asarray(table, np.float32)
    high = table.astype(ml_dtypes.bfloat16)
    low = (table - high.astype(np.float32)).astype(ml_dtypes.bfloat16)
    return high, low


def host_tables():
    b = np.arange(LANES)
    m = np.arange(LANES)
    angle = TURN * np.mod(np.outer(b, m), LANES) / LANES
    scale = math.sqrt(2.0 / N)
    cos, sin = scale * np.cos(angle), scale * np.sin(angle)
    full = np.block([[cos, -sin], [sin, cos]])
    edge = np.zeros((2 * LANES, 2 * LANES))
    freq0 = np.concatenate([np.arange(65), np.arange(1, 64)])
    angle0 = TURN * np.mod(np.outer(b, freq0), LANES) / LANES
    part = np.where(np.arange(LANES)[None, :] < 65, np.cos(angle0), -np.sin(angle0)) * scale
    part[:, 0] *= math.sqrt(0.5)
    part[:, 64] *= math.sqrt(0.5)
    edge[:LANES, :LANES] = part
    freq8 = 16 * np.arange(64) + 8
    angle8 = TURN * np.mod(np.outer(b, freq8), N) / N
    edge[LANES:, LANES:] = scale * np.concatenate([np.cos(angle8), -np.sin(angle8)], 1)
    q = np.array(RESIDUES)
    twist = TURN * np.outer(q, b) / N
    twiddle = np.zeros((16, LANES), np.float32)
    twiddle[:7] = np.cos(twist)
    twiddle[8:15] = np.sin(twist)
    freqs = [np.concatenate([16 * freq0, freq8, freq8])]
    for residue in RESIDUES:
        freqs.append(np.tile(16 * m + residue, 2))
    freqs = np.concatenate(freqs)
    eigen = (4.0 * np.sin(np.pi * freqs / N) ** 2).astype(np.float32).reshape(8, 256)
    spread = (np.arange(32)[:, None] == np.arange(N)[None, :] // BX).astype(ml_dtypes.bfloat16)
    return full, edge, twiddle, eigen, spread


def halves(value):
    high = value.astype(BF16)
    return high, (value - high.astype(F32)).astype(BF16)


def mm(left, right):
    return jnp.dot(left, right, preferred_element_type=F32)


def mm3(left, right):
    return mm(left[0], right[0]) + (mm(left[1], right[0]) + mm(left[0], right[1]))


def cmul(value, cos, sin):
    re, im = value
    return re * cos + im * sin, im * cos - re * sin


def cadd(left, right):
    return left[0] + right[0], left[1] + right[1]


def csub(left, right):
    return left[0] - right[0], left[1] - right[1]


def phase(steps):
    return math.cos(TURN * steps / 16), math.sin(TURN * steps / 16)


def real16(v):
    s = [v[a] + v[a + 8] for a in range(8)]
    d = [v[a] - v[a + 8] for a in range(8)]
    u = [(d[0], -d[4])]
    for a in range(1, 4):
        u.append(cmul((d[a], -d[a + 4]), *phase(a)))
    p02, m02 = cadd(u[0], u[2]), csub(u[0], u[2])
    p13, m13 = cadd(u[1], u[3]), csub(u[1], u[3])
    y1, y9 = cadd(p02, p13), csub(p02, p13)
    y5 = (m02[0] + m13[1], m02[1] - m13[0])
    y13 = (m02[0] - m13[1], m02[1] + m13[0])
    t = [s[a] + s[a + 4] for a in range(4)]
    e = [s[a] - s[a + 4] for a in range(4)]
    z1 = cmul((e[1], -e[3]), *phase(2))
    z0 = (e[0], -e[2])
    y2, y10 = cadd(z0, z1), csub(z0, z1)
    a0, a1 = t[0] + t[2], t[1] + t[3]
    y4 = (t[0] - t[2], t[3] - t[1])
    return (a0 + a1, a0 - a1), (y1, y5, y9, y13, y2, y10, y4)


def real16_back(real, comps):
    g1, g5, g9, g13, g2, g10, g4 = comps
    a0, a1 = real[0] + real[1], real[0] - real[1]
    t = [a0 + g4[0], a1 - g4[1], a0 - g4[0], a1 + g4[1]]
    z0 = cadd(g2, g10)
    cos, sin = phase(2)
    z1 = cmul(csub(g2, g10), cos, -sin)
    e = [z0[0], z1[0], -z0[1], -z1[1]]
    s = [t[a] + e[a] for a in range(4)] + [t[a] - e[a] for a in range(4)]
    p19, m19 = cadd(g1, g9), csub(g1, g9)
    p513, m513 = cadd(g5, g13), csub(g5, g13)
    u = [cadd(p19, p513), None, csub(p19, p513), None]
    u[1] = (m19[0] - m513[1], m19[1] + m513[0])
    u[3] = (m19[0] + m513[1], m19[1] - m513[0])
    d = [None] * 8
    for a in range(4):
        cos, sin = phase(a)
        z = u[a] if a == 0 else cmul(u[a], cos, -sin)
        d[a], d[a + 4] = z[0], -z[1]
    return [s[a] + d[a] for a in range(8)] + [s[a] - d[a] for a in range(8)]


YB = 16


def forward_x_kernel(
    src, solid, spread, twiddle, fh, fl, eh, el, out0, out1, out2, out3, hi, lo, hi0, lo0
):
    lev = lax.axis_index("lev")
    levels = src.shape[1]
    rows = levels * YB
    band = pl.ds(pl.multiple_of(pl.program_id(0) * rows, rows), rows)
    open_cells = (1 - solid[...]).astype(F32).astype(BF16)
    twice = [open_cells[i] for i in range(YB // BY) for _ in range(2)]
    masks = mm(jnp.concatenate(twice, 0), spread[...])
    for part in range(levels):
        near = slice(4 * part, 4 * part + 4)
        mask_at = 8 * (part // 2)
        cells = []
        for a in range(16):
            cols = slice(a * LANES, (a + 1) * LANES)
            piece = src[near, :, cols].reshape(2, 8, LANES)
            cells.append((piece * masks[None, mask_at : mask_at + 8, cols]).reshape(16, LANES))
        real, comps = real16(cells)
        for half in range(2):
            high, low = halves(real[half])
            hi0[part * 16 : part * 16 + 16, half * LANES : (half + 1) * LANES] = high
            lo0[part * 16 : part * 16 + 16, half * LANES : (half + 1) * LANES] = low
        for i in range(1, 8):
            block = cmul(comps[i - 1], twiddle[i - 1 : i, :], twiddle[7 + i : 8 + i, :])
            slot = 2 * ((lev - i // 2) & 3) + i % 2
            place = pl.multiple_of(slot * rows + part * 16, 16)
            for half in range(2):
                high, low = halves(block[half])
                hi[pl.ds(place, 16), half * LANES : (half + 1) * LANES] = high
                lo[pl.ds(place, 16), half * LANES : (half + 1) * LANES] = low
    outs = (out0, out1, out2, out3)
    rest = mm3((hi[...], lo[...]), (fh[...], fl[...]))
    for step in range(4):
        for h in range(2):
            value = rest[(2 * step + h) * rows : (2 * step + h + 1) * rows]
            outs[step][band, h * 256 : h * 256 + 256] = value
    first = mm3((hi0[...], lo0[...]), (eh[...], el[...]))
    for step in range(4):

        @pl.when(lev == step)
        def _(step=step):
            outs[step][band, 0:256] = first


def forward_x(source, solid, consts, half):
    rows, levels, cells = source.shape
    steps = rows // YB // 2
    first = half * steps
    return pl.pallas_call(
        forward_x_kernel,
        grid=(steps,),
        in_specs=[
            pl.BlockSpec((YB, levels, cells), lambda i: (i + first, 0, 0)),
            pl.BlockSpec((YB // BY, levels, cells // BX), lambda i: (i + first, 0, 0)),
        ]
        + [pl.BlockSpec(value.shape, lambda i: (0, 0)) for value in consts],
        out_specs=[VMEM] * 4,
        out_shape=[jax.ShapeDtypeStruct((rows * levels // 2, 512), F32)] * 4,
        scratch_shapes=[pltpu.VMEM((8 * levels * YB, 256), BF16)] * 2
        + [pltpu.VMEM((levels * YB, 256), BF16)] * 2,
        compiler_params=grant(12),
        name=f"forward_x_{half}",
    )(*[pltpu.with_memory_space_constraint(value, pltpu.HBM) for value in (source, solid, *consts)])


def rsqrt(value):
    root = lax.rsqrt(value)
    return root * (1.5 - 0.5 * value * root * root)


def eigen_kernel(coup, lam, modes, w2h, w2l, w4h, w4l):
    sub = lax.broadcasted_iota(jnp.int32, (8, LANES), 0)
    lane = lax.broadcasted_iota(jnp.int32, (8, LANES), 1) & (NZ - 1)
    low = lane < 8
    g = [jnp.zeros((8, LANES), F32), jnp.zeros((8, LANES), F32)]
    link = jnp.zeros((8, LANES), F32)
    for k in range(NZ):
        pivot = coup[k] + coup[k + 1] - link * link
        inverse = rsqrt(pivot)
        here = lane == (k // 2 + 8 * (k % 2))
        g[k // 8] = jnp.where(here & (sub == k % 8), pivot * inverse, g[k // 8])
        link = -coup[k + 1] * inverse
        if k < NZ - 1:
            below = (k + 1) // 8
            g[below] = jnp.where(here & (sub == (k + 1) % 8), link, g[below])
    partners = [pltpu.roll(value, 8, 1) for value in g]

    def total(first, second):
        value = first + second
        for shift in (4, 2, 1):
            value = value + pltpu.roll(value, shift, 0)
        return value

    def right(value):
        return pltpu.roll(value, 1, 1)

    def left(value):
        return pltpu.roll(value, LANES - 1, 1)

    def step(_, carry):
        g0, g1, p0, p1, worst = carry
        own = total(g0 * g0, g1 * g1)
        other = total(p0 * p0, p1 * p1)
        a = total(g0 * p0, g1 * p1)
        d = other - own
        w = d * d + 4.0 * a * a
        h = rsqrt(w)
        x = 0.5 + 0.5 * jnp.abs(d) * h
        y = rsqrt(x)
        positive = (d > 0.0) | ((d == 0.0) & low)
        turn = a * h * y
        still = w == 0.0
        c = jnp.where(still, 1.0, x * y)
        turn = jnp.where(still, 0.0, jnp.where(positive, turn, -turn))
        worst = jnp.maximum(worst, jnp.where(still, 0.0, a * a / (own * other)))
        out = []
        for value, partner in ((g0, p0), (g1, p1)):
            mine = c * value - turn * partner
            theirs = c * partner + turn * value
            rising = right(jnp.where(lane == 0, theirs, mine))
            new = jnp.where(low, rising, jnp.where(lane == 15, theirs, left(mine)))
            new = jnp.where(lane == 0, mine, new)
            falling = right(jnp.where(lane == 8, mine, theirs))
            new_partner = jnp.where(low, jnp.where(lane == 7, mine, left(theirs)), falling)
            new_partner = jnp.where(lane == 8, theirs, new_partner)
            out.append((new, new_partner))
        return out[0][0], out[1][0], out[0][1], out[1][1], worst

    def sweep(carry):
        count, _, *state = carry
        state = lax.fori_loop(0, 15, step, (*state, jnp.zeros((8, LANES), F32)))
        return (count + 1, jnp.max(state[4]), *state[:4])

    def unfinished(carry):
        return (carry[0] < SWEEPS) & (carry[1] > 1e-7)

    state = (jnp.int32(0), jnp.float32(1.0), g[0], g[1], partners[0], partners[1])
    _, _, g0, g1, _, _ = lax.while_loop(unfinished, sweep, state)
    square = total(g0 * g0, g1 * g1)
    inverse = rsqrt(square)
    vectors = jnp.concatenate([g0 * inverse, g1 * inverse], 0)
    lam[...] = jnp.concatenate([square] * NZ, 0).T[:NZ]
    modes[...] = jnp.concatenate([vectors] * 8, 0).T[:NZ]
    wide = [jnp.broadcast_to(vectors[z : z + 1], (8, LANES)) for z in range(NZ)]
    row = lax.broadcasted_iota(jnp.int32, (LANES, LANES), 0)
    col = lax.broadcasted_iota(jnp.int32, (LANES, LANES), 1)
    for section in range(4):
        order = [wide[(z + 4 * section) % NZ] for z in range(NZ)]
        group = []
        for s in range(4):
            at = (4 * section + 4 * s) % NZ
            group += [vectors[at : at + 4]] * 8
        w4 = jnp.where(row % 8 == col // NZ, jnp.concatenate(order, 0), 0.0)
        w4h[section], w4l[section] = halves(w4)
        w2t = jnp.where(row % 32 // 4 == col // NZ, jnp.concatenate(group, 0), 0.0)
        w2h[section], w2l[section] = halves(w2t.T)


def eigen(couplings):
    table = jax.ShapeDtypeStruct((NZ, LANES), F32)
    matrix = jax.ShapeDtypeStruct((4, LANES, LANES), BF16)
    return pl.pallas_call(
        eigen_kernel,
        in_specs=[pl.BlockSpec(memory_space=pltpu.SMEM)],
        out_specs=[VMEM] * 6,
        out_shape=[table, table, matrix, matrix, matrix, matrix],
        compiler_params=grant(4),
        name="level_modes",
    )(couplings)


def decay(lam, e):
    half = 0.5 * (lam + e)
    root = jnp.sqrt(half * (2.0 + half))
    return 1.0 / (1.0 + half + root), 0.5 / root


def power_kernel(lam, eig, rise, fall, octets, shelf):
    b = lax.broadcasted_iota(jnp.int32, (8, LANES), 0)
    odd, half, upper = [(b & bit) != 0 for bit in (1, 2, 4)]

    def choose(mask, factor, start=1.0):
        return jnp.where(mask, factor * start, start)

    for t in range(16):
        e = eig[t // 2 : t // 2 + 1, (t % 2) * LANES : (t % 2 + 1) * LANES]
        r, gain = decay(lam[:, 0:1], e)
        r2 = r * r
        r4 = r2 * r2
        eighth = r4 * r4
        value = jnp.ones_like(eighth)
        for o in range(octets.shape[0]):
            octets[o, t] = value
            value = value * eighth
        for n, value in enumerate((r, r2, r4, gain * r)):
            shelf[t, n] = value
        for k in range(NZ):
            r1, r2, r4, scale = [shelf[t, n, k : k + 1, :] for n in range(4)]
            rise[t, k] = choose(odd, r1, scale) * (choose(half, r2) * choose(upper, r4))
            fall[t, k] = choose(~odd, r1, scale) * (choose(~half, r2) * choose(~upper, r4))


def power_tables(lam, eig, octets):
    table = jax.ShapeDtypeStruct((16, NZ, 8, LANES), F32)
    return pl.pallas_call(
        power_kernel,
        in_specs=[VMEM] * 2,
        out_specs=[VMEM] * 3,
        out_shape=[table, table, jax.ShapeDtypeStruct((octets, 16, NZ, LANES), F32)],
        scratch_shapes=[pltpu.VMEM((16, 4, NZ, LANES), F32)],
        compiler_params=grant(8),
        name="power_tables",
    )(lam, eig)


def inverse_x_kernel(
    spec0, spec1, spec2, spec3, ends, modes, rise, fall, octets, twiddle, fh, fl, eh, el,
    out, hi, lo, above, below,
):
    levels = spec0.shape[0]
    rows = levels * YB
    lev = lax.axis_index("lev")
    i = pl.program_id(0)
    band = pl.ds(pl.multiple_of(i * YB, YB), YB)
    last = octets.shape[0] - 1

    @pl.when(i == 0)
    def _():
        for t in range(16):
            l, h, p = t // 4, (t // 2) % 2, t % 2
            for k in range(NZ):
                above[t, k] = rise[t, k] * ends[h, k, l, p : p + 1, :]
                below[t, k] = fall[t, k] * ends[h, k, l, 2 + p : 3 + p, :]

    first_level = lev * levels
    for step, spec in enumerate((spec0, spec1, spec2, spec3)):
        l = (lev - step) & 3
        for part in range(4):
            t = 4 * l + part
            acc = [[None, None] for _ in range(levels)]
            for k in range(NZ):
                u, d = above[t, k], below[t, k]
                for o in range(2):
                    at = 2 * i + o
                    value = u * octets[at, t, k : k + 1, :] + d * octets[last - at, t, k : k + 1, :]
                    for z in range(levels):
                        term = value * modes[k, first_level + z]
                        acc[z][o] = term if k == 0 else acc[z][o] + term
            for z in range(levels):
                value = spec[z, band, part * LANES : (part + 1) * LANES] + jnp.concatenate(acc[z], 0)
                high, low = halves(value)
                place = pl.multiple_of((2 * l + part // 2) * rows + z * YB, YB)
                half = pl.ds((part % 2) * LANES, LANES)
                hi[pl.ds(place, YB), half] = high
                lo[pl.ds(place, YB), half] = low
    first = mm3((hi[:rows, :], lo[:rows, :]), (eh[...], el[...]))
    rest = mm3((hi[rows:, :], lo[rows:, :]), (fh[...], fl[...]))
    for z in range(levels):
        real = (first[z * YB : (z + 1) * YB, :LANES], first[z * YB : (z + 1) * YB, LANES:])
        comps = []
        for i in range(7):
            place = i * rows + z * YB
            value = (rest[place : place + YB, :LANES], rest[place : place + YB, LANES:])
            comps.append(cmul(value, twiddle[i : i + 1, :], -twiddle[8 + i : 9 + i, :]))
        cells = real16_back(real, comps)
        for a in range(16):
            out[:, z, a * LANES : (a + 1) * LANES] = cells[a]


def inverse_x(specs, ends, modes, tables, consts):
    levels, rows, _ = specs[0].shape
    return pl.pallas_call(
        inverse_x_kernel,
        grid=(rows // YB,),
        in_specs=[VMEM] * 5 + [pl.BlockSpec(memory_space=pltpu.SMEM)] + [VMEM] * 8,
        out_specs=pl.BlockSpec((YB, levels, N), lambda i: (i, 0, 0)),
        out_shape=jax.ShapeDtypeStruct((rows, levels, N), F32),
        scratch_shapes=[pltpu.VMEM((8 * levels * YB, 256), BF16)] * 2
        + [pltpu.VMEM((16, NZ, 8, LANES), F32)] * 2,
        compiler_params=grant(16),
        name="inverse_x",
    )(*specs, ends, modes, *tables, *consts)


def level_kernel(
    x0, x1, x2, x3, x4, x5, x6, x7, w2h, w2l, w4h, w4l, lam, eig,
    out0, out1, out2, out3, ends, f, work,
):
    lev = lax.axis_index("lev")
    octets = x0.shape[0] // 32
    rows = 16 * octets
    sources = ((x0, x1, x2, x3), (x4, x5, x6, x7))
    w2 = (w2h[lev], w2l[lev])
    w4 = (w4h[lev], w4l[lev])
    for h in range(x0.shape[1] // 256):
        cols = pl.ds(h * 256, 256)
        e = eig[pl.ds(lev * 2 + h, 1), :]
        r, gain = decay(lam[:, 0:1], e)
        for o in range(rows // 8):
            start = 32 * (o % octets)
            block = [x[start : start + 32, cols] for x in sources[o // octets]]
            value = mm3(w2, halves(jnp.concatenate(block, 0)))
            f[8 * o : 8 * o + 8] = value.reshape(8, NZ, 256)
        up = jnp.zeros((NZ, 256), F32)
        down = jnp.zeros((NZ, 256), F32)
        for y in range(rows):
            up = r * up
            work[y] = up
            up = up + f[y]
        for y in reversed(range(rows)):
            down = f[y] + r * down
            work[y] = (work[y] + down) * gain
        place = pl.ds(h * NZ, NZ)
        ends[place, 0, :] = up[:, :LANES]
        ends[place, 1, :] = up[:, LANES:]
        ends[place, 2, :] = down[:, :LANES]
        ends[place, 3, :] = down[:, LANES:]
        for o in range(rows // 8):
            block = work[8 * o : 8 * o + 8].reshape(LANES, 256)
            value = mm3(w4, halves(block))
            for step, out in enumerate((out0, out1, out2, out3)):
                out[:, 8 * o : 8 * o + 8, cols] = value[32 * step : 32 * step + 32].reshape(4, 8, 256)


def level_solve(xs, weights, lam, eig):
    pairs, width = xs[0].shape
    rows = pairs // 2
    return pl.pallas_call(
        level_kernel,
        in_specs=[VMEM] * 14,
        out_specs=[VMEM] * 5,
        out_shape=[jax.ShapeDtypeStruct((4, rows, width), F32)] * 4
        + [jax.ShapeDtypeStruct((2 * NZ, 4, LANES), F32)],
        scratch_shapes=[pltpu.VMEM((rows, NZ, 256), F32)] * 2,
        compiler_params=grant(12),
        name="level_solve",
    )(*xs, *weights, lam, eig)


def carry_kernel(ends, lam, eig, out):
    sections = ends.shape[0]
    j = lax.axis_index("rows")
    k = lax.rem(j, NZ)
    h = lax.div(j, NZ)
    e = eig[pl.ds(lax.axis_index("lev") * 2 + h, 1), :]
    r, _ = decay(lam[pl.ds(k, 1), 0:1], e)
    for _ in range(6):
        r = r * r
    row = lax.broadcasted_iota(jnp.int32, (4, LANES), 0)
    ratio = jnp.where(lax.rem(row, 2) == 0, r[:, :LANES], r[:, LANES:])
    whole = ratio
    for _ in range(5):
        whole = whole * whole
    scale = 1.0 / (1.0 - whole)
    up = jnp.zeros((4, LANES), F32)
    down = jnp.zeros((4, LANES), F32)
    for s in range(sections):
        up = ends[s] + ratio * up
        down = ends[sections - 1 - s] + ratio * down
    up = up * scale
    down = down * scale
    first = row < 2
    ups = []
    for s in range(sections):
        ups.append(up)
        up = ends[s] + ratio * up
    for s in reversed(range(sections)):
        value = jnp.where(first, ups[s], down)
        for section in range(4):
            out[s, section] = value
        down = ends[s] + ratio * down


def carries(ends, lam, eig):
    return pl.pallas_call(
        carry_kernel,
        in_specs=[VMEM] * 3,
        out_specs=VMEM,
        out_shape=jax.ShapeDtypeStruct((ends.shape[0], 4) + ends.shape[1:], F32),
        compiler_params=grant(4),
        name="section_carries",
    )(ends, lam, eig)


def shift(value, step):
    return lax.ppermute(value, "lev", [(i, (i + step) % 4) for i in range(4)])


def body(source, solid, couplings):
    full, edge, twiddle, eig, spread = host_tables()
    fh, fl = split_host(full)
    eh, el = split_host(edge)
    fth, ftl = split_host(full.T)
    eth, etl = split_host(edge.T)
    lam, modes, w2h, w2l, w4h, w4l = eigen(couplings)
    xs = []
    for half in range(2):
        parts = forward_x(source, solid, (spread, twiddle, fh, fl, eh, el), half)
        xs += [parts[0]] + [shift(parts[step], -step) for step in (1, 2, 3)]
    tables = power_tables(lam, eig, source.shape[0] // 8)
    *parts, ends = level_solve(xs, (w2h, w2l, w4h, w4l), lam, eig)
    specs = [parts[0]] + [shift(parts[step], step) for step in (1, 2, 3)]
    ends = lax.all_to_all(ends, "rows", 0, 0, tiled=True)
    ends = carries(ends, lam, eig).reshape(128, 4, LANES)
    ends = lax.all_to_all(ends, ("rows", "lev"), 0, 0, tiled=True).reshape(2, NZ, 4, 4, LANES)
    return inverse_x(specs, ends, modes, tables, (twiddle, fth, ftl, eth, etl))


def solution(mesh):
    return jax.shard_map(
        body,
        mesh=mesh,
        in_specs=(P("rows", "lev", None), P("rows", "lev", None), P()),
        out_specs=P("rows", "lev", None),
        check_vma=False,
    )
```

```python
import math

import jax
import jax.numpy as jnp
import ml_dtypes
import numpy as np
from jax import lax
from jax.experimental import pallas as pl
from jax.experimental.pallas import tpu as pltpu
from jax.sharding import PartitionSpec as P

F32 = jnp.float32
BF16 = jnp.bfloat16
BY = 8
BX = 64
N = 2048
LANES = 128
NZ = 16
TURN = 2.0 * math.pi
RESIDUES = (1, 5, 9, 13, 2, 10, 4)
SWEEPS = 12


VMEM = pl.BlockSpec(memory_space=pltpu.VMEM)


def grant(mebibytes):
    return pltpu.CompilerParams(vmem_limit_bytes=mebibytes << 20)


def split_host(table):
    table = np.asarray(table, np.float32)
    high = table.astype(ml_dtypes.bfloat16)
    low = (table - high.astype(np.float32)).astype(ml_dtypes.bfloat16)
    return high, low


def host_tables():
    b = np.arange(LANES)
    m = np.arange(LANES)
    angle = TURN * np.mod(np.outer(b, m), LANES) / LANES
    scale = math.sqrt(2.0 / N)
    cos, sin = scale * np.cos(angle), scale * np.sin(angle)
    full = np.block([[cos, -sin], [sin, cos]])
    edge = np.zeros((2 * LANES, 2 * LANES))
    freq0 = np.concatenate([np.arange(65), np.arange(1, 64)])
    angle0 = TURN * np.mod(np.outer(b, freq0), LANES) / LANES
    part = np.where(np.arange(LANES)[None, :] < 65, np.cos(angle0), -np.sin(angle0)) * scale
    part[:, 0] *= math.sqrt(0.5)
    part[:, 64] *= math.sqrt(0.5)
    edge[:LANES, :LANES] = part
    freq8 = 16 * np.arange(64) + 8
    angle8 = TURN * np.mod(np.outer(b, freq8), N) / N
    edge[LANES:, LANES:] = scale * np.concatenate([np.cos(angle8), -np.sin(angle8)], 1)
    q = np.array(RESIDUES)
    twist = TURN * np.outer(q, b) / N
    twiddle = np.zeros((16, LANES), np.float32)
    twiddle[:7] = np.cos(twist)
    twiddle[8:15] = np.sin(twist)
    freqs = [np.concatenate([16 * freq0, freq8, freq8])]
    for residue in RESIDUES:
        freqs.append(np.tile(16 * m + residue, 2))
    freqs = np.concatenate(freqs)
    eigen = (4.0 * np.sin(np.pi * freqs / N) ** 2).astype(np.float32).reshape(8, 256)
    spread = (np.arange(32)[:, None] == np.arange(N)[None, :] // BX).astype(ml_dtypes.bfloat16)
    return full, edge, twiddle, eigen, spread


def halves(value):
    high = value.astype(BF16)
    return high, (value - high.astype(F32)).astype(BF16)


def mm(left, right):
    return jnp.dot(left, right, preferred_element_type=F32)


def mm3(left, right):
    return mm(left[0], right[0]) + (mm(left[1], right[0]) + mm(left[0], right[1]))


def cmul(value, cos, sin):
    re, im = value
    return re * cos + im * sin, im * cos - re * sin


def cadd(left, right):
    return left[0] + right[0], left[1] + right[1]


def csub(left, right):
    return left[0] - right[0], left[1] - right[1]


def phase(steps):
    return math.cos(TURN * steps / 16), math.sin(TURN * steps / 16)


def real16(v):
    s = [v[a] + v[a + 8] for a in range(8)]
    d = [v[a] - v[a + 8] for a in range(8)]
    u = [(d[0], -d[4])]
    for a in range(1, 4):
        u.append(cmul((d[a], -d[a + 4]), *phase(a)))
    p02, m02 = cadd(u[0], u[2]), csub(u[0], u[2])
    p13, m13 = cadd(u[1], u[3]), csub(u[1], u[3])
    y1, y9 = cadd(p02, p13), csub(p02, p13)
    y5 = (m02[0] + m13[1], m02[1] - m13[0])
    y13 = (m02[0] - m13[1], m02[1] + m13[0])
    t = [s[a] + s[a + 4] for a in range(4)]
    e = [s[a] - s[a + 4] for a in range(4)]
    z1 = cmul((e[1], -e[3]), *phase(2))
    z0 = (e[0], -e[2])
    y2, y10 = cadd(z0, z1), csub(z0, z1)
    a0, a1 = t[0] + t[2], t[1] + t[3]
    y4 = (t[0] - t[2], t[3] - t[1])
    return (a0 + a1, a0 - a1), (y1, y5, y9, y13, y2, y10, y4)


def real16_back(real, comps):
    g1, g5, g9, g13, g2, g10, g4 = comps
    a0, a1 = real[0] + real[1], real[0] - real[1]
    t = [a0 + g4[0], a1 - g4[1], a0 - g4[0], a1 + g4[1]]
    z0 = cadd(g2, g10)
    cos, sin = phase(2)
    z1 = cmul(csub(g2, g10), cos, -sin)
    e = [z0[0], z1[0], -z0[1], -z1[1]]
    s = [t[a] + e[a] for a in range(4)] + [t[a] - e[a] for a in range(4)]
    p19, m19 = cadd(g1, g9), csub(g1, g9)
    p513, m513 = cadd(g5, g13), csub(g5, g13)
    u = [cadd(p19, p513), None, csub(p19, p513), None]
    u[1] = (m19[0] - m513[1], m19[1] + m513[0])
    u[3] = (m19[0] + m513[1], m19[1] - m513[0])
    d = [None] * 8
    for a in range(4):
        cos, sin = phase(a)
        z = u[a] if a == 0 else cmul(u[a], cos, -sin)
        d[a], d[a + 4] = z[0], -z[1]
    return [s[a] + d[a] for a in range(8)] + [s[a] - d[a] for a in range(8)]


YB = 16


def forward_x_kernel(
    src, solid, spread, twiddle, fh, fl, eh, el, out0, out1, out2, out3, hi, lo, hi0, lo0
):
    lev = lax.axis_index("lev")
    levels = src.shape[1]
    rows = levels * YB
    band = pl.ds(pl.multiple_of(pl.program_id(0) * rows, rows), rows)
    open_cells = (1 - solid[...]).astype(F32).astype(BF16)
    twice = [open_cells[i] for i in range(YB // BY) for _ in range(2)]
    masks = mm(jnp.concatenate(twice, 0), spread[...])
    for part in range(levels):
        near = slice(4 * part, 4 * part + 4)
        mask_at = 8 * (part // 2)
        cells = []
        for a in range(16):
            cols = slice(a * LANES, (a + 1) * LANES)
            piece = src[near, :, cols].reshape(2, 8, LANES)
            cells.append((piece * masks[None, mask_at : mask_at + 8, cols]).reshape(16, LANES))
        real, comps = real16(cells)
        for half in range(2):
            high, low = halves(real[half])
            hi0[part * 16 : part * 16 + 16, half * LANES : (half + 1) * LANES] = high
            lo0[part * 16 : part * 16 + 16, half * LANES : (half + 1) * LANES] = low
        for i in range(1, 8):
            block = cmul(comps[i - 1], twiddle[i - 1 : i, :], twiddle[7 + i : 8 + i, :])
            slot = 2 * ((lev - i // 2) & 3) + i % 2
            place = pl.multiple_of(slot * rows + part * 16, 16)
            for half in range(2):
                high, low = halves(block[half])
                hi[pl.ds(place, 16), half * LANES : (half + 1) * LANES] = high
                lo[pl.ds(place, 16), half * LANES : (half + 1) * LANES] = low
    outs = (out0, out1, out2, out3)
    rest = mm3((hi[...], lo[...]), (fh[...], fl[...]))
    for step in range(4):
        for h in range(2):
            value = rest[(2 * step + h) * rows : (2 * step + h + 1) * rows]
            outs[step][band, h * 256 : h * 256 + 256] = value
    first = mm3((hi0[...], lo0[...]), (eh[...], el[...]))
    for step in range(4):

        @pl.when(lev == step)
        def _(step=step):
            outs[step][band, 0:256] = first


def forward_x(source, solid, consts, half):
    rows, levels, cells = source.shape
    steps = rows // YB // 2
    first = half * steps
    return pl.pallas_call(
        forward_x_kernel,
        grid=(steps,),
        in_specs=[
            pl.BlockSpec((YB, levels, cells), lambda i: (i + first, 0, 0)),
            pl.BlockSpec((YB // BY, levels, cells // BX), lambda i: (i + first, 0, 0)),
        ]
        + [pl.BlockSpec(value.shape, lambda i: (0, 0)) for value in consts],
        out_specs=[VMEM] * 4,
        out_shape=[jax.ShapeDtypeStruct((rows * levels // 2, 512), F32)] * 4,
        scratch_shapes=[pltpu.VMEM((8 * levels * YB, 256), BF16)] * 2
        + [pltpu.VMEM((levels * YB, 256), BF16)] * 2,
        compiler_params=grant(12),
        name=f"forward_x_{half}",
    )(*[pltpu.with_memory_space_constraint(value, pltpu.HBM) for value in (source, solid, *consts)])


def rsqrt(value):
    root = lax.rsqrt(value)
    return root * (1.5 - 0.5 * value * root * root)


def eigen_kernel(coup, lam, modes, w2h, w2l, w4h, w4l):
    sub = lax.broadcasted_iota(jnp.int32, (8, LANES), 0)
    lane = lax.broadcasted_iota(jnp.int32, (8, LANES), 1) & (NZ - 1)
    low = lane < 8
    g = [jnp.zeros((8, LANES), F32), jnp.zeros((8, LANES), F32)]
    link = jnp.zeros((8, LANES), F32)
    for k in range(NZ):
        pivot = coup[k] + coup[k + 1] - link * link
        inverse = rsqrt(pivot)
        here = lane == (k // 2 + 8 * (k % 2))
        g[k // 8] = jnp.where(here & (sub == k % 8), pivot * inverse, g[k // 8])
        link = -coup[k + 1] * inverse
        if k < NZ - 1:
            below = (k + 1) // 8
            g[below] = jnp.where(here & (sub == (k + 1) % 8), link, g[below])
    partners = [pltpu.roll(value, 8, 1) for value in g]

    def total(first, second):
        value = first + second
        for shift in (4, 2, 1):
            value = value + pltpu.roll(value, shift, 0)
        return value

    def right(value):
        return pltpu.roll(value, 1, 1)

    def left(value):
        return pltpu.roll(value, LANES - 1, 1)

    def step(_, carry):
        g0, g1, p0, p1, worst = carry
        own = total(g0 * g0, g1 * g1)
        other = total(p0 * p0, p1 * p1)
        a = total(g0 * p0, g1 * p1)
        d = other - own
        w = d * d + 4.0 * a * a
        h = rsqrt(w)
        x = 0.5 + 0.5 * jnp.abs(d) * h
        y = rsqrt(x)
        positive = (d > 0.0) | ((d == 0.0) & low)
        turn = a * h * y
        still = w == 0.0
        c = jnp.where(still, 1.0, x * y)
        turn = jnp.where(still, 0.0, jnp.where(positive, turn, -turn))
        worst = jnp.maximum(worst, jnp.where(still, 0.0, a * a / (own * other)))
        out = []
        for value, partner in ((g0, p0), (g1, p1)):
            mine = c * value - turn * partner
            theirs = c * partner + turn * value
            rising = right(jnp.where(lane == 0, theirs, mine))
            new = jnp.where(low, rising, jnp.where(lane == 15, theirs, left(mine)))
            new = jnp.where(lane == 0, mine, new)
            falling = right(jnp.where(lane == 8, mine, theirs))
            new_partner = jnp.where(low, jnp.where(lane == 7, mine, left(theirs)), falling)
            new_partner = jnp.where(lane == 8, theirs, new_partner)
            out.append((new, new_partner))
        return out[0][0], out[1][0], out[0][1], out[1][1], worst

    def sweep(carry):
        count, _, *state = carry
        state = lax.fori_loop(0, 15, step, (*state, jnp.zeros((8, LANES), F32)))
        return (count + 1, jnp.max(state[4]), *state[:4])

    def unfinished(carry):
        return (carry[0] < SWEEPS) & (carry[1] > 1e-7)

    state = (jnp.int32(0), jnp.float32(1.0), g[0], g[1], partners[0], partners[1])
    _, _, g0, g1, _, _ = lax.while_loop(unfinished, sweep, state)
    square = total(g0 * g0, g1 * g1)
    inverse = rsqrt(square)
    vectors = jnp.concatenate([g0 * inverse, g1 * inverse], 0)
    lam[...] = jnp.concatenate([square] * NZ, 0).T[:NZ]
    modes[...] = jnp.concatenate([vectors] * 8, 0).T[:NZ]
    wide = [jnp.broadcast_to(vectors[z : z + 1], (8, LANES)) for z in range(NZ)]
    row = lax.broadcasted_iota(jnp.int32, (LANES, LANES), 0)
    col = lax.broadcasted_iota(jnp.int32, (LANES, LANES), 1)
    for section in range(4):
        order = [wide[(z + 4 * section) % NZ] for z in range(NZ)]
        group = []
        for s in range(4):
            at = (4 * section + 4 * s) % NZ
            group += [vectors[at : at + 4]] * 8
        w4 = jnp.where(row % 8 == col // NZ, jnp.concatenate(order, 0), 0.0)
        w4h[section], w4l[section] = halves(w4)
        w2t = jnp.where(row % 32 // 4 == col // NZ, jnp.concatenate(group, 0), 0.0)
        w2h[section], w2l[section] = halves(w2t.T)


def eigen(couplings):
    table = jax.ShapeDtypeStruct((NZ, LANES), F32)
    matrix = jax.ShapeDtypeStruct((4, LANES, LANES), BF16)
    return pl.pallas_call(
        eigen_kernel,
        in_specs=[pl.BlockSpec(memory_space=pltpu.SMEM)],
        out_specs=[VMEM] * 6,
        out_shape=[table, table, matrix, matrix, matrix, matrix],
        compiler_params=grant(4),
        name="level_modes",
    )(couplings)


def decay(lam, e):
    half = 0.5 * (lam + e)
    root = jnp.sqrt(half * (2.0 + half))
    return 1.0 / (1.0 + half + root), 0.5 / root


def powers(base, count):
    square = base * base
    value = jnp.where((count & 1) != 0, base, 1.0)
    value = value * jnp.where((count & 2) != 0, square, 1.0)
    return value * jnp.where((count & 4) != 0, square * square, 1.0)


def inverse_x_kernel(
    spec0, spec1, spec2, spec3, ends, modes, lam, eig, twiddle, fh, fl, eh, el,
    out, hi, lo, above, below, eighth, steps, shelf,
):
    levels = spec0.shape[0]
    rows = levels * YB
    lev = lax.axis_index("lev")
    i = pl.program_id(0)
    band = pl.ds(pl.multiple_of(i * YB, YB), YB)
    blocks = 2 * pl.num_programs(0)

    @pl.when(i == 0)
    def _():
        b = lax.broadcasted_iota(jnp.int32, (8, LANES), 0)
        odd, half, upper = [(b & bit) != 0 for bit in (1, 2, 4)]

        def choose(mask, factor, start=1.0):
            return jnp.where(mask, factor * start, start)

        for t in range(16):
            l, h, p = t // 4, (t // 2) % 2, t % 2
            e = eig[t // 2 : t // 2 + 1, p * LANES : (p + 1) * LANES]
            r, gain = decay(lam[:, 0:1], e)
            r2 = r * r
            r4 = r2 * r2
            eighth[t] = r4 * r4
            for n, value in enumerate((r, r2, r4, gain * r)):
                shelf[t, n] = value
            for k in range(NZ):
                r1, r2, r4, scale = [shelf[t, n, k : k + 1, :] for n in range(4)]
                up = scale * ends[h, k, l, p : p + 1, :]
                down = scale * ends[h, k, l, 2 + p : 3 + p, :]
                above[t, k] = choose(odd, r1, up) * (choose(half, r2) * choose(upper, r4))
                below[t, k] = choose(~odd, r1, down) * (choose(~half, r2) * choose(~upper, r4))

    r8 = eighth[...]
    for o in range(2):
        steps[o] = powers(r8, 2 * i + o)
        steps[2 + o] = powers(r8, blocks - 1 - 2 * i - o)
    first_level = lev * levels
    for step, spec in enumerate((spec0, spec1, spec2, spec3)):
        l = (lev - step) & 3
        for part in range(4):
            t = 4 * l + part
            acc = [[None, None] for _ in range(levels)]
            for k in range(NZ):
                u, d = above[t, k], below[t, k]
                for o in range(2):
                    value = u * steps[o, t, k : k + 1, :] + d * steps[2 + o, t, k : k + 1, :]
                    for z in range(levels):
                        term = value * modes[k, first_level + z]
                        acc[z][o] = term if k == 0 else acc[z][o] + term
            for z in range(levels):
                value = spec[z, band, part * LANES : (part + 1) * LANES] + jnp.concatenate(acc[z], 0)
                high, low = halves(value)
                place = pl.multiple_of((2 * l + part // 2) * rows + z * YB, YB)
                half = pl.ds((part % 2) * LANES, LANES)
                hi[pl.ds(place, YB), half] = high
                lo[pl.ds(place, YB), half] = low
    first = mm3((hi[:rows, :], lo[:rows, :]), (eh[...], el[...]))
    rest = mm3((hi[rows:, :], lo[rows:, :]), (fh[...], fl[...]))
    for z in range(levels):
        real = (first[z * YB : (z + 1) * YB, :LANES], first[z * YB : (z + 1) * YB, LANES:])
        comps = []
        for i in range(7):
            place = i * rows + z * YB
            value = (rest[place : place + YB, :LANES], rest[place : place + YB, LANES:])
            comps.append(cmul(value, twiddle[i : i + 1, :], -twiddle[8 + i : 9 + i, :]))
        cells = real16_back(real, comps)
        for a in range(16):
            out[:, z, a * LANES : (a + 1) * LANES] = cells[a]


def inverse_x(specs, ends, modes, lam, eig, consts):
    levels, rows, _ = specs[0].shape
    return pl.pallas_call(
        inverse_x_kernel,
        grid=(rows // YB,),
        in_specs=[VMEM] * 5 + [pl.BlockSpec(memory_space=pltpu.SMEM)] + [VMEM] * 7,
        out_specs=pl.BlockSpec((YB, levels, N), lambda i: (i, 0, 0)),
        out_shape=jax.ShapeDtypeStruct((rows, levels, N), F32),
        scratch_shapes=[pltpu.VMEM((8 * levels * YB, 256), BF16)] * 2
        + [pltpu.VMEM((16, NZ, 8, LANES), F32)] * 2
        + [pltpu.VMEM((16, NZ, LANES), F32), pltpu.VMEM((4, 16, NZ, LANES), F32)]
        + [pltpu.VMEM((16, 4, NZ, LANES), F32)],
        compiler_params=grant(16),
        name="inverse_x",
    )(*specs, ends, modes, lam, eig, *consts)


def level_kernel(
    x0, x1, x2, x3, x4, x5, x6, x7, w2h, w2l, w4h, w4l, lam, eig,
    out0, out1, out2, out3, ends, f, work,
):
    lev = lax.axis_index("lev")
    octets = x0.shape[0] // 32
    rows = 16 * octets
    sources = ((x0, x1, x2, x3), (x4, x5, x6, x7))
    w2 = (w2h[lev], w2l[lev])
    w4 = (w4h[lev], w4l[lev])
    for h in range(x0.shape[1] // 256):
        cols = pl.ds(h * 256, 256)
        e = eig[pl.ds(lev * 2 + h, 1), :]
        r, gain = decay(lam[:, 0:1], e)
        for o in range(rows // 8):
            start = 32 * (o % octets)
            block = [x[start : start + 32, cols] for x in sources[o // octets]]
            value = mm3(w2, halves(jnp.concatenate(block, 0)))
            f[8 * o : 8 * o + 8] = value.reshape(8, NZ, 256)
        up = jnp.zeros((NZ, 256), F32)
        down = jnp.zeros((NZ, 256), F32)
        for y in range(rows):
            up = r * up
            work[y] = up
            up = up + f[y]
        for y in reversed(range(rows)):
            down = f[y] + r * down
            work[y] = (work[y] + down) * gain
        place = pl.ds(h * NZ, NZ)
        ends[place, 0, :] = up[:, :LANES]
        ends[place, 1, :] = up[:, LANES:]
        ends[place, 2, :] = down[:, :LANES]
        ends[place, 3, :] = down[:, LANES:]
        for o in range(rows // 8):
            block = work[8 * o : 8 * o + 8].reshape(LANES, 256)
            value = mm3(w4, halves(block))
            for step, out in enumerate((out0, out1, out2, out3)):
                out[:, 8 * o : 8 * o + 8, cols] = value[32 * step : 32 * step + 32].reshape(4, 8, 256)


def level_solve(xs, weights, lam, eig):
    pairs, width = xs[0].shape
    rows = pairs // 2
    return pl.pallas_call(
        level_kernel,
        in_specs=[VMEM] * 14,
        out_specs=[VMEM] * 5,
        out_shape=[jax.ShapeDtypeStruct((4, rows, width), F32)] * 4
        + [jax.ShapeDtypeStruct((2 * NZ, 4, LANES), F32)],
        scratch_shapes=[pltpu.VMEM((rows, NZ, 256), F32)] * 2,
        compiler_params=grant(12),
        name="level_solve",
    )(*xs, *weights, lam, eig)


def carry_kernel(ends, lam, eig, out):
    sections = ends.shape[0]
    j = lax.axis_index("rows")
    k = lax.rem(j, NZ)
    h = lax.div(j, NZ)
    e = eig[pl.ds(lax.axis_index("lev") * 2 + h, 1), :]
    r, _ = decay(lam[pl.ds(k, 1), 0:1], e)
    for _ in range(6):
        r = r * r
    row = lax.broadcasted_iota(jnp.int32, (4, LANES), 0)
    ratio = jnp.where(lax.rem(row, 2) == 0, r[:, :LANES], r[:, LANES:])
    whole = ratio
    for _ in range(5):
        whole = whole * whole
    scale = 1.0 / (1.0 - whole)
    up = jnp.zeros((4, LANES), F32)
    down = jnp.zeros((4, LANES), F32)
    for s in range(sections):
        up = ends[s] + ratio * up
        down = ends[sections - 1 - s] + ratio * down
    up = up * scale
    down = down * scale
    first = row < 2
    ups = []
    for s in range(sections):
        ups.append(up)
        up = ends[s] + ratio * up
    for s in reversed(range(sections)):
        value = jnp.where(first, ups[s], down)
        for section in range(4):
            out[s, section] = value
        down = ends[s] + ratio * down


def carries(ends, lam, eig):
    return pl.pallas_call(
        carry_kernel,
        in_specs=[VMEM] * 3,
        out_specs=VMEM,
        out_shape=jax.ShapeDtypeStruct((ends.shape[0], 4) + ends.shape[1:], F32),
        compiler_params=grant(4),
        name="section_carries",
    )(ends, lam, eig)


def shift(value, step):
    return lax.ppermute(value, "lev", [(i, (i + step) % 4) for i in range(4)])


def body(source, solid, couplings):
    full, edge, twiddle, eig, spread = host_tables()
    fh, fl = split_host(full)
    eh, el = split_host(edge)
    fth, ftl = split_host(full.T)
    eth, etl = split_host(edge.T)
    lam, modes, w2h, w2l, w4h, w4l = eigen(couplings)
    xs = []
    for half in range(2):
        parts = forward_x(source, solid, (spread, twiddle, fh, fl, eh, el), half)
        xs += [parts[0]] + [shift(parts[step], -step) for step in (1, 2, 3)]
    *parts, ends = level_solve(xs, (w2h, w2l, w4h, w4l), lam, eig)
    specs = [parts[0]] + [shift(parts[step], step) for step in (1, 2, 3)]
    ends = lax.all_to_all(ends, "rows", 0, 0, tiled=True)
    ends = carries(ends, lam, eig).reshape(128, 4, LANES)
    ends = lax.all_to_all(ends, ("rows", "lev"), 0, 0, tiled=True).reshape(2, NZ, 4, 4, LANES)
    return inverse_x(specs, ends, modes, lam, eig, (twiddle, fth, ftl, eth, etl))


def solution(mesh):
    return jax.shard_map(
        body,
        mesh=mesh,
        in_specs=(P("rows", "lev", None), P("rows", "lev", None), P()),
        out_specs=P("rows", "lev", None),
        check_vma=False,
    )
```

```python
import math

import jax
import jax.numpy as jnp
import ml_dtypes
import numpy as np
from jax import lax
from jax.experimental import pallas as pl
from jax.experimental.pallas import tpu as pltpu
from jax.sharding import PartitionSpec as P

F32 = jnp.float32
BF16 = jnp.bfloat16
BY = 8
BX = 64
N = 2048
LANES = 128
NZ = 16
TURN = 2.0 * math.pi
RESIDUES = (1, 5, 9, 13, 2, 10, 4)
SWEEPS = 12
TILES = 4


VMEM = pl.BlockSpec(memory_space=pltpu.VMEM)


def grant(mebibytes):
    return pltpu.CompilerParams(vmem_limit_bytes=mebibytes << 20)


def split_host(table):
    table = np.asarray(table, np.float32)
    high = table.astype(ml_dtypes.bfloat16)
    low = (table - high.astype(np.float32)).astype(ml_dtypes.bfloat16)
    return high, low


def host_tables():
    b = np.arange(LANES)
    m = np.arange(LANES)
    angle = TURN * np.mod(np.outer(b, m), LANES) / LANES
    scale = math.sqrt(2.0 / N)
    cos, sin = scale * np.cos(angle), scale * np.sin(angle)
    full = np.block([[cos, -sin], [sin, cos]])
    edge = np.zeros((2 * LANES, 2 * LANES))
    freq0 = np.concatenate([np.arange(65), np.arange(1, 64)])
    angle0 = TURN * np.mod(np.outer(b, freq0), LANES) / LANES
    part = np.where(np.arange(LANES)[None, :] < 65, np.cos(angle0), -np.sin(angle0)) * scale
    part[:, 0] *= math.sqrt(0.5)
    part[:, 64] *= math.sqrt(0.5)
    edge[:LANES, :LANES] = part
    freq8 = 16 * np.arange(64) + 8
    angle8 = TURN * np.mod(np.outer(b, freq8), N) / N
    edge[LANES:, LANES:] = scale * np.concatenate([np.cos(angle8), -np.sin(angle8)], 1)
    q = np.array(RESIDUES)
    twist = TURN * np.outer(q, b) / N
    twiddle = np.zeros((16, LANES), np.float32)
    twiddle[:7] = np.cos(twist)
    twiddle[8:15] = np.sin(twist)
    freqs = [np.concatenate([16 * freq0, freq8, freq8])]
    for residue in RESIDUES:
        freqs.append(np.tile(16 * m + residue, 2))
    freqs = np.concatenate(freqs)
    eigen = (4.0 * np.sin(np.pi * freqs / N) ** 2).astype(np.float32).reshape(8, 256)
    spread = (np.arange(32)[:, None] == np.arange(N)[None, :] // BX).astype(ml_dtypes.bfloat16)
    return full, edge, twiddle, eigen, spread


def halves(value):
    high = value.astype(BF16)
    return high, (value - high.astype(F32)).astype(BF16)


def mm(left, right):
    return jnp.dot(left, right, preferred_element_type=F32)


def mm3(left, right):
    return mm(left[0], right[0]) + (mm(left[1], right[0]) + mm(left[0], right[1]))


def cmul(value, cos, sin):
    re, im = value
    return re * cos + im * sin, im * cos - re * sin


def cadd(left, right):
    return left[0] + right[0], left[1] + right[1]


def csub(left, right):
    return left[0] - right[0], left[1] - right[1]


def phase(steps):
    return math.cos(TURN * steps / 16), math.sin(TURN * steps / 16)


def real16(v):
    s = [v[a] + v[a + 8] for a in range(8)]
    d = [v[a] - v[a + 8] for a in range(8)]
    u = [(d[0], -d[4])]
    for a in range(1, 4):
        u.append(cmul((d[a], -d[a + 4]), *phase(a)))
    p02, m02 = cadd(u[0], u[2]), csub(u[0], u[2])
    p13, m13 = cadd(u[1], u[3]), csub(u[1], u[3])
    y1, y9 = cadd(p02, p13), csub(p02, p13)
    y5 = (m02[0] + m13[1], m02[1] - m13[0])
    y13 = (m02[0] - m13[1], m02[1] + m13[0])
    t = [s[a] + s[a + 4] for a in range(4)]
    e = [s[a] - s[a + 4] for a in range(4)]
    z1 = cmul((e[1], -e[3]), *phase(2))
    z0 = (e[0], -e[2])
    y2, y10 = cadd(z0, z1), csub(z0, z1)
    a0, a1 = t[0] + t[2], t[1] + t[3]
    y4 = (t[0] - t[2], t[3] - t[1])
    return (a0 + a1, a0 - a1), (y1, y5, y9, y13, y2, y10, y4)


def real16_back(real, comps):
    g1, g5, g9, g13, g2, g10, g4 = comps
    a0, a1 = real[0] + real[1], real[0] - real[1]
    t = [a0 + g4[0], a1 - g4[1], a0 - g4[0], a1 + g4[1]]
    z0 = cadd(g2, g10)
    cos, sin = phase(2)
    z1 = cmul(csub(g2, g10), cos, -sin)
    e = [z0[0], z1[0], -z0[1], -z1[1]]
    s = [t[a] + e[a] for a in range(4)] + [t[a] - e[a] for a in range(4)]
    p19, m19 = cadd(g1, g9), csub(g1, g9)
    p513, m513 = cadd(g5, g13), csub(g5, g13)
    u = [cadd(p19, p513), None, csub(p19, p513), None]
    u[1] = (m19[0] - m513[1], m19[1] + m513[0])
    u[3] = (m19[0] + m513[1], m19[1] - m513[0])
    d = [None] * 8
    for a in range(4):
        cos, sin = phase(a)
        z = u[a] if a == 0 else cmul(u[a], cos, -sin)
        d[a], d[a + 4] = z[0], -z[1]
    return [s[a] + d[a] for a in range(8)] + [s[a] - d[a] for a in range(8)]


YB = 16


def forward_x_kernel(
    src, solid, spread, twiddle, fh, fl, eh, el, out0, out1, out2, out3, hi, lo, hi0, lo0
):
    lev = lax.axis_index("lev")
    levels = src.shape[1]
    rows = levels * YB
    band = pl.ds(pl.multiple_of(pl.program_id(0) * rows, rows), rows)
    open_cells = (1 - solid[...]).astype(F32).astype(BF16)
    twice = [open_cells[i] for i in range(YB // BY) for _ in range(2)]
    masks = mm(jnp.concatenate(twice, 0), spread[...])
    for part in range(levels):
        near = slice(4 * part, 4 * part + 4)
        mask_at = 8 * (part // 2)
        cells = []
        for a in range(16):
            cols = slice(a * LANES, (a + 1) * LANES)
            piece = src[near, :, cols].reshape(2, 8, LANES)
            cells.append((piece * masks[None, mask_at : mask_at + 8, cols]).reshape(16, LANES))
        real, comps = real16(cells)
        for half in range(2):
            high, low = halves(real[half])
            hi0[part * 16 : part * 16 + 16, half * LANES : (half + 1) * LANES] = high
            lo0[part * 16 : part * 16 + 16, half * LANES : (half + 1) * LANES] = low
        for i in range(1, 8):
            block = cmul(comps[i - 1], twiddle[i - 1 : i, :], twiddle[7 + i : 8 + i, :])
            slot = 2 * ((lev - i // 2) & 3) + i % 2
            place = pl.multiple_of(slot * rows + part * 16, 16)
            for half in range(2):
                high, low = halves(block[half])
                hi[pl.ds(place, 16), half * LANES : (half + 1) * LANES] = high
                lo[pl.ds(place, 16), half * LANES : (half + 1) * LANES] = low
    outs = (out0, out1, out2, out3)
    rest = mm3((hi[...], lo[...]), (fh[...], fl[...]))
    for step in range(4):
        for h in range(2):
            value = rest[(2 * step + h) * rows : (2 * step + h + 1) * rows]
            outs[step][band, h * 256 : h * 256 + 256] = value
    first = mm3((hi0[...], lo0[...]), (eh[...], el[...]))
    for step in range(4):

        @pl.when(lev == step)
        def _(step=step):
            outs[step][band, 0:256] = first


def forward_x(source, solid, consts, half):
    rows, levels, cells = source.shape
    steps = rows // YB // 2
    first = half * steps
    return pl.pallas_call(
        forward_x_kernel,
        grid=(steps,),
        in_specs=[
            pl.BlockSpec((YB, levels, cells), lambda i: (i + first, 0, 0)),
            pl.BlockSpec((YB // BY, levels, cells // BX), lambda i: (i + first, 0, 0)),
        ]
        + [pl.BlockSpec(value.shape, lambda i: (0, 0)) for value in consts],
        out_specs=[VMEM] * 4,
        out_shape=[jax.ShapeDtypeStruct((rows * levels // 2, 512), F32)] * 4,
        scratch_shapes=[pltpu.VMEM((8 * levels * YB, 256), BF16)] * 2
        + [pltpu.VMEM((levels * YB, 256), BF16)] * 2,
        compiler_params=grant(12),
        name=f"forward_x_{half}",
    )(*[pltpu.with_memory_space_constraint(value, pltpu.HBM) for value in (source, solid, *consts)])


def rsqrt(value):
    root = lax.rsqrt(value)
    return root * (1.5 - 0.5 * value * root * root)


def eigen_kernel(coup, lam, modes, w2h, w2l, w4h, w4l):
    sub = lax.broadcasted_iota(jnp.int32, (8, LANES), 0)
    lane = lax.broadcasted_iota(jnp.int32, (8, LANES), 1) & (NZ - 1)
    low = lane < 8
    g = [jnp.zeros((8, LANES), F32), jnp.zeros((8, LANES), F32)]
    link = jnp.zeros((8, LANES), F32)
    for k in range(NZ):
        pivot = coup[k] + coup[k + 1] - link * link
        inverse = rsqrt(pivot)
        here = lane == (k // 2 + 8 * (k % 2))
        g[k // 8] = jnp.where(here & (sub == k % 8), pivot * inverse, g[k // 8])
        link = -coup[k + 1] * inverse
        if k < NZ - 1:
            below = (k + 1) // 8
            g[below] = jnp.where(here & (sub == (k + 1) % 8), link, g[below])
    partners = [pltpu.roll(value, 8, 1) for value in g]

    def total(first, second):
        value = first + second
        for shift in (4, 2, 1):
            value = value + pltpu.roll(value, shift, 0)
        return value

    def right(value):
        return pltpu.roll(value, 1, 1)

    def left(value):
        return pltpu.roll(value, LANES - 1, 1)

    def step(_, carry):
        g0, g1, p0, p1, worst = carry
        own = total(g0 * g0, g1 * g1)
        other = total(p0 * p0, p1 * p1)
        a = total(g0 * p0, g1 * p1)
        d = other - own
        w = d * d + 4.0 * a * a
        h = rsqrt(w)
        x = 0.5 + 0.5 * jnp.abs(d) * h
        y = rsqrt(x)
        positive = (d > 0.0) | ((d == 0.0) & low)
        turn = a * h * y
        still = w == 0.0
        c = jnp.where(still, 1.0, x * y)
        turn = jnp.where(still, 0.0, jnp.where(positive, turn, -turn))
        worst = jnp.maximum(worst, jnp.where(still, 0.0, a * a / (own * other)))
        out = []
        for value, partner in ((g0, p0), (g1, p1)):
            mine = c * value - turn * partner
            theirs = c * partner + turn * value
            rising = right(jnp.where(lane == 0, theirs, mine))
            new = jnp.where(low, rising, jnp.where(lane == 15, theirs, left(mine)))
            new = jnp.where(lane == 0, mine, new)
            falling = right(jnp.where(lane == 8, mine, theirs))
            new_partner = jnp.where(low, jnp.where(lane == 7, mine, left(theirs)), falling)
            new_partner = jnp.where(lane == 8, theirs, new_partner)
            out.append((new, new_partner))
        return out[0][0], out[1][0], out[0][1], out[1][1], worst

    def sweep(carry):
        count, _, *state = carry
        state = lax.fori_loop(0, 15, step, (*state, jnp.zeros((8, LANES), F32)))
        return (count + 1, jnp.max(state[4]), *state[:4])

    def unfinished(carry):
        return (carry[0] < SWEEPS) & (carry[1] > 1e-7)

    state = (jnp.int32(0), jnp.float32(1.0), g[0], g[1], partners[0], partners[1])
    _, _, g0, g1, _, _ = lax.while_loop(unfinished, sweep, state)
    square = total(g0 * g0, g1 * g1)
    inverse = rsqrt(square)
    vectors = jnp.concatenate([g0 * inverse, g1 * inverse], 0)
    lam[...] = jnp.concatenate([square] * NZ, 0).T[:NZ]
    modes[...] = jnp.concatenate([vectors] * 8, 0).T[:NZ]
    row = lax.broadcasted_iota(jnp.int32, (LANES, LANES), 0)
    col = lax.broadcasted_iota(jnp.int32, (LANES, LANES), 1)
    for section in range(4):
        group = []
        for s in range(4):
            at = (4 * section + 4 * s) % NZ
            group += [vectors[at : at + 4]] * 8
        w4 = jnp.where(row % 32 // 4 == col // NZ, jnp.concatenate(group, 0), 0.0)
        w4h[section], w4l[section] = halves(w4)
        w2h[section], w2l[section] = halves(w4.T)


def eigen(couplings):
    table = jax.ShapeDtypeStruct((NZ, LANES), F32)
    matrix = jax.ShapeDtypeStruct((4, LANES, LANES), BF16)
    return pl.pallas_call(
        eigen_kernel,
        in_specs=[pl.BlockSpec(memory_space=pltpu.SMEM)],
        out_specs=[VMEM] * 6,
        out_shape=[table, table, matrix, matrix, matrix, matrix],
        compiler_params=grant(4),
        name="level_modes",
    )(couplings)


def decay(lam, e):
    half = 0.5 * (lam + e)
    root = jnp.sqrt(half * (2.0 + half))
    return 1.0 / (1.0 + half + root), 0.5 / root


def powers(base, count):
    square = base * base
    value = jnp.where((count & 1) != 0, base, 1.0)
    value = value * jnp.where((count & 2) != 0, square, 1.0)
    return value * jnp.where((count & 4) != 0, square * square, 1.0)


def inverse_x_kernel(
    spec0, spec1, spec2, spec3, ends, modes, lam, eig, twiddle, fh, fl, eh, el,
    out, hi, lo, above, below, eighth, steps, shelf, turn,
):
    levels = out.shape[1]
    rows = levels * YB
    lev = lax.axis_index("lev")
    i = pl.program_id(0)
    blocks = 2 * pl.num_programs(0)

    @pl.when(i == 0)
    def _():
        b = lax.broadcasted_iota(jnp.int32, (8, LANES), 0)
        odd, half, upper = [(b & bit) != 0 for bit in (1, 2, 4)]

        def choose(mask, factor, start=1.0):
            return jnp.where(mask, factor * start, start)

        for t in range(16):
            l, h, p = t // 4, (t // 2) % 2, t % 2
            e = eig[t // 2 : t // 2 + 1, p * LANES : (p + 1) * LANES]
            r, gain = decay(lam[:, 0:1], e)
            r2 = r * r
            r4 = r2 * r2
            eighth[t] = r4 * r4
            for n, value in enumerate((r, r2, r4, gain * r)):
                shelf[t, n] = value
            for k in range(NZ):
                r1, r2, r4, scale = [shelf[t, n, k : k + 1, :] for n in range(4)]
                up = scale * ends[h, k, l, p : p + 1, :]
                down = scale * ends[h, k, l, 2 + p : 3 + p, :]
                above[t, k] = choose(odd, r1, up) * (choose(half, r2) * choose(upper, r4))
                below[t, k] = choose(~odd, r1, down) * (choose(~half, r2) * choose(~upper, r4))

    r8 = eighth[...]
    for o in range(2):
        steps[o] = powers(r8, 2 * i + o)
        steps[2 + o] = powers(r8, blocks - 1 - 2 * i - o)
    first_level = lev * levels
    for step, spec in enumerate((spec0, spec1, spec2, spec3)):
        l = (lev - step) & 3
        for group in range(4 // TILES):
            parts = range(group * TILES, (group + 1) * TILES)
            acc = {}
            for k in range(NZ):
                scale = [modes[k, first_level + z] for z in range(levels)]
                for part in parts:
                    t = 4 * l + part
                    u, d = above[t, k], below[t, k]
                    for o in range(2):
                        value = u * steps[o, t, k : k + 1, :] + d * steps[2 + o, t, k : k + 1, :]
                        for z in range(levels):
                            term = value * scale[z]
                            acc[part, z, o] = term if k == 0 else acc[part, z, o] + term
            for part in parts:
                place = turn.at[4 * step + part]
                for o in range(2):
                    for z in range(levels):
                        place[pl.ds(32 * o + z, 8, stride=4), :] = acc[part, z, o]
        for part in range(4):
            for q in range(rows // 16):
                near = pl.ds(pl.multiple_of(i * rows + 16 * q, 16), 16)
                value = spec[near, part * LANES : (part + 1) * LANES]
                value = value + turn[4 * step + part, 16 * q : 16 * q + 16, :]
                high, low = halves(value)
                place = pl.multiple_of((2 * l + part // 2) * rows + 16 * q, 16)
                half = pl.ds((part % 2) * LANES, LANES)
                hi[pl.ds(place, 16), half] = high
                lo[pl.ds(place, 16), half] = low
    first = mm3((hi[:rows, :], lo[:rows, :]), (eh[...], el[...]))
    rest = mm3((hi[rows:, :], lo[rows:, :]), (fh[...], fl[...]))
    for q in range(rows // 16):
        at = slice(16 * q, 16 * q + 16)
        real = (first[at, :LANES], first[at, LANES:])
        comps = []
        for n in range(7):
            at = slice(n * rows + 16 * q, n * rows + 16 * q + 16)
            value = (rest[at, :LANES], rest[at, LANES:])
            comps.append(cmul(value, twiddle[n : n + 1, :], -twiddle[8 + n : 9 + n, :]))
        cells = real16_back(real, comps)
        for a in range(16):
            out[4 * q : 4 * q + 4, :, a * LANES : (a + 1) * LANES] = cells[a].reshape(4, levels, LANES)


def inverse_x(specs, ends, modes, lam, eig, consts):
    levels = 4
    rows = specs[0].shape[0] // levels
    return pl.pallas_call(
        inverse_x_kernel,
        grid=(rows // YB,),
        in_specs=[VMEM] * 5 + [pl.BlockSpec(memory_space=pltpu.SMEM)] + [VMEM] * 7,
        out_specs=pl.BlockSpec((YB, levels, N), lambda i: (i, 0, 0)),
        out_shape=jax.ShapeDtypeStruct((rows, levels, N), F32),
        scratch_shapes=[pltpu.VMEM((8 * levels * YB, 256), BF16)] * 2
        + [pltpu.VMEM((16, NZ, 8, LANES), F32)] * 2
        + [pltpu.VMEM((16, NZ, LANES), F32), pltpu.VMEM((4, 16, NZ, LANES), F32)]
        + [pltpu.VMEM((16, 4, NZ, LANES), F32), pltpu.VMEM((16, 4 * YB, LANES), F32)],
        compiler_params=grant(16),
        name="inverse_x",
    )(*specs, ends, modes, lam, eig, *consts)


def level_kernel(
    x0, x1, x2, x3, x4, x5, x6, x7, w2h, w2l, w4h, w4l, lam, eig,
    out0, out1, out2, out3, ends, f, work,
):
    lev = lax.axis_index("lev")
    octets = x0.shape[0] // 32
    rows = 16 * octets
    sources = ((x0, x1, x2, x3), (x4, x5, x6, x7))
    w2 = (w2h[lev], w2l[lev])
    w4 = (w4h[lev], w4l[lev])
    for h in range(x0.shape[1] // 256):
        cols = pl.ds(h * 256, 256)
        e = eig[pl.ds(lev * 2 + h, 1), :]
        r, gain = decay(lam[:, 0:1], e)
        for o in range(rows // 8):
            start = 32 * (o % octets)
            block = [x[start : start + 32, cols] for x in sources[o // octets]]
            value = mm3(w2, halves(jnp.concatenate(block, 0)))
            f[8 * o : 8 * o + 8] = value.reshape(8, NZ, 256)
        up = jnp.zeros((NZ, 256), F32)
        down = jnp.zeros((NZ, 256), F32)
        for y in range(rows):
            up = r * up
            work[y] = up
            up = up + f[y]
        for y in reversed(range(rows)):
            down = f[y] + r * down
            work[y] = (work[y] + down) * gain
        place = pl.ds(h * NZ, NZ)
        ends[place, 0, :] = up[:, :LANES]
        ends[place, 1, :] = up[:, LANES:]
        ends[place, 2, :] = down[:, :LANES]
        ends[place, 3, :] = down[:, LANES:]
        for o in range(rows // 8):
            block = work[8 * o : 8 * o + 8].reshape(LANES, 256)
            value = mm3(w4, halves(block))
            for step, out in enumerate((out0, out1, out2, out3)):
                out[32 * o : 32 * o + 32, cols] = value[32 * step : 32 * step + 32]


def level_solve(xs, weights, lam, eig):
    pairs, width = xs[0].shape
    rows = pairs // 2
    return pl.pallas_call(
        level_kernel,
        in_specs=[VMEM] * 14,
        out_specs=[VMEM] * 5,
        out_shape=[jax.ShapeDtypeStruct((4 * rows, width), F32)] * 4
        + [jax.ShapeDtypeStruct((2 * NZ, 4, LANES), F32)],
        scratch_shapes=[pltpu.VMEM((rows, NZ, 256), F32)] * 2,
        compiler_params=grant(12),
        name="level_solve",
    )(*xs, *weights, lam, eig)


def carry_kernel(ends, lam, eig, out):
    sections = ends.shape[0]
    j = lax.axis_index("rows")
    k = lax.rem(j, NZ)
    h = lax.div(j, NZ)
    e = eig[pl.ds(lax.axis_index("lev") * 2 + h, 1), :]
    r, _ = decay(lam[pl.ds(k, 1), 0:1], e)
    for _ in range(6):
        r = r * r
    row = lax.broadcasted_iota(jnp.int32, (4, LANES), 0)
    ratio = jnp.where(lax.rem(row, 2) == 0, r[:, :LANES], r[:, LANES:])
    whole = ratio
    for _ in range(5):
        whole = whole * whole
    scale = 1.0 / (1.0 - whole)
    up = jnp.zeros((4, LANES), F32)
    down = jnp.zeros((4, LANES), F32)
    for s in range(sections):
        up = ends[s] + ratio * up
        down = ends[sections - 1 - s] + ratio * down
    up = up * scale
    down = down * scale
    first = row < 2
    ups = []
    for s in range(sections):
        ups.append(up)
        up = ends[s] + ratio * up
    for s in reversed(range(sections)):
        value = jnp.where(first, ups[s], down)
        for section in range(4):
            out[s, section] = value
        down = ends[s] + ratio * down


def carries(ends, lam, eig):
    return pl.pallas_call(
        carry_kernel,
        in_specs=[VMEM] * 3,
        out_specs=VMEM,
        out_shape=jax.ShapeDtypeStruct((ends.shape[0], 4) + ends.shape[1:], F32),
        compiler_params=grant(4),
        name="section_carries",
    )(ends, lam, eig)


def shift(value, step):
    return lax.ppermute(value, "lev", [(i, (i + step) % 4) for i in range(4)])


def body(source, solid, couplings):
    full, edge, twiddle, eig, spread = host_tables()
    fh, fl = split_host(full)
    eh, el = split_host(edge)
    fth, ftl = split_host(full.T)
    eth, etl = split_host(edge.T)
    lam, modes, w2h, w2l, w4h, w4l = eigen(couplings)
    xs = []
    for half in range(2):
        parts = forward_x(source, solid, (spread, twiddle, fh, fl, eh, el), half)
        xs += [parts[0]] + [shift(parts[step], -step) for step in (1, 2, 3)]
    *parts, ends = level_solve(xs, (w2h, w2l, w4h, w4l), lam, eig)
    specs = [parts[0]] + [shift(parts[step], step) for step in (1, 2, 3)]
    ends = lax.all_to_all(ends, "rows", 0, 0, tiled=True)
    ends = carries(ends, lam, eig).reshape(128, 4, LANES)
    ends = lax.all_to_all(ends, ("rows", "lev"), 0, 0, tiled=True).reshape(2, NZ, 4, 4, LANES)
    return inverse_x(specs, ends, modes, lam, eig, (twiddle, fth, ftl, eth, etl))


def solution(mesh):
    return jax.shard_map(
        body,
        mesh=mesh,
        in_specs=(P("rows", "lev", None), P("rows", "lev", None), P()),
        out_specs=P("rows", "lev", None),
        check_vma=False,
    )
```

```python
import math

import jax
import jax.numpy as jnp
import ml_dtypes
import numpy as np
from jax import lax
from jax.experimental import pallas as pl
from jax.experimental.pallas import tpu as pltpu
from jax.sharding import PartitionSpec as P

F32 = jnp.float32
BF16 = jnp.bfloat16
BY = 8
BX = 64
N = 2048
LANES = 128
NZ = 16
TURN = 2.0 * math.pi
RESIDUES = (1, 5, 9, 13, 2, 10, 4)
SWEEPS = 12
TILES = 4


VMEM = pl.BlockSpec(memory_space=pltpu.VMEM)


def grant(mebibytes):
    return pltpu.CompilerParams(vmem_limit_bytes=mebibytes << 20)


def split_host(table):
    table = np.asarray(table, np.float32)
    high = table.astype(ml_dtypes.bfloat16)
    low = (table - high.astype(np.float32)).astype(ml_dtypes.bfloat16)
    return high, low


def host_tables():
    b = np.arange(LANES)
    m = np.arange(LANES)
    angle = TURN * np.mod(np.outer(b, m), LANES) / LANES
    scale = math.sqrt(2.0 / N)
    cos, sin = scale * np.cos(angle), scale * np.sin(angle)
    full = np.block([[cos, -sin], [sin, cos]])
    edge = np.zeros((2 * LANES, 2 * LANES))
    freq0 = np.concatenate([np.arange(65), np.arange(1, 64)])
    angle0 = TURN * np.mod(np.outer(b, freq0), LANES) / LANES
    part = np.where(np.arange(LANES)[None, :] < 65, np.cos(angle0), -np.sin(angle0)) * scale
    part[:, 0] *= math.sqrt(0.5)
    part[:, 64] *= math.sqrt(0.5)
    edge[:LANES, :LANES] = part
    freq8 = 16 * np.arange(64) + 8
    angle8 = TURN * np.mod(np.outer(b, freq8), N) / N
    edge[LANES:, LANES:] = scale * np.concatenate([np.cos(angle8), -np.sin(angle8)], 1)
    q = np.array(RESIDUES)
    twist = TURN * np.outer(q, b) / N
    twiddle = np.zeros((16, LANES), np.float32)
    twiddle[:7] = np.cos(twist)
    twiddle[8:15] = np.sin(twist)
    freqs = [np.concatenate([16 * freq0, freq8, freq8])]
    for residue in RESIDUES:
        freqs.append(np.tile(16 * m + residue, 2))
    freqs = np.concatenate(freqs)
    eigen = (4.0 * np.sin(np.pi * freqs / N) ** 2).astype(np.float32).reshape(8, 256)
    spread = (np.arange(32)[:, None] == np.arange(N)[None, :] // BX).astype(ml_dtypes.bfloat16)
    return full, edge, twiddle, eigen, spread


def halves(value):
    high = value.astype(BF16)
    return high, (value - high.astype(F32)).astype(BF16)


def mm(left, right):
    return jnp.dot(left, right, preferred_element_type=F32)


def mm3(left, right):
    return mm(left[0], right[0]) + (mm(left[1], right[0]) + mm(left[0], right[1]))


def cmul(value, cos, sin):
    re, im = value
    return re * cos + im * sin, im * cos - re * sin


def cadd(left, right):
    return left[0] + right[0], left[1] + right[1]


def csub(left, right):
    return left[0] - right[0], left[1] - right[1]


def phase(steps):
    return math.cos(TURN * steps / 16), math.sin(TURN * steps / 16)


def real16(v):
    s = [v[a] + v[a + 8] for a in range(8)]
    d = [v[a] - v[a + 8] for a in range(8)]
    u = [(d[0], -d[4])]
    for a in range(1, 4):
        u.append(cmul((d[a], -d[a + 4]), *phase(a)))
    p02, m02 = cadd(u[0], u[2]), csub(u[0], u[2])
    p13, m13 = cadd(u[1], u[3]), csub(u[1], u[3])
    y1, y9 = cadd(p02, p13), csub(p02, p13)
    y5 = (m02[0] + m13[1], m02[1] - m13[0])
    y13 = (m02[0] - m13[1], m02[1] + m13[0])
    t = [s[a] + s[a + 4] for a in range(4)]
    e = [s[a] - s[a + 4] for a in range(4)]
    z1 = cmul((e[1], -e[3]), *phase(2))
    z0 = (e[0], -e[2])
    y2, y10 = cadd(z0, z1), csub(z0, z1)
    a0, a1 = t[0] + t[2], t[1] + t[3]
    y4 = (t[0] - t[2], t[3] - t[1])
    return (a0 + a1, a0 - a1), (y1, y5, y9, y13, y2, y10, y4)


def real16_back(real, comps):
    g1, g5, g9, g13, g2, g10, g4 = comps
    a0, a1 = real[0] + real[1], real[0] - real[1]
    t = [a0 + g4[0], a1 - g4[1], a0 - g4[0], a1 + g4[1]]
    z0 = cadd(g2, g10)
    cos, sin = phase(2)
    z1 = cmul(csub(g2, g10), cos, -sin)
    e = [z0[0], z1[0], -z0[1], -z1[1]]
    s = [t[a] + e[a] for a in range(4)] + [t[a] - e[a] for a in range(4)]
    p19, m19 = cadd(g1, g9), csub(g1, g9)
    p513, m513 = cadd(g5, g13), csub(g5, g13)
    u = [cadd(p19, p513), None, csub(p19, p513), None]
    u[1] = (m19[0] - m513[1], m19[1] + m513[0])
    u[3] = (m19[0] + m513[1], m19[1] - m513[0])
    d = [None] * 8
    for a in range(4):
        cos, sin = phase(a)
        z = u[a] if a == 0 else cmul(u[a], cos, -sin)
        d[a], d[a + 4] = z[0], -z[1]
    return [s[a] + d[a] for a in range(8)] + [s[a] - d[a] for a in range(8)]


YB = 16


def forward_x_kernel(
    src, solid, spread, twiddle, fh, fl, eh, el, out0, out1, out2, out3, hi, lo, hi0, lo0
):
    lev = lax.axis_index("lev")
    levels = src.shape[1]
    rows = levels * YB
    band = pl.ds(pl.multiple_of(pl.program_id(0) * rows, rows), rows)
    open_cells = (1 - solid[...]).astype(F32).astype(BF16)
    twice = [open_cells[i] for i in range(YB // BY) for _ in range(2)]
    masks = mm(jnp.concatenate(twice, 0), spread[...])
    for part in range(levels):
        near = slice(4 * part, 4 * part + 4)
        mask_at = 8 * (part // 2)
        cells = []
        for a in range(16):
            cols = slice(a * LANES, (a + 1) * LANES)
            piece = src[near, :, cols].reshape(2, 8, LANES)
            cells.append((piece * masks[None, mask_at : mask_at + 8, cols]).reshape(16, LANES))
        real, comps = real16(cells)
        for half in range(2):
            high, low = halves(real[half])
            hi0[part * 16 : part * 16 + 16, half * LANES : (half + 1) * LANES] = high
            lo0[part * 16 : part * 16 + 16, half * LANES : (half + 1) * LANES] = low
        for i in range(1, 8):
            block = cmul(comps[i - 1], twiddle[i - 1 : i, :], twiddle[7 + i : 8 + i, :])
            slot = 2 * ((lev - i // 2) & 3) + i % 2
            place = pl.multiple_of(slot * rows + part * 16, 16)
            for half in range(2):
                high, low = halves(block[half])
                hi[pl.ds(place, 16), half * LANES : (half + 1) * LANES] = high
                lo[pl.ds(place, 16), half * LANES : (half + 1) * LANES] = low
    outs = (out0, out1, out2, out3)
    rest = mm3((hi[...], lo[...]), (fh[...], fl[...]))
    for step in range(4):
        for h in range(2):
            value = rest[(2 * step + h) * rows : (2 * step + h + 1) * rows]
            outs[step][band, h * 256 : h * 256 + 256] = value
    first = mm3((hi0[...], lo0[...]), (eh[...], el[...]))
    for step in range(4):

        @pl.when(lev == step)
        def _(step=step):
            outs[step][band, 0:256] = first


def forward_x(source, solid, consts, half):
    rows, levels, cells = source.shape
    steps = rows // YB // 2
    first = half * steps
    return pl.pallas_call(
        forward_x_kernel,
        grid=(steps,),
        in_specs=[
            pl.BlockSpec((YB, levels, cells), lambda i: (i + first, 0, 0)),
            pl.BlockSpec((YB // BY, levels, cells // BX), lambda i: (i + first, 0, 0)),
        ]
        + [pl.BlockSpec(value.shape, lambda i: (0, 0)) for value in consts],
        out_specs=[VMEM] * 4,
        out_shape=[jax.ShapeDtypeStruct((rows * levels // 2, 512), F32)] * 4,
        scratch_shapes=[pltpu.VMEM((8 * levels * YB, 256), BF16)] * 2
        + [pltpu.VMEM((levels * YB, 256), BF16)] * 2,
        compiler_params=grant(12),
        name=f"forward_x_{half}",
    )(*[pltpu.with_memory_space_constraint(value, pltpu.HBM) for value in (source, solid, *consts)])


def rsqrt(value):
    root = lax.rsqrt(value)
    return root * (1.5 - 0.5 * value * root * root)


def eigen_kernel(coup, lam, modes, w2h, w2l, w4h, w4l):
    sub = lax.broadcasted_iota(jnp.int32, (8, LANES), 0)
    lane = lax.broadcasted_iota(jnp.int32, (8, LANES), 1) & (NZ - 1)
    low = lane < 8
    g = [jnp.zeros((8, LANES), F32), jnp.zeros((8, LANES), F32)]
    link = jnp.zeros((8, LANES), F32)
    for k in range(NZ):
        pivot = coup[k] + coup[k + 1] - link * link
        inverse = rsqrt(pivot)
        here = lane == (k // 2 + 8 * (k % 2))
        g[k // 8] = jnp.where(here & (sub == k % 8), pivot * inverse, g[k // 8])
        link = -coup[k + 1] * inverse
        if k < NZ - 1:
            below = (k + 1) // 8
            g[below] = jnp.where(here & (sub == (k + 1) % 8), link, g[below])
    partners = [pltpu.roll(value, 8, 1) for value in g]

    def total(first, second):
        value = first + second
        for shift in (4, 2, 1):
            value = value + pltpu.roll(value, shift, 0)
        return value

    def right(value):
        return pltpu.roll(value, 1, 1)

    def left(value):
        return pltpu.roll(value, LANES - 1, 1)

    def step(_, carry):
        g0, g1, p0, p1, worst = carry
        own = total(g0 * g0, g1 * g1)
        other = total(p0 * p0, p1 * p1)
        a = total(g0 * p0, g1 * p1)
        d = other - own
        w = d * d + 4.0 * a * a
        h = rsqrt(w)
        x = 0.5 + 0.5 * jnp.abs(d) * h
        y = rsqrt(x)
        positive = (d > 0.0) | ((d == 0.0) & low)
        turn = a * h * y
        still = w == 0.0
        c = jnp.where(still, 1.0, x * y)
        turn = jnp.where(still, 0.0, jnp.where(positive, turn, -turn))
        worst = jnp.maximum(worst, jnp.where(still, 0.0, a * a / (own * other)))
        out = []
        for value, partner in ((g0, p0), (g1, p1)):
            mine = c * value - turn * partner
            theirs = c * partner + turn * value
            rising = right(jnp.where(lane == 0, theirs, mine))
            new = jnp.where(low, rising, jnp.where(lane == 15, theirs, left(mine)))
            new = jnp.where(lane == 0, mine, new)
            falling = right(jnp.where(lane == 8, mine, theirs))
            new_partner = jnp.where(low, jnp.where(lane == 7, mine, left(theirs)), falling)
            new_partner = jnp.where(lane == 8, theirs, new_partner)
            out.append((new, new_partner))
        return out[0][0], out[1][0], out[0][1], out[1][1], worst

    def sweep(carry):
        count, _, *state = carry
        state = lax.fori_loop(0, 15, step, (*state, jnp.zeros((8, LANES), F32)))
        return (count + 1, jnp.max(state[4]), *state[:4])

    def unfinished(carry):
        return (carry[0] < SWEEPS) & (carry[1] > 1e-7)

    state = (jnp.int32(0), jnp.float32(1.0), g[0], g[1], partners[0], partners[1])
    _, _, g0, g1, _, _ = lax.while_loop(unfinished, sweep, state)
    square = total(g0 * g0, g1 * g1)
    inverse = rsqrt(square)
    vectors = jnp.concatenate([g0 * inverse, g1 * inverse], 0)
    lam[...] = jnp.concatenate([square] * NZ, 0).T[:NZ]
    modes[...] = jnp.concatenate([vectors] * 8, 0).T[:NZ]
    row = lax.broadcasted_iota(jnp.int32, (LANES, LANES), 0)
    col = lax.broadcasted_iota(jnp.int32, (LANES, LANES), 1)
    for section in range(4):
        group = []
        for s in range(4):
            at = (4 * section + 4 * s) % NZ
            group += [vectors[at : at + 4]] * 8
        w4 = jnp.where(row % 32 // 4 == col // NZ, jnp.concatenate(group, 0), 0.0)
        w4h[section], w4l[section] = halves(w4)
        w2h[section], w2l[section] = halves(w4.T)


def eigen(couplings):
    table = jax.ShapeDtypeStruct((NZ, LANES), F32)
    matrix = jax.ShapeDtypeStruct((4, LANES, LANES), BF16)
    return pl.pallas_call(
        eigen_kernel,
        in_specs=[pl.BlockSpec(memory_space=pltpu.SMEM)],
        out_specs=[VMEM] * 6,
        out_shape=[table, table, matrix, matrix, matrix, matrix],
        compiler_params=grant(4),
        name="level_modes",
    )(couplings)


def decay(lam, e):
    half = 0.5 * (lam + e)
    root = jnp.sqrt(half * (2.0 + half))
    return 1.0 / (1.0 + half + root), 0.5 / root


def powers(base, count):
    square = base * base
    value = jnp.where((count & 1) != 0, base, 1.0)
    value = value * jnp.where((count & 2) != 0, square, 1.0)
    return value * jnp.where((count & 4) != 0, square * square, 1.0)


def inverse_x_kernel(
    spec0, spec1, spec2, spec3, ends, modes, lam, eig, twiddle, fh, fl, eh, el,
    out, hi, lo, even, odds, eighth, steps, shelf, turn, ready, sems,
):
    levels = out.shape[1]
    rows = levels * YB
    lev = lax.axis_index("lev")
    i = pl.program_id(0)
    last = pl.num_programs(0) - 1
    mirror = 2 * last + 1 - i
    side = i & 1

    def leave(step, o):
        octet = step if o == 0 else 2 * last + 1 - step
        return pltpu.make_async_copy(
            ready.at[step & 1, o], out.at[pl.ds(octet * 8, 8)], sems.at[step & 1, o]
        )

    @pl.when(i >= 2)
    def _():
        for o in range(2):
            leave(i - 2, o).wait()

    @pl.when(i == 0)
    def _():
        b = lax.broadcasted_iota(jnp.int32, (8, LANES), 0)
        odd, half, upper = [(b & bit) != 0 for bit in (1, 2, 4)]

        def choose(mask, factor):
            return jnp.where(mask, factor, 1.0)

        for t in range(16):
            l, h, p = t // 4, (t // 2) % 2, t % 2
            e = eig[t // 2 : t // 2 + 1, p * LANES : (p + 1) * LANES]
            r, gain = decay(lam[:, 0:1], e)
            r2 = r * r
            r4 = r2 * r2
            eighth[t] = r4 * r4
            for n, value in enumerate((r, r2, r4, gain * r)):
                shelf[t, n, :NZ] = value
            for k in range(NZ):
                row = pl.ds(k, 8, stride=0)
                r1, r2, r4, scale = [shelf[t, n, row, :] for n in range(4)]
                up = scale * ends[h, k, l, p : p + 1, :]
                down = scale * ends[h, k, l, 2 + p : 3 + p, :]
                up = jnp.where(odd, r1 * up, up) * (choose(half, r2) * choose(upper, r4))
                down = jnp.where(odd, down, r1 * down) * (choose(~half, r2) * choose(~upper, r4))
                even[t, k] = up + down
                odds[t, k] = up - down

    r8 = eighth[...]
    near_step, far_step = powers(r8, i), powers(r8, mirror)
    steps[0] = 0.5 * (near_step + far_step)
    steps[1] = 0.5 * (near_step - far_step)
    first_level = lev * levels
    for step, spec in enumerate((spec0, spec1, spec2, spec3)):
        l = (lev - step) & 3
        for group in range(4 // TILES):
            parts = range(group * TILES, (group + 1) * TILES)
            acc = {}
            for k in range(NZ):
                scale = [modes[k, first_level + z] for z in range(levels)]
                for part in parts:
                    t = 4 * l + part
                    for o, table in enumerate((even, odds)):
                        value = table[t, k] * steps[o, t, k : k + 1, :]
                        for z in range(levels):
                            term = value * scale[z]
                            acc[part, z, o] = term if k == 0 else acc[part, z, o] + term
            for part in parts:
                place = turn.at[4 * step + part]
                for z in range(levels):
                    place[pl.ds(z, 8, stride=4), :] = acc[part, z, 0] + acc[part, z, 1]
                    place[pl.ds(32 + z, 8, stride=4), :] = acc[part, z, 0] - acc[part, z, 1]
        for part in range(4):
            for q in range(rows // 16):
                octet = i if q < 2 else mirror
                near = pl.ds(pl.multiple_of(32 * octet + 16 * (q % 2), 16), 16)
                value = spec[near, part * LANES : (part + 1) * LANES]
                value = value + turn[4 * step + part, 16 * q : 16 * q + 16, :]
                high, low = halves(value)
                place = pl.multiple_of((2 * l + part // 2) * rows + 16 * q, 16)
                half = pl.ds((part % 2) * LANES, LANES)
                hi[pl.ds(place, 16), half] = high
                lo[pl.ds(place, 16), half] = low
    first = mm3((hi[:rows, :], lo[:rows, :]), (eh[...], el[...]))
    rest = mm3((hi[rows:, :], lo[rows:, :]), (fh[...], fl[...]))
    for q in range(rows // 16):
        at = slice(16 * q, 16 * q + 16)
        real = (first[at, :LANES], first[at, LANES:])
        comps = []
        for n in range(7):
            at = slice(n * rows + 16 * q, n * rows + 16 * q + 16)
            value = (rest[at, :LANES], rest[at, LANES:])
            comps.append(cmul(value, twiddle[n : n + 1, :], -twiddle[8 + n : 9 + n, :]))
        cells = real16_back(real, comps)
        here = slice(4 * (q % 2), 4 * (q % 2) + 4)
        for a in range(16):
            cols = slice(a * LANES, (a + 1) * LANES)
            ready[side, q // 2, here, :, cols] = cells[a].reshape(4, levels, LANES)
    for o in range(2):
        leave(i, o).start()

    @pl.when(i == last)
    def _():
        for step in (i - 1, i):
            for o in range(2):
                leave(step, o).wait()


def inverse_x(specs, ends, modes, lam, eig, consts):
    levels = 4
    rows = specs[0].shape[0] // levels
    return pl.pallas_call(
        inverse_x_kernel,
        grid=(rows // YB,),
        in_specs=[VMEM] * 5 + [pl.BlockSpec(memory_space=pltpu.SMEM)] + [VMEM] * 7,
        out_specs=pl.BlockSpec(memory_space=pl.ANY),
        out_shape=jax.ShapeDtypeStruct((rows, levels, N), F32),
        scratch_shapes=[pltpu.VMEM((8 * levels * YB, 256), BF16)] * 2
        + [pltpu.VMEM((16, NZ, 8, LANES), F32)] * 2
        + [pltpu.VMEM((16, NZ, LANES), F32), pltpu.VMEM((2, 16, NZ, LANES), F32)]
        + [pltpu.VMEM((16, 4, NZ + 8, LANES), F32), pltpu.VMEM((16, 4 * YB, LANES), F32)]
        + [pltpu.VMEM((2, 2, 8, levels, N), F32), pltpu.SemaphoreType.DMA((2, 2))],
        compiler_params=grant(16),
        name="inverse_x",
    )(*specs, ends, modes, lam, eig, *consts)


def level_kernel(
    x0, x1, x2, x3, x4, x5, x6, x7, w2h, w2l, w4h, w4l, lam, eig,
    out0, out1, out2, out3, ends, f, work,
):
    lev = lax.axis_index("lev")
    octets = x0.shape[0] // 32
    rows = 16 * octets
    sources = ((x0, x1, x2, x3), (x4, x5, x6, x7))
    w2 = (w2h[lev], w2l[lev])
    w4 = (w4h[lev], w4l[lev])
    for h in range(x0.shape[1] // 256):
        cols = pl.ds(h * 256, 256)
        e = eig[pl.ds(lev * 2 + h, 1), :]
        r, gain = decay(lam[:, 0:1], e)
        for o in range(rows // 8):
            start = 32 * (o % octets)
            block = [x[start : start + 32, cols] for x in sources[o // octets]]
            value = mm3(w2, halves(jnp.concatenate(block, 0)))
            f[8 * o : 8 * o + 8] = value.reshape(8, NZ, 256)
        up = jnp.zeros((NZ, 256), F32)
        down = jnp.zeros((NZ, 256), F32)
        for y in range(rows):
            up = r * up
            work[y] = up
            up = up + f[y]
        for y in reversed(range(rows)):
            down = f[y] + r * down
            work[y] = (work[y] + down) * gain
        place = pl.ds(h * NZ, NZ)
        ends[place, 0, :] = up[:, :LANES]
        ends[place, 1, :] = up[:, LANES:]
        ends[place, 2, :] = down[:, :LANES]
        ends[place, 3, :] = down[:, LANES:]
        for o in range(rows // 8):
            block = work[8 * o : 8 * o + 8].reshape(LANES, 256)
            value = mm3(w4, halves(block))
            for step, out in enumerate((out0, out1, out2, out3)):
                out[32 * o : 32 * o + 32, cols] = value[32 * step : 32 * step + 32]


def level_solve(xs, weights, lam, eig):
    pairs, width = xs[0].shape
    rows = pairs // 2
    return pl.pallas_call(
        level_kernel,
        in_specs=[VMEM] * 14,
        out_specs=[VMEM] * 5,
        out_shape=[jax.ShapeDtypeStruct((4 * rows, width), F32)] * 4
        + [jax.ShapeDtypeStruct((2 * NZ, 4, LANES), F32)],
        scratch_shapes=[pltpu.VMEM((rows, NZ, 256), F32)] * 2,
        compiler_params=grant(12),
        name="level_solve",
    )(*xs, *weights, lam, eig)


def carry_kernel(ends, lam, eig, out):
    sections = ends.shape[0]
    j = lax.axis_index("rows")
    k = lax.rem(j, NZ)
    h = lax.div(j, NZ)
    e = eig[pl.ds(lax.axis_index("lev") * 2 + h, 1), :]
    r, _ = decay(lam[pl.ds(k, 1), 0:1], e)
    for _ in range(6):
        r = r * r
    row = lax.broadcasted_iota(jnp.int32, (4, LANES), 0)
    ratio = jnp.where(lax.rem(row, 2) == 0, r[:, :LANES], r[:, LANES:])
    whole = ratio
    for _ in range(5):
        whole = whole * whole
    scale = 1.0 / (1.0 - whole)
    up = jnp.zeros((4, LANES), F32)
    down = jnp.zeros((4, LANES), F32)
    for s in range(sections):
        up = ends[s] + ratio * up
        down = ends[sections - 1 - s] + ratio * down
    up = up * scale
    down = down * scale
    first = row < 2
    ups = []
    for s in range(sections):
        ups.append(up)
        up = ends[s] + ratio * up
    for s in reversed(range(sections)):
        value = jnp.where(first, ups[s], down)
        for section in range(4):
            out[s, section] = value
        down = ends[s] + ratio * down


def carries(ends, lam, eig):
    return pl.pallas_call(
        carry_kernel,
        in_specs=[VMEM] * 3,
        out_specs=VMEM,
        out_shape=jax.ShapeDtypeStruct((ends.shape[0], 4) + ends.shape[1:], F32),
        compiler_params=grant(4),
        name="section_carries",
    )(ends, lam, eig)


def shift(value, step):
    return lax.ppermute(value, "lev", [(i, (i + step) % 4) for i in range(4)])


def body(source, solid, couplings):
    full, edge, twiddle, eig, spread = host_tables()
    fh, fl = split_host(full)
    eh, el = split_host(edge)
    fth, ftl = split_host(full.T)
    eth, etl = split_host(edge.T)
    lam, modes, w2h, w2l, w4h, w4l = eigen(couplings)
    xs = []
    for half in range(2):
        parts = forward_x(source, solid, (spread, twiddle, fh, fl, eh, el), half)
        xs += [parts[0]] + [shift(parts[step], -step) for step in (1, 2, 3)]
    *parts, ends = level_solve(xs, (w2h, w2l, w4h, w4l), lam, eig)
    specs = [parts[0]] + [shift(parts[step], step) for step in (1, 2, 3)]
    ends = lax.all_to_all(ends, "rows", 0, 0, tiled=True)
    ends = carries(ends, lam, eig).reshape(128, 4, LANES)
    ends = lax.all_to_all(ends, ("rows", "lev"), 0, 0, tiled=True).reshape(2, NZ, 4, 4, LANES)
    return inverse_x(specs, ends, modes, lam, eig, (twiddle, fth, ftl, eth, etl))


def solution(mesh):
    return jax.shard_map(
        body,
        mesh=mesh,
        in_specs=(P("rows", "lev", None), P("rows", "lev", None), P()),
        out_specs=P("rows", "lev", None),
        check_vma=False,
    )
```

```python
import math

import jax
import jax.numpy as jnp
import ml_dtypes
import numpy as np
from jax import lax
from jax.experimental import pallas as pl
from jax.experimental.pallas import tpu as pltpu
from jax.sharding import PartitionSpec as P

F32 = jnp.float32
BF16 = jnp.bfloat16
BY = 8
BX = 64
N = 2048
LANES = 128
NZ = 16
TURN = 2.0 * math.pi
RESIDUES = (1, 5, 9, 13, 2, 10, 4)
SWEEPS = 12
TILES = 4


VMEM = pl.BlockSpec(memory_space=pltpu.VMEM)


def grant(mebibytes):
    return pltpu.CompilerParams(vmem_limit_bytes=mebibytes << 20)


def split_host(table):
    table = np.asarray(table, np.float32)
    high = table.astype(ml_dtypes.bfloat16)
    low = (table - high.astype(np.float32)).astype(ml_dtypes.bfloat16)
    return high, low


def host_tables():
    b = np.arange(LANES)
    m = np.arange(LANES)
    angle = TURN * np.mod(np.outer(b, m), LANES) / LANES
    scale = math.sqrt(2.0 / N)
    cos, sin = scale * np.cos(angle), scale * np.sin(angle)
    full = np.block([[cos, -sin], [sin, cos]])
    edge = np.zeros((2 * LANES, 2 * LANES))
    freq0 = np.concatenate([np.arange(65), np.arange(1, 64)])
    angle0 = TURN * np.mod(np.outer(b, freq0), LANES) / LANES
    part = np.where(np.arange(LANES)[None, :] < 65, np.cos(angle0), -np.sin(angle0)) * scale
    part[:, 0] *= math.sqrt(0.5)
    part[:, 64] *= math.sqrt(0.5)
    edge[:LANES, :LANES] = part
    freq8 = 16 * np.arange(64) + 8
    angle8 = TURN * np.mod(np.outer(b, freq8), N) / N
    edge[LANES:, LANES:] = scale * np.concatenate([np.cos(angle8), -np.sin(angle8)], 1)
    q = np.array(RESIDUES)
    twist = TURN * np.outer(q, b) / N
    twiddle = np.zeros((16, LANES), np.float32)
    twiddle[:7] = np.cos(twist)
    twiddle[8:15] = np.sin(twist)
    freqs = [np.concatenate([16 * freq0, freq8, freq8])]
    for residue in RESIDUES:
        freqs.append(np.tile(16 * m + residue, 2))
    freqs = np.concatenate(freqs)
    eigen = (4.0 * np.sin(np.pi * freqs / N) ** 2).astype(np.float32).reshape(8, 256)
    spread = (np.arange(32)[:, None] == np.arange(N)[None, :] // BX).astype(ml_dtypes.bfloat16)
    return full, edge, twiddle, eigen, spread


def halves(value):
    high = value.astype(BF16)
    return high, (value - high.astype(F32)).astype(BF16)


def mm(left, right):
    return jnp.dot(left, right, preferred_element_type=F32)


def mm3(left, right):
    return mm(left[0], right[0]) + (mm(left[1], right[0]) + mm(left[0], right[1]))


def cmul(value, cos, sin):
    re, im = value
    return re * cos + im * sin, im * cos - re * sin


def cadd(left, right):
    return left[0] + right[0], left[1] + right[1]


def csub(left, right):
    return left[0] - right[0], left[1] - right[1]


def phase(steps):
    return math.cos(TURN * steps / 16), math.sin(TURN * steps / 16)


def real16(v):
    s = [v[a] + v[a + 8] for a in range(8)]
    d = [v[a] - v[a + 8] for a in range(8)]
    u = [(d[0], -d[4])]
    for a in range(1, 4):
        u.append(cmul((d[a], -d[a + 4]), *phase(a)))
    p02, m02 = cadd(u[0], u[2]), csub(u[0], u[2])
    p13, m13 = cadd(u[1], u[3]), csub(u[1], u[3])
    y1, y9 = cadd(p02, p13), csub(p02, p13)
    y5 = (m02[0] + m13[1], m02[1] - m13[0])
    y13 = (m02[0] - m13[1], m02[1] + m13[0])
    t = [s[a] + s[a + 4] for a in range(4)]
    e = [s[a] - s[a + 4] for a in range(4)]
    z1 = cmul((e[1], -e[3]), *phase(2))
    z0 = (e[0], -e[2])
    y2, y10 = cadd(z0, z1), csub(z0, z1)
    a0, a1 = t[0] + t[2], t[1] + t[3]
    y4 = (t[0] - t[2], t[3] - t[1])
    return (a0 + a1, a0 - a1), (y1, y5, y9, y13, y2, y10, y4)


def real16_back(real, comps):
    g1, g5, g9, g13, g2, g10, g4 = comps
    a0, a1 = real[0] + real[1], real[0] - real[1]
    t = [a0 + g4[0], a1 - g4[1], a0 - g4[0], a1 + g4[1]]
    z0 = cadd(g2, g10)
    cos, sin = phase(2)
    z1 = cmul(csub(g2, g10), cos, -sin)
    e = [z0[0], z1[0], -z0[1], -z1[1]]
    s = [t[a] + e[a] for a in range(4)] + [t[a] - e[a] for a in range(4)]
    p19, m19 = cadd(g1, g9), csub(g1, g9)
    p513, m513 = cadd(g5, g13), csub(g5, g13)
    u = [cadd(p19, p513), None, csub(p19, p513), None]
    u[1] = (m19[0] - m513[1], m19[1] + m513[0])
    u[3] = (m19[0] + m513[1], m19[1] - m513[0])
    d = [None] * 8
    for a in range(4):
        cos, sin = phase(a)
        z = u[a] if a == 0 else cmul(u[a], cos, -sin)
        d[a], d[a + 4] = z[0], -z[1]
    return [s[a] + d[a] for a in range(8)] + [s[a] - d[a] for a in range(8)]


YB = 16


def forward_x_kernel(
    src, solid, spread, twiddle, fh, fl, eh, el, out0, out1, out2, out3, *scratch
):
    hi, lo, hi0, lo0 = [scratch[2 * n : 2 * n + 2] for n in range(4)]
    outs = (out0, out1, out2, out3)
    firsts = []
    lev = lax.axis_index("lev")
    levels = src.shape[1]
    rows = levels * YB
    open_cells = (1 - solid[...]).astype(F32).astype(BF16)
    twice = [open_cells[i] for i in range(YB // BY) for _ in range(2)]
    masks = mm(jnp.concatenate(twice, 0), spread[...])
    for part in range(levels):
        near = slice(4 * part, 4 * part + 4)
        mask_at = 8 * (part // 2)
        cells = []
        for a in range(16):
            cols = slice(a * LANES, (a + 1) * LANES)
            piece = src[near, :, cols].reshape(2, 8, LANES)
            cells.append((piece * masks[None, mask_at : mask_at + 8, cols]).reshape(16, LANES))
        real, comps = real16(cells)
        group, at = part // 2, 16 * (part % 2)
        for half in range(2):
            cols = slice(half * LANES, (half + 1) * LANES)
            hi0[group][at : at + 16, cols], lo0[group][at : at + 16, cols] = halves(real[half])
        for i in range(1, 8):
            block = cmul(comps[i - 1], twiddle[i - 1 : i, :], twiddle[7 + i : 8 + i, :])
            slot = 2 * ((lev - i // 2) & 3) + i % 2
            place = pl.ds(pl.multiple_of(slot * 32 + at, 16), 16)
            for half in range(2):
                cols = slice(half * LANES, (half + 1) * LANES)
                hi[group][place, cols], lo[group][place, cols] = halves(block[half])
        if part % 2 == 0:
            continue
        band = pl.ds(pl.multiple_of(pl.program_id(0) * rows + 32 * group, 32), 32)
        rest = mm3((hi[group][...], lo[group][...]), (fh[...], fl[...]))
        for slot in range(8):
            cols = slice(slot % 2 * 256, slot % 2 * 256 + 256)
            outs[slot // 2][band, cols] = rest[slot * 32 : slot * 32 + 32]
        firsts.append((band, mm3((hi0[group][...], lo0[group][...]), (eh[...], el[...]))))
    for step in range(4):

        @pl.when(lev == step)
        def _(step=step):
            for band, first in firsts:
                outs[step][band, 0:256] = first


def forward_x(source, solid, consts, half):
    rows, levels, cells = source.shape
    steps = rows // YB // 2
    first = half * steps
    return pl.pallas_call(
        forward_x_kernel,
        grid=(steps,),
        in_specs=[
            pl.BlockSpec((YB, levels, cells), lambda i: (i + first, 0, 0)),
            pl.BlockSpec((YB // BY, levels, cells // BX), lambda i: (i + first, 0, 0)),
        ]
        + [pl.BlockSpec(value.shape, lambda i: (0, 0)) for value in consts],
        out_specs=[VMEM] * 4,
        out_shape=[jax.ShapeDtypeStruct((rows * levels // 2, 512), F32)] * 4,
        scratch_shapes=[pltpu.VMEM((4 * levels * YB, 256), BF16)] * 4
        + [pltpu.VMEM((levels * YB // 2, 256), BF16)] * 4,
        compiler_params=grant(12),
        name=f"forward_x_{half}",
    )(*[pltpu.with_memory_space_constraint(value, pltpu.HBM) for value in (source, solid, *consts)])


def rsqrt(value):
    root = lax.rsqrt(value)
    return root * (1.5 - 0.5 * value * root * root)


def eigen_kernel(coup, lam, modes, w2h, w2l, w4h, w4l):
    sub = lax.broadcasted_iota(jnp.int32, (8, LANES), 0)
    lane = lax.broadcasted_iota(jnp.int32, (8, LANES), 1) & (NZ - 1)
    low = lane < 8
    g = [jnp.zeros((8, LANES), F32), jnp.zeros((8, LANES), F32)]
    link = jnp.zeros((8, LANES), F32)
    for k in range(NZ):
        pivot = coup[k] + coup[k + 1] - link * link
        inverse = rsqrt(pivot)
        here = lane == (k // 2 + 8 * (k % 2))
        g[k // 8] = jnp.where(here & (sub == k % 8), pivot * inverse, g[k // 8])
        link = -coup[k + 1] * inverse
        if k < NZ - 1:
            below = (k + 1) // 8
            g[below] = jnp.where(here & (sub == (k + 1) % 8), link, g[below])
    partners = [pltpu.roll(value, 8, 1) for value in g]

    def total(first, second):
        value = first + second
        for shift in (4, 2, 1):
            value = value + pltpu.roll(value, shift, 0)
        return value

    def right(value):
        return pltpu.roll(value, 1, 1)

    def left(value):
        return pltpu.roll(value, LANES - 1, 1)

    def step(_, carry):
        g0, g1, p0, p1, worst = carry
        own = total(g0 * g0, g1 * g1)
        other = total(p0 * p0, p1 * p1)
        a = total(g0 * p0, g1 * p1)
        d = other - own
        w = d * d + 4.0 * a * a
        h = rsqrt(w)
        x = 0.5 + 0.5 * jnp.abs(d) * h
        y = rsqrt(x)
        positive = (d > 0.0) | ((d == 0.0) & low)
        turn = a * h * y
        still = w == 0.0
        c = jnp.where(still, 1.0, x * y)
        turn = jnp.where(still, 0.0, jnp.where(positive, turn, -turn))
        worst = jnp.maximum(worst, jnp.where(still, 0.0, a * a / (own * other)))
        out = []
        for value, partner in ((g0, p0), (g1, p1)):
            mine = c * value - turn * partner
            theirs = c * partner + turn * value
            rising = right(jnp.where(lane == 0, theirs, mine))
            new = jnp.where(low, rising, jnp.where(lane == 15, theirs, left(mine)))
            new = jnp.where(lane == 0, mine, new)
            falling = right(jnp.where(lane == 8, mine, theirs))
            new_partner = jnp.where(low, jnp.where(lane == 7, mine, left(theirs)), falling)
            new_partner = jnp.where(lane == 8, theirs, new_partner)
            out.append((new, new_partner))
        return out[0][0], out[1][0], out[0][1], out[1][1], worst

    def sweep(carry):
        count, _, *state = carry
        state = lax.fori_loop(0, 15, step, (*state, jnp.zeros((8, LANES), F32)))
        return (count + 1, jnp.max(state[4]), *state[:4])

    def unfinished(carry):
        return (carry[0] < SWEEPS) & (carry[1] > 1e-7)

    state = (jnp.int32(0), jnp.float32(1.0), g[0], g[1], partners[0], partners[1])
    _, _, g0, g1, _, _ = lax.while_loop(unfinished, sweep, state)
    square = total(g0 * g0, g1 * g1)
    inverse = rsqrt(square)
    vectors = jnp.concatenate([g0 * inverse, g1 * inverse], 0)
    lam[...] = jnp.concatenate([square] * NZ, 0).T[:NZ]
    modes[...] = jnp.concatenate([vectors] * 8, 0).T[:NZ]
    row = lax.broadcasted_iota(jnp.int32, (LANES, LANES), 0)
    col = lax.broadcasted_iota(jnp.int32, (LANES, LANES), 1)
    for section in range(4):
        group = []
        for s in range(4):
            at = (4 * section + 4 * s) % NZ
            group += [vectors[at : at + 4]] * 8
        w4 = jnp.where(row % 32 // 4 == col // NZ, jnp.concatenate(group, 0), 0.0)
        w4h[section], w4l[section] = halves(w4)
        w2h[section], w2l[section] = halves(w4.T)


def eigen(couplings):
    table = jax.ShapeDtypeStruct((NZ, LANES), F32)
    matrix = jax.ShapeDtypeStruct((4, LANES, LANES), BF16)
    return pl.pallas_call(
        eigen_kernel,
        in_specs=[pl.BlockSpec(memory_space=pltpu.SMEM)],
        out_specs=[VMEM] * 6,
        out_shape=[table, table, matrix, matrix, matrix, matrix],
        compiler_params=grant(4),
        name="level_modes",
    )(couplings)


def decay(lam, e):
    half = 0.5 * (lam + e)
    root = jnp.sqrt(half * (2.0 + half))
    return 1.0 / (1.0 + half + root), 0.5 / root


def powers(base, count):
    square = base * base
    value = jnp.where((count & 1) != 0, base, 1.0)
    value = value * jnp.where((count & 2) != 0, square, 1.0)
    return value * jnp.where((count & 4) != 0, square * square, 1.0)


def inverse_x_kernel(
    spec0, spec1, spec2, spec3, ends, modes, lam, eig, twiddle, fh, fl, eh, el,
    out, hi, lo, even, odds, eighth, steps, shelf, turn, ready, sems,
):
    levels = out.shape[1]
    rows = levels * YB
    lev = lax.axis_index("lev")
    i = pl.program_id(0)
    last = pl.num_programs(0) - 1
    mirror = 2 * last + 1 - i
    side = i & 1

    def leave(step, o):
        octet = step if o == 0 else 2 * last + 1 - step
        return pltpu.make_async_copy(
            ready.at[step & 1, o], out.at[pl.ds(octet * 8, 8)], sems.at[step & 1, o]
        )

    @pl.when(i >= 2)
    def _():
        for o in range(2):
            leave(i - 2, o).wait()

    @pl.when(i == 0)
    def _():
        b = lax.broadcasted_iota(jnp.int32, (8, LANES), 0)
        odd, half, upper = [(b & bit) != 0 for bit in (1, 2, 4)]

        def choose(mask, factor):
            return jnp.where(mask, factor, 1.0)

        for t in range(16):
            l, h, p = t // 4, (t // 2) % 2, t % 2
            e = eig[t // 2 : t // 2 + 1, p * LANES : (p + 1) * LANES]
            r, gain = decay(lam[:, 0:1], e)
            r2 = r * r
            r4 = r2 * r2
            eighth[t] = r4 * r4
            for n, value in enumerate((r, r2, r4, gain * r)):
                shelf[t, n, :NZ] = value
            for k in range(NZ):
                row = pl.ds(k, 8, stride=0)
                r1, r2, r4, scale = [shelf[t, n, row, :] for n in range(4)]
                up = scale * ends[h, k, l, p : p + 1, :]
                down = scale * ends[h, k, l, 2 + p : 3 + p, :]
                up = jnp.where(odd, r1 * up, up) * (choose(half, r2) * choose(upper, r4))
                down = jnp.where(odd, down, r1 * down) * (choose(~half, r2) * choose(~upper, r4))
                even[t, k] = up + down
                odds[t, k] = up - down

    r8 = eighth[...]
    near_step, far_step = powers(r8, i), powers(r8, mirror)
    steps[0] = 0.5 * (near_step + far_step)
    steps[1] = 0.5 * (near_step - far_step)
    first_level = lev * levels
    for step, spec in enumerate((spec0, spec1, spec2, spec3)):
        l = (lev - step) & 3
        for group in range(4 // TILES):
            parts = range(group * TILES, (group + 1) * TILES)
            acc = {}
            for k in range(NZ):
                scale = [modes[k, first_level + z] for z in range(levels)]
                for part in parts:
                    t = 4 * l + part
                    for o, table in enumerate((even, odds)):
                        value = table[t, k] * steps[o, t, k : k + 1, :]
                        for z in range(levels):
                            term = value * scale[z]
                            acc[part, z, o] = term if k == 0 else acc[part, z, o] + term
            for part in parts:
                place = turn.at[4 * step + part]
                for z in range(levels):
                    place[pl.ds(z, 8, stride=4), :] = acc[part, z, 0] + acc[part, z, 1]
                    place[pl.ds(32 + z, 8, stride=4), :] = acc[part, z, 0] - acc[part, z, 1]
        for part in range(4):
            for q in range(rows // 16):
                octet = i if q < 2 else mirror
                near = pl.ds(pl.multiple_of(32 * octet + 16 * (q % 2), 16), 16)
                value = spec[near, part * LANES : (part + 1) * LANES]
                value = value + turn[4 * step + part, 16 * q : 16 * q + 16, :]
                high, low = halves(value)
                place = pl.multiple_of(128 * q + 16 * (2 * l + part // 2), 16)
                half = pl.ds((part % 2) * LANES, LANES)
                hi[pl.ds(place, 16), half] = high
                lo[pl.ds(place, 16), half] = low
    edges = [jnp.concatenate([ref[128 * q : 128 * q + 16] for q in range(rows // 16)], 0) for ref in (hi, lo)]
    first = mm3(edges, (eh[...], el[...]))
    rest = mm3((hi[...], lo[...]), (fh[...], fl[...]))
    for q in range(rows // 16):
        at = slice(16 * q, 16 * q + 16)
        real = (first[at, :LANES], first[at, LANES:])
        comps = []
        for n in range(7):
            at = slice(128 * q + 16 * n + 16, 128 * q + 16 * n + 32)
            value = (rest[at, :LANES], rest[at, LANES:])
            comps.append(cmul(value, twiddle[n : n + 1, :], -twiddle[8 + n : 9 + n, :]))
        cells = real16_back(real, comps)
        here = slice(4 * (q % 2), 4 * (q % 2) + 4)
        for a in range(16):
            cols = slice(a * LANES, (a + 1) * LANES)
            ready[side, q // 2, here, :, cols] = cells[a].reshape(4, levels, LANES)
    for o in range(2):
        leave(i, o).start()

    @pl.when(i == last)
    def _():
        for step in (i - 1, i):
            for o in range(2):
                leave(step, o).wait()


def inverse_x(specs, ends, modes, lam, eig, consts):
    levels = 4
    rows = specs[0].shape[0] // levels
    return pl.pallas_call(
        inverse_x_kernel,
        grid=(rows // YB,),
        in_specs=[VMEM] * 5 + [pl.BlockSpec(memory_space=pltpu.SMEM)] + [VMEM] * 7,
        out_specs=pl.BlockSpec(memory_space=pl.ANY),
        out_shape=jax.ShapeDtypeStruct((rows, levels, N), F32),
        scratch_shapes=[pltpu.VMEM((8 * levels * YB, 256), BF16)] * 2
        + [pltpu.VMEM((16, NZ, 8, LANES), F32)] * 2
        + [pltpu.VMEM((16, NZ, LANES), F32), pltpu.VMEM((2, 16, NZ, LANES), F32)]
        + [pltpu.VMEM((16, 4, NZ + 8, LANES), F32), pltpu.VMEM((16, 4 * YB, LANES), F32)]
        + [pltpu.VMEM((2, 2, 8, levels, N), F32), pltpu.SemaphoreType.DMA((2, 2))],
        compiler_params=grant(16),
        name="inverse_x",
    )(*specs, ends, modes, lam, eig, *consts)


def modes_kernel(x0, x1, x2, x3, wh, wl, f):
    lev = lax.axis_index("lev")
    w = (wh[lev], wl[lev])
    for h in range(f.shape[0]):
        cols = pl.ds(h * 256, 256)
        for o in range(x0.shape[0] // 32):
            block = [x[32 * o : 32 * o + 32, cols] for x in (x0, x1, x2, x3)]
            value = mm3(w, halves(jnp.concatenate(block, 0)))
            f[h, 8 * o : 8 * o + 8] = value.reshape(8, NZ, 256)


def level_modes_of(xs, wh, wl):
    pairs, width = xs[0].shape
    return pl.pallas_call(
        modes_kernel,
        in_specs=[VMEM] * 6,
        out_specs=VMEM,
        out_shape=jax.ShapeDtypeStruct((width // 256, pairs // 4, NZ, 256), F32),
        compiler_params=grant(8),
        name="mode_values",
    )(*xs, wh, wl)


def level_kernel(
    x0, x1, x2, x3, upper, w2h, w2l, w4h, w4l, lam, eig, out0, out1, out2, out3, ends, f, work
):
    lev = lax.axis_index("lev")
    octets = x0.shape[0] // 32
    half = 8 * octets
    rows = 2 * half
    w2 = (w2h[lev], w2l[lev])
    w4 = (w4h[lev], w4l[lev])
    for h in range(x0.shape[1] // 256):
        cols = pl.ds(h * 256, 256)
        e = eig[pl.ds(lev * 2 + h, 1), :]
        r, gain = decay(lam[:, 0:1], e)
        for o in range(octets):
            block = [x[32 * o : 32 * o + 32, cols] for x in (x0, x1, x2, x3)]
            value = mm3(w2, halves(jnp.concatenate(block, 0)))
            f[8 * o : 8 * o + 8] = value.reshape(8, NZ, 256)

        def source(y):
            return f[y] if y < half else upper[h, y - half]

        up = jnp.zeros((NZ, 256), F32)
        down = jnp.zeros((NZ, 256), F32)
        for y in range(rows):
            up = r * up
            work[y] = up
            up = up + source(y)
        for y in reversed(range(rows)):
            down = source(y) + r * down
            work[y] = (work[y] + down) * gain
        place = pl.ds(h * NZ, NZ)
        ends[place, 0, :] = up[:, :LANES]
        ends[place, 1, :] = up[:, LANES:]
        ends[place, 2, :] = down[:, :LANES]
        ends[place, 3, :] = down[:, LANES:]
        for o in range(rows // 8):
            block = work[8 * o : 8 * o + 8].reshape(LANES, 256)
            value = mm3(w4, halves(block))
            for step, out in enumerate((out0, out1, out2, out3)):
                out[32 * o : 32 * o + 32, cols] = value[32 * step : 32 * step + 32]


def level_solve(xs, upper, weights, lam, eig):
    pairs, width = xs[0].shape
    rows = pairs // 2
    return pl.pallas_call(
        level_kernel,
        in_specs=[VMEM] * 11,
        out_specs=[VMEM] * 5,
        out_shape=[jax.ShapeDtypeStruct((4 * rows, width), F32)] * 4
        + [jax.ShapeDtypeStruct((2 * NZ, 4, LANES), F32)],
        scratch_shapes=[
            pltpu.VMEM((rows // 2, NZ, 256), F32),
            pltpu.VMEM((rows, NZ, 256), F32),
        ],
        compiler_params=grant(12),
        name="level_solve",
    )(*xs, upper, *weights, lam, eig)


def carry_kernel(ends, lam, eig, out):
    sections = ends.shape[0]
    j = lax.axis_index("rows")
    k = lax.rem(j, NZ)
    h = lax.div(j, NZ)
    e = eig[pl.ds(lax.axis_index("lev") * 2 + h, 1), :]
    r, _ = decay(lam[pl.ds(k, 1), 0:1], e)
    for _ in range(6):
        r = r * r
    row = lax.broadcasted_iota(jnp.int32, (4, LANES), 0)
    ratio = jnp.where(lax.rem(row, 2) == 0, r[:, :LANES], r[:, LANES:])
    whole = ratio
    for _ in range(5):
        whole = whole * whole
    scale = 1.0 / (1.0 - whole)
    up = jnp.zeros((4, LANES), F32)
    down = jnp.zeros((4, LANES), F32)
    for s in range(sections):
        up = ends[s] + ratio * up
        down = ends[sections - 1 - s] + ratio * down
    up = up * scale
    down = down * scale
    first = row < 2
    ups = []
    for s in range(sections):
        ups.append(up)
        up = ends[s] + ratio * up
    for s in reversed(range(sections)):
        value = jnp.where(first, ups[s], down)
        for section in range(4):
            out[s, section] = value
        down = ends[s] + ratio * down


def carries(ends, lam, eig):
    return pl.pallas_call(
        carry_kernel,
        in_specs=[VMEM] * 3,
        out_specs=VMEM,
        out_shape=jax.ShapeDtypeStruct((ends.shape[0], 4) + ends.shape[1:], F32),
        compiler_params=grant(4),
        name="section_carries",
    )(ends, lam, eig)


def shift(value, step):
    return lax.ppermute(value, "lev", [(i, (i + step) % 4) for i in range(4)])


def body(source, solid, couplings):
    full, edge, twiddle, eig, spread = host_tables()
    fh, fl = split_host(full)
    eh, el = split_host(edge)
    fth, ftl = split_host(full.T)
    eth, etl = split_host(edge.T)
    lam, modes, w2h, w2l, w4h, w4l = eigen(couplings)
    xs = []
    for half in (1, 0):
        parts = forward_x(source, solid, (spread, twiddle, fh, fl, eh, el), half)
        xs.append([parts[0]] + [shift(parts[step], -step) for step in (1, 2, 3)])
    upper = level_modes_of(xs[0], w2h, w2l)
    *parts, ends = level_solve(xs[1], upper, (w2h, w2l, w4h, w4l), lam, eig)
    specs = [parts[0]] + [shift(parts[step], step) for step in (1, 2, 3)]
    ends = lax.all_to_all(ends, "rows", 0, 0, tiled=True)
    ends = carries(ends, lam, eig).reshape(128, 4, LANES)
    ends = lax.all_to_all(ends, ("rows", "lev"), 0, 0, tiled=True).reshape(2, NZ, 4, 4, LANES)
    return inverse_x(specs, ends, modes, lam, eig, (twiddle, fth, ftl, eth, etl))


def solution(mesh):
    return jax.shard_map(
        body,
        mesh=mesh,
        in_specs=(P("rows", "lev", None), P("rows", "lev", None), P()),
        out_specs=P("rows", "lev", None),
        check_vma=False,
    )
```

```python
import math

import jax
import jax.numpy as jnp
import ml_dtypes
import numpy as np
from jax import lax
from jax.experimental import pallas as pl
from jax.experimental.pallas import tpu as pltpu
from jax.sharding import PartitionSpec as P

F32 = jnp.float32
BF16 = jnp.bfloat16
BY = 8
BX = 64
N = 2048
LANES = 128
NZ = 16
TURN = 2.0 * math.pi
RESIDUES = (1, 5, 9, 13, 2, 10, 4)
SWEEPS = 12
TILES = 4


VMEM = pl.BlockSpec(memory_space=pltpu.VMEM)


def grant(mebibytes):
    return pltpu.CompilerParams(vmem_limit_bytes=mebibytes << 20)


def split_host(table):
    table = np.asarray(table, np.float32)
    high = table.astype(ml_dtypes.bfloat16)
    low = (table - high.astype(np.float32)).astype(ml_dtypes.bfloat16)
    return high, low


def host_tables():
    b = np.arange(LANES)
    m = np.arange(LANES)
    angle = TURN * np.mod(np.outer(b, m), LANES) / LANES
    scale = math.sqrt(2.0 / N)
    cos, sin = scale * np.cos(angle), scale * np.sin(angle)
    full = np.block([[cos, -sin], [sin, cos]])
    edge = np.zeros((2 * LANES, 2 * LANES))
    freq0 = np.concatenate([np.arange(65), np.arange(1, 64)])
    angle0 = TURN * np.mod(np.outer(b, freq0), LANES) / LANES
    part = np.where(np.arange(LANES)[None, :] < 65, np.cos(angle0), -np.sin(angle0)) * scale
    part[:, 0] *= math.sqrt(0.5)
    part[:, 64] *= math.sqrt(0.5)
    edge[:LANES, :LANES] = part
    freq8 = 16 * np.arange(64) + 8
    angle8 = TURN * np.mod(np.outer(b, freq8), N) / N
    edge[LANES:, LANES:] = scale * np.concatenate([np.cos(angle8), -np.sin(angle8)], 1)
    q = np.array(RESIDUES)
    twist = TURN * np.outer(q, b) / N
    twiddle = np.zeros((16, LANES), np.float32)
    twiddle[:7] = np.cos(twist)
    twiddle[8:15] = np.sin(twist)
    freqs = [np.concatenate([16 * freq0, freq8, freq8])]
    for residue in RESIDUES:
        freqs.append(np.tile(16 * m + residue, 2))
    freqs = np.concatenate(freqs)
    eigen = (4.0 * np.sin(np.pi * freqs / N) ** 2).astype(np.float32).reshape(8, 256)
    spread = (np.arange(32)[:, None] == np.arange(N)[None, :] // BX).astype(ml_dtypes.bfloat16)
    return full, edge, twiddle, eigen, spread


def halves(value):
    high = value.astype(BF16)
    return high, (value - high.astype(F32)).astype(BF16)


def mm(left, right):
    return jnp.dot(left, right, preferred_element_type=F32)


def mm3(left, right):
    return mm(left[0], right[0]) + (mm(left[1], right[0]) + mm(left[0], right[1]))


def cmul(value, cos, sin):
    re, im = value
    return re * cos + im * sin, im * cos - re * sin


def cadd(left, right):
    return left[0] + right[0], left[1] + right[1]


def csub(left, right):
    return left[0] - right[0], left[1] - right[1]


def phase(steps):
    return math.cos(TURN * steps / 16), math.sin(TURN * steps / 16)


def real16(v):
    s = [v[a] + v[a + 8] for a in range(8)]
    d = [v[a] - v[a + 8] for a in range(8)]
    u = [(d[0], -d[4])]
    for a in range(1, 4):
        u.append(cmul((d[a], -d[a + 4]), *phase(a)))
    p02, m02 = cadd(u[0], u[2]), csub(u[0], u[2])
    p13, m13 = cadd(u[1], u[3]), csub(u[1], u[3])
    y1, y9 = cadd(p02, p13), csub(p02, p13)
    y5 = (m02[0] + m13[1], m02[1] - m13[0])
    y13 = (m02[0] - m13[1], m02[1] + m13[0])
    t = [s[a] + s[a + 4] for a in range(4)]
    e = [s[a] - s[a + 4] for a in range(4)]
    z1 = cmul((e[1], -e[3]), *phase(2))
    z0 = (e[0], -e[2])
    y2, y10 = cadd(z0, z1), csub(z0, z1)
    a0, a1 = t[0] + t[2], t[1] + t[3]
    y4 = (t[0] - t[2], t[3] - t[1])
    return (a0 + a1, a0 - a1), (y1, y5, y9, y13, y2, y10, y4)


def real16_back(real, comps):
    g1, g5, g9, g13, g2, g10, g4 = comps
    a0, a1 = real[0] + real[1], real[0] - real[1]
    t = [a0 + g4[0], a1 - g4[1], a0 - g4[0], a1 + g4[1]]
    z0 = cadd(g2, g10)
    cos, sin = phase(2)
    z1 = cmul(csub(g2, g10), cos, -sin)
    e = [z0[0], z1[0], -z0[1], -z1[1]]
    s = [t[a] + e[a] for a in range(4)] + [t[a] - e[a] for a in range(4)]
    p19, m19 = cadd(g1, g9), csub(g1, g9)
    p513, m513 = cadd(g5, g13), csub(g5, g13)
    u = [cadd(p19, p513), None, csub(p19, p513), None]
    u[1] = (m19[0] - m513[1], m19[1] + m513[0])
    u[3] = (m19[0] + m513[1], m19[1] - m513[0])
    d = [None] * 8
    for a in range(4):
        cos, sin = phase(a)
        z = u[a] if a == 0 else cmul(u[a], cos, -sin)
        d[a], d[a + 4] = z[0], -z[1]
    return [s[a] + d[a] for a in range(8)] + [s[a] - d[a] for a in range(8)]


YB = 16


def forward_x_kernel(
    src, solid, spread, twiddle, fh, fl, eh, el, out0, out1, out2, out3, *scratch
):
    hi, lo, hi0, lo0 = [scratch[2 * n : 2 * n + 2] for n in range(4)]
    outs = (out0, out1, out2, out3)
    firsts = []
    lev = lax.axis_index("lev")
    levels = src.shape[1]
    rows = levels * YB
    open_cells = (1 - solid[...]).astype(F32).astype(BF16)
    twice = [open_cells[i] for i in range(YB // BY) for _ in range(2)]
    masks = mm(jnp.concatenate(twice, 0), spread[...])
    for part in range(levels):
        near = slice(4 * part, 4 * part + 4)
        mask_at = 8 * (part // 2)
        cells = []
        for a in range(16):
            cols = slice(a * LANES, (a + 1) * LANES)
            piece = src[near, :, cols].reshape(2, 8, LANES)
            cells.append((piece * masks[None, mask_at : mask_at + 8, cols]).reshape(16, LANES))
        real, comps = real16(cells)
        group, at = part // 2, 16 * (part % 2)
        for half in range(2):
            cols = slice(half * LANES, (half + 1) * LANES)
            hi0[group][at : at + 16, cols], lo0[group][at : at + 16, cols] = halves(real[half])
        for i in range(1, 8):
            block = cmul(comps[i - 1], twiddle[i - 1 : i, :], twiddle[7 + i : 8 + i, :])
            slot = 2 * ((lev - i // 2) & 3) + i % 2
            place = pl.ds(pl.multiple_of(slot * 32 + at, 16), 16)
            for half in range(2):
                cols = slice(half * LANES, (half + 1) * LANES)
                hi[group][place, cols], lo[group][place, cols] = halves(block[half])
        if part % 2 == 0:
            continue
        band = pl.ds(pl.multiple_of(pl.program_id(0) * rows + 32 * group, 32), 32)
        rest = mm3((hi[group][...], lo[group][...]), (fh[...], fl[...]))
        for slot in range(8):
            cols = slice(slot % 2 * 256, slot % 2 * 256 + 256)
            outs[slot // 2][band, cols] = rest[slot * 32 : slot * 32 + 32]
        firsts.append((band, mm3((hi0[group][...], lo0[group][...]), (eh[...], el[...]))))
    for step in range(4):

        @pl.when(lev == step)
        def _(step=step):
            for band, first in firsts:
                outs[step][band, 0:256] = first


def forward_x(source, solid, consts, half):
    rows, levels, cells = source.shape
    steps = rows // YB // 2
    first = half * steps
    return pl.pallas_call(
        forward_x_kernel,
        grid=(steps,),
        in_specs=[
            pl.BlockSpec((YB, levels, cells), lambda i: (i + first, 0, 0)),
            pl.BlockSpec((YB // BY, levels, cells // BX), lambda i: (i + first, 0, 0)),
        ]
        + [pl.BlockSpec(value.shape, lambda i: (0, 0)) for value in consts],
        out_specs=[VMEM] * 4,
        out_shape=[jax.ShapeDtypeStruct((rows * levels // 2, 512), F32)] * 4,
        scratch_shapes=[pltpu.VMEM((4 * levels * YB, 256), BF16)] * 4
        + [pltpu.VMEM((levels * YB // 2, 256), BF16)] * 4,
        compiler_params=grant(12),
        name=f"forward_x_{half}",
    )(*[pltpu.with_memory_space_constraint(value, pltpu.HBM) for value in (source, solid, *consts)])


def rsqrt(value):
    root = lax.rsqrt(value)
    return root * (1.5 - 0.5 * value * root * root)


def eigen_kernel(coup, lam, modes, w2h, w2l, w4h, w4l):
    sub = lax.broadcasted_iota(jnp.int32, (8, LANES), 0)
    lane = lax.broadcasted_iota(jnp.int32, (8, LANES), 1) & (NZ - 1)
    low = lane < 8
    g = [jnp.zeros((8, LANES), F32), jnp.zeros((8, LANES), F32)]
    link = jnp.zeros((8, LANES), F32)
    for k in range(NZ):
        pivot = coup[k] + coup[k + 1] - link * link
        inverse = rsqrt(pivot)
        here = lane == (k // 2 + 8 * (k % 2))
        g[k // 8] = jnp.where(here & (sub == k % 8), pivot * inverse, g[k // 8])
        link = -coup[k + 1] * inverse
        if k < NZ - 1:
            below = (k + 1) // 8
            g[below] = jnp.where(here & (sub == (k + 1) % 8), link, g[below])
    partners = [pltpu.roll(value, 8, 1) for value in g]

    def total(first, second):
        value = first + second
        for shift in (4, 2, 1):
            value = value + pltpu.roll(value, shift, 0)
        return value

    def right(value):
        return pltpu.roll(value, 1, 1)

    def left(value):
        return pltpu.roll(value, LANES - 1, 1)

    def step(_, carry):
        g0, g1, p0, p1, worst = carry
        own = total(g0 * g0, g1 * g1)
        other = total(p0 * p0, p1 * p1)
        a = total(g0 * p0, g1 * p1)
        d = other - own
        w = d * d + 4.0 * a * a
        h = rsqrt(w)
        x = 0.5 + 0.5 * jnp.abs(d) * h
        y = rsqrt(x)
        positive = (d > 0.0) | ((d == 0.0) & low)
        turn = a * h * y
        still = w == 0.0
        c = jnp.where(still, 1.0, x * y)
        turn = jnp.where(still, 0.0, jnp.where(positive, turn, -turn))
        worst = jnp.maximum(worst, jnp.where(still, 0.0, a * a / (own * other)))
        out = []
        for value, partner in ((g0, p0), (g1, p1)):
            mine = c * value - turn * partner
            theirs = c * partner + turn * value
            rising = right(jnp.where(lane == 0, theirs, mine))
            new = jnp.where(low, rising, jnp.where(lane == 15, theirs, left(mine)))
            new = jnp.where(lane == 0, mine, new)
            falling = right(jnp.where(lane == 8, mine, theirs))
            new_partner = jnp.where(low, jnp.where(lane == 7, mine, left(theirs)), falling)
            new_partner = jnp.where(lane == 8, theirs, new_partner)
            out.append((new, new_partner))
        return out[0][0], out[1][0], out[0][1], out[1][1], worst

    def sweep(carry):
        count, _, *state = carry
        state = lax.fori_loop(0, 15, step, (*state, jnp.zeros((8, LANES), F32)))
        return (count + 1, jnp.max(state[4]), *state[:4])

    def unfinished(carry):
        return (carry[0] < SWEEPS) & (carry[1] > 1e-7)

    state = (jnp.int32(0), jnp.float32(1.0), g[0], g[1], partners[0], partners[1])
    _, _, g0, g1, _, _ = lax.while_loop(unfinished, sweep, state)
    square = total(g0 * g0, g1 * g1)
    inverse = rsqrt(square)
    vectors = jnp.concatenate([g0 * inverse, g1 * inverse], 0)
    lam[...] = jnp.concatenate([square] * NZ, 0).T[:NZ]
    modes[...] = jnp.concatenate([vectors] * 8, 0).T[:NZ]
    row = lax.broadcasted_iota(jnp.int32, (LANES, LANES), 0)
    col = lax.broadcasted_iota(jnp.int32, (LANES, LANES), 1)
    for section in range(4):
        group = []
        for s in range(4):
            at = (4 * section + 4 * s) % NZ
            group += [vectors[at : at + 4]] * 8
        w4 = jnp.where(row % 32 // 4 == col // NZ, jnp.concatenate(group, 0), 0.0)
        w4h[section], w4l[section] = halves(w4)
        w2h[section], w2l[section] = halves(w4.T)


def eigen(couplings):
    table = jax.ShapeDtypeStruct((NZ, LANES), F32)
    matrix = jax.ShapeDtypeStruct((4, LANES, LANES), BF16)
    return pl.pallas_call(
        eigen_kernel,
        in_specs=[pl.BlockSpec(memory_space=pltpu.SMEM)],
        out_specs=[VMEM] * 6,
        out_shape=[table, table, matrix, matrix, matrix, matrix],
        compiler_params=grant(4),
        name="level_modes",
    )(couplings)


def decay(lam, e):
    half = 0.5 * (lam + e)
    root = jnp.sqrt(half * (2.0 + half))
    return 1.0 / (1.0 + half + root), 0.5 / root


def powers(base, count):
    square = base * base
    value = jnp.where((count & 1) != 0, base, 1.0)
    value = value * jnp.where((count & 2) != 0, square, 1.0)
    return value * jnp.where((count & 4) != 0, square * square, 1.0)


def decay_kernel(lam, eig, rise, fall, shelf):
    b = lax.broadcasted_iota(jnp.int32, (8, LANES), 0)
    odd, half, upper = [(b & bit) != 0 for bit in (1, 2, 4)]

    def choose(mask, factor):
        return jnp.where(mask, factor, 1.0)

    for t in range(16):
        e = eig[t // 2 : t // 2 + 1, (t % 2) * LANES : (t % 2 + 1) * LANES]
        r, gain = decay(lam[:, 0:1], e)
        r2 = r * r
        for n, value in enumerate((r, r2, r2 * r2, gain * r)):
            shelf[t, n, :NZ] = value
        for k in range(NZ):
            row = pl.ds(k, 8, stride=0)
            r1, r2, r4, scale = [shelf[t, n, row, :] for n in range(4)]
            more = scale * r1
            rise[t, k] = jnp.where(odd, more, scale) * (choose(half, r2) * choose(upper, r4))
            fall[t, k] = jnp.where(odd, scale, more) * (choose(~half, r2) * choose(~upper, r4))


def decay_tables(lam, eig):
    return pl.pallas_call(
        decay_kernel,
        in_specs=[VMEM] * 2,
        out_specs=[VMEM] * 2,
        out_shape=[jax.ShapeDtypeStruct((16, NZ, 8, LANES), F32)] * 2,
        scratch_shapes=[pltpu.VMEM((16, 4, NZ + 8, LANES), F32)],
        compiler_params=grant(8),
        name="decay_tables",
    )(lam, eig)


def inverse_x_kernel(
    spec0, spec1, spec2, spec3, ends, modes, lam, eig, rise, fall, twiddle, fh, fl, eh, el,
    out, hi, lo, even, odds, eighth, steps, turn, ready, sems,
):
    levels = out.shape[1]
    rows = levels * YB
    lev = lax.axis_index("lev")
    i = pl.program_id(0)
    last = pl.num_programs(0) - 1
    mirror = 2 * last + 1 - i
    side = i & 1

    def leave(step, o):
        octet = step if o == 0 else 2 * last + 1 - step
        return pltpu.make_async_copy(
            ready.at[step & 1, o], out.at[pl.ds(octet * 8, 8)], sems.at[step & 1, o]
        )

    @pl.when(i >= 2)
    def _():
        for o in range(2):
            leave(i - 2, o).wait()

    @pl.when(i == 0)
    def _():
        for t in range(16):
            l, h, p = t // 4, (t // 2) % 2, t % 2
            e = eig[t // 2 : t // 2 + 1, p * LANES : (p + 1) * LANES]
            r = decay(lam[:, 0:1], e)[0]
            for _ in range(3):
                r = r * r
            eighth[t] = r
            for k in range(NZ):
                up = rise[t, k] * ends[h, k, l, p : p + 1, :]
                down = fall[t, k] * ends[h, k, l, 2 + p : 3 + p, :]
                even[t, k] = up + down
                odds[t, k] = up - down

    r8 = eighth[...]
    near_step, far_step = powers(r8, i), powers(r8, mirror)
    steps[0] = 0.5 * (near_step + far_step)
    steps[1] = 0.5 * (near_step - far_step)
    first_level = lev * levels
    for step, spec in enumerate((spec0, spec1, spec2, spec3)):
        l = (lev - step) & 3
        for group in range(4 // TILES):
            parts = range(group * TILES, (group + 1) * TILES)
            acc = {}
            for k in range(NZ):
                scale = [modes[k, first_level + z] for z in range(levels)]
                for part in parts:
                    t = 4 * l + part
                    for o, table in enumerate((even, odds)):
                        value = table[t, k] * steps[o, t, k : k + 1, :]
                        for z in range(levels):
                            term = value * scale[z]
                            acc[part, z, o] = term if k == 0 else acc[part, z, o] + term
            for part in parts:
                place = turn.at[4 * step + part]
                for z in range(levels):
                    place[pl.ds(z, 8, stride=4), :] = acc[part, z, 0] + acc[part, z, 1]
                    place[pl.ds(32 + z, 8, stride=4), :] = acc[part, z, 0] - acc[part, z, 1]
        for part in range(4):
            for q in range(rows // 16):
                octet = i if q < 2 else mirror
                near = pl.ds(pl.multiple_of(32 * octet + 16 * (q % 2), 16), 16)
                value = spec[near, part * LANES : (part + 1) * LANES]
                value = value + turn[4 * step + part, 16 * q : 16 * q + 16, :]
                high, low = halves(value)
                place = pl.multiple_of((2 * l + part // 2) * rows + 16 * q, 16)
                half = pl.ds((part % 2) * LANES, LANES)
                hi[pl.ds(place, 16), half] = high
                lo[pl.ds(place, 16), half] = low
    first = mm3((hi[:rows, :], lo[:rows, :]), (eh[...], el[...]))
    rest = mm3((hi[rows:, :], lo[rows:, :]), (fh[...], fl[...]))
    for q in range(rows // 16):
        at = slice(16 * q, 16 * q + 16)
        real = (first[at, :LANES], first[at, LANES:])
        comps = []
        for n in range(7):
            at = slice(n * rows + 16 * q, n * rows + 16 * q + 16)
            value = (rest[at, :LANES], rest[at, LANES:])
            comps.append(cmul(value, twiddle[n : n + 1, :], -twiddle[8 + n : 9 + n, :]))
        cells = real16_back(real, comps)
        here = slice(4 * (q % 2), 4 * (q % 2) + 4)
        for a in range(16):
            cols = slice(a * LANES, (a + 1) * LANES)
            ready[side, q // 2, here, :, cols] = cells[a].reshape(4, levels, LANES)
    for o in range(2):
        leave(i, o).start()

    @pl.when(i == last)
    def _():
        for step in (i - 1, i):
            for o in range(2):
                leave(step, o).wait()


def inverse_x(specs, ends, modes, lam, eig, tables, consts):
    levels = 4
    rows = specs[0].shape[0] // levels
    return pl.pallas_call(
        inverse_x_kernel,
        grid=(rows // YB,),
        in_specs=[VMEM] * 5 + [pl.BlockSpec(memory_space=pltpu.SMEM)] + [VMEM] * 9,
        out_specs=pl.BlockSpec(memory_space=pl.ANY),
        out_shape=jax.ShapeDtypeStruct((rows, levels, N), F32),
        scratch_shapes=[pltpu.VMEM((8 * levels * YB, 256), BF16)] * 2
        + [pltpu.VMEM((16, NZ, 8, LANES), F32)] * 2
        + [pltpu.VMEM((16, NZ, LANES), F32), pltpu.VMEM((2, 16, NZ, LANES), F32)]
        + [pltpu.VMEM((16, 4 * YB, LANES), F32)]
        + [pltpu.VMEM((2, 2, 8, levels, N), F32), pltpu.SemaphoreType.DMA((2, 2))],
        compiler_params=grant(16),
        name="inverse_x",
    )(*specs, ends, modes, lam, eig, *tables, *consts)


def modes_kernel(x0, x1, x2, x3, wh, wl, _, f):
    lev = lax.axis_index("lev")
    w = (wh[lev], wl[lev])
    for h in range(f.shape[0]):
        cols = pl.ds(h * 256, 256)
        for o in range(x0.shape[0] // 32):
            block = [x[32 * o : 32 * o + 32, cols] for x in (x0, x1, x2, x3)]
            value = mm3(w, halves(jnp.concatenate(block, 0)))
            f[h, 8 * o : 8 * o + 8] = value.reshape(8, NZ, 256)


def level_modes_of(xs, wh, wl, after):
    pairs, width = xs[0].shape
    return pl.pallas_call(
        modes_kernel,
        in_specs=[VMEM] * 7,
        out_specs=VMEM,
        out_shape=jax.ShapeDtypeStruct((width // 256, pairs // 4, NZ, 256), F32),
        compiler_params=grant(8),
        name="mode_values",
    )(*xs, wh, wl, after)


def level_kernel(
    x0, x1, x2, x3, upper, w2h, w2l, w4h, w4l, lam, eig, out0, out1, out2, out3, ends, f, work
):
    lev = lax.axis_index("lev")
    octets = x0.shape[0] // 32
    half = 8 * octets
    rows = 2 * half
    w2 = (w2h[lev], w2l[lev])
    w4 = (w4h[lev], w4l[lev])
    for h in range(x0.shape[1] // 256):
        cols = pl.ds(h * 256, 256)
        e = eig[pl.ds(lev * 2 + h, 1), :]
        r, gain = decay(lam[:, 0:1], e)
        for o in range(octets):
            block = [x[32 * o : 32 * o + 32, cols] for x in (x0, x1, x2, x3)]
            value = mm3(w2, halves(jnp.concatenate(block, 0)))
            f[8 * o : 8 * o + 8] = value.reshape(8, NZ, 256)

        def source(y):
            return f[y] if y < half else upper[h, y - half]

        up = jnp.zeros((NZ, 256), F32)
        down = jnp.zeros((NZ, 256), F32)
        for y in range(rows):
            up = r * up
            work[y] = up
            up = up + source(y)
        for y in reversed(range(rows)):
            down = source(y) + r * down
            work[y] = (work[y] + down) * gain
        place = pl.ds(h * NZ, NZ)
        ends[place, 0, :] = up[:, :LANES]
        ends[place, 1, :] = up[:, LANES:]
        ends[place, 2, :] = down[:, :LANES]
        ends[place, 3, :] = down[:, LANES:]
        for o in range(rows // 8):
            block = work[8 * o : 8 * o + 8].reshape(LANES, 256)
            value = mm3(w4, halves(block))
            for step, out in enumerate((out0, out1, out2, out3)):
                out[32 * o : 32 * o + 32, cols] = value[32 * step : 32 * step + 32]


def level_solve(xs, upper, weights, lam, eig):
    pairs, width = xs[0].shape
    rows = pairs // 2
    return pl.pallas_call(
        level_kernel,
        in_specs=[VMEM] * 11,
        out_specs=[VMEM] * 5,
        out_shape=[jax.ShapeDtypeStruct((4 * rows, width), F32)] * 4
        + [jax.ShapeDtypeStruct((2 * NZ, 4, LANES), F32)],
        scratch_shapes=[
            pltpu.VMEM((rows // 2, NZ, 256), F32),
            pltpu.VMEM((rows, NZ, 256), F32),
        ],
        compiler_params=grant(12),
        name="level_solve",
    )(*xs, upper, *weights, lam, eig)


def carry_kernel(ends, lam, eig, out):
    sections = ends.shape[0]
    j = lax.axis_index("rows")
    k = lax.rem(j, NZ)
    h = lax.div(j, NZ)
    e = eig[pl.ds(lax.axis_index("lev") * 2 + h, 1), :]
    r, _ = decay(lam[pl.ds(k, 1), 0:1], e)
    for _ in range(6):
        r = r * r
    row = lax.broadcasted_iota(jnp.int32, (4, LANES), 0)
    ratio = jnp.where(lax.rem(row, 2) == 0, r[:, :LANES], r[:, LANES:])
    whole = ratio
    for _ in range(5):
        whole = whole * whole
    scale = 1.0 / (1.0 - whole)
    up = jnp.zeros((4, LANES), F32)
    down = jnp.zeros((4, LANES), F32)
    for s in range(sections):
        up = ends[s] + ratio * up
        down = ends[sections - 1 - s] + ratio * down
    up = up * scale
    down = down * scale
    first = row < 2
    ups = []
    for s in range(sections):
        ups.append(up)
        up = ends[s] + ratio * up
    for s in reversed(range(sections)):
        value = jnp.where(first, ups[s], down)
        for section in range(4):
            out[s, section] = value
        down = ends[s] + ratio * down


def carries(ends, lam, eig):
    return pl.pallas_call(
        carry_kernel,
        in_specs=[VMEM] * 3,
        out_specs=VMEM,
        out_shape=jax.ShapeDtypeStruct((ends.shape[0], 4) + ends.shape[1:], F32),
        compiler_params=grant(4),
        name="section_carries",
    )(ends, lam, eig)


def shift(value, step):
    return lax.ppermute(value, "lev", [(i, (i + step) % 4) for i in range(4)])


def body(source, solid, couplings):
    full, edge, twiddle, eig, spread = host_tables()
    fh, fl = split_host(full)
    eh, el = split_host(edge)
    fth, ftl = split_host(full.T)
    eth, etl = split_host(edge.T)
    lam, modes, w2h, w2l, w4h, w4l = eigen(couplings)
    xs = []
    for half in (1, 0):
        parts = forward_x(source, solid, (spread, twiddle, fh, fl, eh, el), half)
        xs.append([parts[0]] + [shift(parts[step], -step) for step in (1, 2, 3)])
    tables = decay_tables(lam, eig)
    upper = level_modes_of(xs[0], w2h, w2l, tables[0])
    *parts, ends = level_solve(xs[1], upper, (w2h, w2l, w4h, w4l), lam, eig)
    specs = [parts[0]] + [shift(parts[step], step) for step in (1, 2, 3)]
    ends = lax.all_to_all(ends, "rows", 0, 0, tiled=True)
    ends = carries(ends, lam, eig).reshape(128, 4, LANES)
    ends = lax.all_to_all(ends, ("rows", "lev"), 0, 0, tiled=True).reshape(2, NZ, 4, 4, LANES)
    return inverse_x(specs, ends, modes, lam, eig, tables, (twiddle, fth, ftl, eth, etl))


def solution(mesh):
    return jax.shard_map(
        body,
        mesh=mesh,
        in_specs=(P("rows", "lev", None), P("rows", "lev", None), P()),
        out_specs=P("rows", "lev", None),
        check_vma=False,
    )
```

```python
import math

import jax
import jax.numpy as jnp
import ml_dtypes
import numpy as np
from jax import lax
from jax.experimental import pallas as pl
from jax.experimental.pallas import tpu as pltpu
from jax.sharding import PartitionSpec as P

F32 = jnp.float32
BF16 = jnp.bfloat16
BY = 8
BX = 64
N = 2048
LANES = 128
NZ = 16
TURN = 2.0 * math.pi
RESIDUES = (1, 5, 9, 13, 2, 10, 4)
SWEEPS = 12
TILES = 4


VMEM = pl.BlockSpec(memory_space=pltpu.VMEM)


def grant(mebibytes):
    return pltpu.CompilerParams(vmem_limit_bytes=mebibytes << 20)


def split_host(table):
    table = np.asarray(table, np.float32)
    high = table.astype(ml_dtypes.bfloat16)
    low = (table - high.astype(np.float32)).astype(ml_dtypes.bfloat16)
    return high, low


def host_tables():
    b = np.arange(LANES)
    m = np.arange(LANES)
    angle = TURN * np.mod(np.outer(b, m), LANES) / LANES
    scale = math.sqrt(2.0 / N)
    cos, sin = scale * np.cos(angle), scale * np.sin(angle)
    full = np.block([[cos, -sin], [sin, cos]])
    edge = np.zeros((2 * LANES, 2 * LANES))
    freq0 = np.concatenate([np.arange(65), np.arange(1, 64)])
    angle0 = TURN * np.mod(np.outer(b, freq0), LANES) / LANES
    part = np.where(np.arange(LANES)[None, :] < 65, np.cos(angle0), -np.sin(angle0)) * scale
    part[:, 0] *= math.sqrt(0.5)
    part[:, 64] *= math.sqrt(0.5)
    edge[:LANES, :LANES] = part
    freq8 = 16 * np.arange(64) + 8
    angle8 = TURN * np.mod(np.outer(b, freq8), N) / N
    edge[LANES:, LANES:] = scale * np.concatenate([np.cos(angle8), -np.sin(angle8)], 1)
    q = np.array(RESIDUES)
    twist = TURN * np.outer(q, b) / N
    twiddle = np.zeros((16, LANES), np.float32)
    twiddle[:7] = np.cos(twist)
    twiddle[8:15] = np.sin(twist)
    freqs = [np.concatenate([16 * freq0, freq8, freq8])]
    for residue in RESIDUES:
        freqs.append(np.tile(16 * m + residue, 2))
    freqs = np.concatenate(freqs)
    eigen = (4.0 * np.sin(np.pi * freqs / N) ** 2).astype(np.float32).reshape(8, 256)
    spread = (np.arange(32)[:, None] == np.arange(N)[None, :] // BX).astype(ml_dtypes.bfloat16)
    return full, edge, twiddle, eigen, spread


def halves(value):
    high = value.astype(BF16)
    return high, (value - high.astype(F32)).astype(BF16)


def mm(left, right):
    return jnp.dot(left, right, preferred_element_type=F32)


def mm3(left, right):
    return mm(left[0], right[0]) + (mm(left[1], right[0]) + mm(left[0], right[1]))


def cmul(value, cos, sin):
    re, im = value
    return re * cos + im * sin, im * cos - re * sin


def cadd(left, right):
    return left[0] + right[0], left[1] + right[1]


def csub(left, right):
    return left[0] - right[0], left[1] - right[1]


def phase(steps):
    return math.cos(TURN * steps / 16), math.sin(TURN * steps / 16)


def real16(v):
    s = [v[a] + v[a + 8] for a in range(8)]
    d = [v[a] - v[a + 8] for a in range(8)]
    u = [(d[0], -d[4])]
    for a in range(1, 4):
        u.append(cmul((d[a], -d[a + 4]), *phase(a)))
    p02, m02 = cadd(u[0], u[2]), csub(u[0], u[2])
    p13, m13 = cadd(u[1], u[3]), csub(u[1], u[3])
    y1, y9 = cadd(p02, p13), csub(p02, p13)
    y5 = (m02[0] + m13[1], m02[1] - m13[0])
    y13 = (m02[0] - m13[1], m02[1] + m13[0])
    t = [s[a] + s[a + 4] for a in range(4)]
    e = [s[a] - s[a + 4] for a in range(4)]
    z1 = cmul((e[1], -e[3]), *phase(2))
    z0 = (e[0], -e[2])
    y2, y10 = cadd(z0, z1), csub(z0, z1)
    a0, a1 = t[0] + t[2], t[1] + t[3]
    y4 = (t[0] - t[2], t[3] - t[1])
    return (a0 + a1, a0 - a1), (y1, y5, y9, y13, y2, y10, y4)


def real16_back(real, comps):
    g1, g5, g9, g13, g2, g10, g4 = comps
    a0, a1 = real[0] + real[1], real[0] - real[1]
    t = [a0 + g4[0], a1 - g4[1], a0 - g4[0], a1 + g4[1]]
    z0 = cadd(g2, g10)
    cos, sin = phase(2)
    z1 = cmul(csub(g2, g10), cos, -sin)
    e = [z0[0], z1[0], -z0[1], -z1[1]]
    s = [t[a] + e[a] for a in range(4)] + [t[a] - e[a] for a in range(4)]
    p19, m19 = cadd(g1, g9), csub(g1, g9)
    p513, m513 = cadd(g5, g13), csub(g5, g13)
    u = [cadd(p19, p513), None, csub(p19, p513), None]
    u[1] = (m19[0] - m513[1], m19[1] + m513[0])
    u[3] = (m19[0] + m513[1], m19[1] - m513[0])
    d = [None] * 8
    for a in range(4):
        cos, sin = phase(a)
        z = u[a] if a == 0 else cmul(u[a], cos, -sin)
        d[a], d[a + 4] = z[0], -z[1]
    return [s[a] + d[a] for a in range(8)] + [s[a] - d[a] for a in range(8)]


YB = 16


def forward_x_kernel(
    src, solid, spread, twiddle, fh, fl, eh, el, out0, out1, out2, out3, *scratch
):
    hi, lo, hi0, lo0 = [scratch[2 * n : 2 * n + 2] for n in range(4)]
    outs = (out0, out1, out2, out3)
    firsts = []
    lev = lax.axis_index("lev")
    levels = src.shape[1]
    rows = levels * YB
    open_cells = (1 - solid[...]).astype(F32).astype(BF16)
    twice = [open_cells[i] for i in range(YB // BY) for _ in range(2)]
    masks = mm(jnp.concatenate(twice, 0), spread[...])
    for part in range(levels):
        near = slice(4 * part, 4 * part + 4)
        mask_at = 8 * (part // 2)
        cells = []
        for a in range(16):
            cols = slice(a * LANES, (a + 1) * LANES)
            piece = src[near, :, cols].reshape(2, 8, LANES)
            cells.append((piece * masks[None, mask_at : mask_at + 8, cols]).reshape(16, LANES))
        real, comps = real16(cells)
        group, at = part // 2, 16 * (part % 2)
        for half in range(2):
            cols = slice(half * LANES, (half + 1) * LANES)
            hi0[group][at : at + 16, cols], lo0[group][at : at + 16, cols] = halves(real[half])
        for i in range(1, 8):
            block = cmul(comps[i - 1], twiddle[i - 1 : i, :], twiddle[7 + i : 8 + i, :])
            slot = 2 * ((lev - i // 2) & 3) + i % 2
            place = pl.ds(pl.multiple_of(slot * 32 + at, 16), 16)
            for half in range(2):
                cols = slice(half * LANES, (half + 1) * LANES)
                hi[group][place, cols], lo[group][place, cols] = halves(block[half])
        if part % 2 == 0:
            continue
        band = pl.ds(pl.multiple_of(pl.program_id(0) * rows + 32 * group, 32), 32)
        rest = mm3((hi[group][...], lo[group][...]), (fh[...], fl[...]))
        for slot in range(8):
            cols = slice(slot % 2 * 256, slot % 2 * 256 + 256)
            outs[slot // 2][band, cols] = rest[slot * 32 : slot * 32 + 32]
        firsts.append((band, mm3((hi0[group][...], lo0[group][...]), (eh[...], el[...]))))
    for step in range(4):

        @pl.when(lev == step)
        def _(step=step):
            for band, first in firsts:
                outs[step][band, 0:256] = first


def forward_x(source, solid, consts, half):
    rows, levels, cells = source.shape
    steps = rows // YB // 2
    first = half * steps
    return pl.pallas_call(
        forward_x_kernel,
        grid=(steps,),
        in_specs=[
            pl.BlockSpec((YB, levels, cells), lambda i: (i + first, 0, 0)),
            pl.BlockSpec((YB // BY, levels, cells // BX), lambda i: (i + first, 0, 0)),
        ]
        + [pl.BlockSpec(value.shape, lambda i: (0, 0)) for value in consts],
        out_specs=[VMEM] * 4,
        out_shape=[jax.ShapeDtypeStruct((rows * levels // 2, 512), F32)] * 4,
        scratch_shapes=[pltpu.VMEM((4 * levels * YB, 256), BF16)] * 4
        + [pltpu.VMEM((levels * YB // 2, 256), BF16)] * 4,
        compiler_params=grant(12),
        name=f"forward_x_{half}",
    )(*[pltpu.with_memory_space_constraint(value, pltpu.HBM) for value in (source, solid, *consts)])


def rsqrt(value):
    root = lax.rsqrt(value)
    return root * (1.5 - 0.5 * value * root * root)


def eigen_kernel(coup, lam, modes, w2h, w2l, w4h, w4l):
    sub = lax.broadcasted_iota(jnp.int32, (8, LANES), 0)
    lane = lax.broadcasted_iota(jnp.int32, (8, LANES), 1) & (NZ - 1)
    low = lane < 8
    g = [jnp.zeros((8, LANES), F32), jnp.zeros((8, LANES), F32)]
    link = jnp.zeros((8, LANES), F32)
    for k in range(NZ):
        pivot = coup[k] + coup[k + 1] - link * link
        inverse = rsqrt(pivot)
        here = lane == (k // 2 + 8 * (k % 2))
        g[k // 8] = jnp.where(here & (sub == k % 8), pivot * inverse, g[k // 8])
        link = -coup[k + 1] * inverse
        if k < NZ - 1:
            below = (k + 1) // 8
            g[below] = jnp.where(here & (sub == (k + 1) % 8), link, g[below])
    partners = [pltpu.roll(value, 8, 1) for value in g]

    def total(first, second):
        value = first + second
        for shift in (4, 2, 1):
            value = value + pltpu.roll(value, shift, 0)
        return value

    def right(value):
        return pltpu.roll(value, 1, 1)

    def left(value):
        return pltpu.roll(value, LANES - 1, 1)

    def step(_, carry):
        g0, g1, p0, p1, worst = carry
        own = total(g0 * g0, g1 * g1)
        other = total(p0 * p0, p1 * p1)
        a = total(g0 * p0, g1 * p1)
        d = other - own
        w = d * d + 4.0 * a * a
        h = rsqrt(w)
        x = 0.5 + 0.5 * jnp.abs(d) * h
        y = rsqrt(x)
        positive = (d > 0.0) | ((d == 0.0) & low)
        turn = a * h * y
        still = w == 0.0
        c = jnp.where(still, 1.0, x * y)
        turn = jnp.where(still, 0.0, jnp.where(positive, turn, -turn))
        worst = jnp.maximum(worst, jnp.where(still, 0.0, a * a / (own * other)))
        out = []
        for value, partner in ((g0, p0), (g1, p1)):
            mine = c * value - turn * partner
            theirs = c * partner + turn * value
            rising = right(jnp.where(lane == 0, theirs, mine))
            new = jnp.where(low, rising, jnp.where(lane == 15, theirs, left(mine)))
            new = jnp.where(lane == 0, mine, new)
            falling = right(jnp.where(lane == 8, mine, theirs))
            new_partner = jnp.where(low, jnp.where(lane == 7, mine, left(theirs)), falling)
            new_partner = jnp.where(lane == 8, theirs, new_partner)
            out.append((new, new_partner))
        return out[0][0], out[1][0], out[0][1], out[1][1], worst

    def sweep(carry):
        count, _, *state = carry
        state = lax.fori_loop(0, 15, step, (*state, jnp.zeros((8, LANES), F32)))
        return (count + 1, jnp.max(state[4]), *state[:4])

    def unfinished(carry):
        return (carry[0] < SWEEPS) & (carry[1] > 1e-7)

    state = (jnp.int32(0), jnp.float32(1.0), g[0], g[1], partners[0], partners[1])
    _, _, g0, g1, _, _ = lax.while_loop(unfinished, sweep, state)
    square = total(g0 * g0, g1 * g1)
    inverse = rsqrt(square)
    vectors = jnp.concatenate([g0 * inverse, g1 * inverse], 0)
    lam[...] = jnp.concatenate([square] * NZ, 0).T[:NZ]
    modes[...] = jnp.concatenate([vectors] * 8, 0).T[:NZ]
    row = lax.broadcasted_iota(jnp.int32, (LANES, LANES), 0)
    col = lax.broadcasted_iota(jnp.int32, (LANES, LANES), 1)
    for section in range(4):
        group = []
        for s in range(4):
            at = (4 * section + 4 * s) % NZ
            group += [vectors[at : at + 4]] * 8
        w4 = jnp.where(row % 32 // 4 == col // NZ, jnp.concatenate(group, 0), 0.0)
        w4h[section], w4l[section] = halves(w4)
        w2h[section], w2l[section] = halves(w4.T)


def eigen(couplings):
    table = jax.ShapeDtypeStruct((NZ, LANES), F32)
    matrix = jax.ShapeDtypeStruct((4, LANES, LANES), BF16)
    return pl.pallas_call(
        eigen_kernel,
        in_specs=[pl.BlockSpec(memory_space=pltpu.SMEM)],
        out_specs=[VMEM] * 6,
        out_shape=[table, table, matrix, matrix, matrix, matrix],
        compiler_params=grant(4),
        name="level_modes",
    )(couplings)


def decay(lam, e):
    half = 0.5 * (lam + e)
    root = jnp.sqrt(half * (2.0 + half))
    return 1.0 / (1.0 + half + root), 0.5 / root


def decay_kernel(lam, eig, rise, fall, steps, shelf):
    b = lax.broadcasted_iota(jnp.int32, (8, LANES), 0)
    odd, half, upper = [(b & bit) != 0 for bit in (1, 2, 4)]

    def choose(mask, factor):
        return jnp.where(mask, factor, 1.0)

    for t in range(16):
        e = eig[t // 2 : t // 2 + 1, (t % 2) * LANES : (t % 2 + 1) * LANES]
        r, gain = decay(lam[:, 0:1], e)
        r2 = r * r
        r4 = r2 * r2
        for n, value in enumerate((r, r2, r4, gain * r)):
            shelf[t, n, :NZ] = value
        ladder = [jnp.ones_like(r)]
        for _ in range(2 * steps.shape[0] - 1):
            ladder.append(ladder[-1] * (r4 * r4))
        for i in range(steps.shape[0]):
            near, far = ladder[i], ladder[-1 - i]
            steps[i, 0, t] = 0.5 * (near + far)
            steps[i, 1, t] = 0.5 * (near - far)
        for k in range(NZ):
            row = pl.ds(k, 8, stride=0)
            r1, r2, r4, scale = [shelf[t, n, row, :] for n in range(4)]
            more = scale * r1
            rise[t, k] = jnp.where(odd, more, scale) * (choose(half, r2) * choose(upper, r4))
            fall[t, k] = jnp.where(odd, scale, more) * (choose(~half, r2) * choose(~upper, r4))


def decay_tables(lam, eig, octets):
    return pl.pallas_call(
        decay_kernel,
        in_specs=[VMEM] * 2,
        out_specs=[VMEM] * 3,
        out_shape=[jax.ShapeDtypeStruct((16, NZ, 8, LANES), F32)] * 2
        + [jax.ShapeDtypeStruct((octets // 2, 2, 16, NZ, LANES), F32)],
        scratch_shapes=[pltpu.VMEM((16, 4, NZ + 8, LANES), F32)],
        compiler_params=grant(8),
        name="decay_tables",
    )(lam, eig)


def inverse_x_kernel(
    spec0, spec1, spec2, spec3, ends, modes, rise, fall, steps, twiddle, fh, fl, eh, el,
    out, hi, lo, even, odds, turn, ready, sems,
):
    levels = out.shape[1]
    rows = levels * YB
    lev = lax.axis_index("lev")
    i = pl.program_id(0)
    last = pl.num_programs(0) - 1
    mirror = 2 * last + 1 - i
    side = i & 1

    def leave(step, o):
        octet = step if o == 0 else 2 * last + 1 - step
        return pltpu.make_async_copy(
            ready.at[step & 1, o], out.at[pl.ds(octet * 8, 8)], sems.at[step & 1, o]
        )

    @pl.when(i >= 2)
    def _():
        for o in range(2):
            leave(i - 2, o).wait()

    @pl.when(i == 0)
    def _():
        for t in range(16):
            l, h, p = t // 4, (t // 2) % 2, t % 2
            for k in range(NZ):
                up = rise[t, k] * ends[h, k, l, p : p + 1, :]
                down = fall[t, k] * ends[h, k, l, 2 + p : 3 + p, :]
                even[t, k] = up + down
                odds[t, k] = up - down

    first_level = lev * levels
    for step, spec in enumerate((spec0, spec1, spec2, spec3)):
        l = (lev - step) & 3
        for group in range(4 // TILES):
            parts = range(group * TILES, (group + 1) * TILES)
            acc = {}
            for k in range(NZ):
                scale = [modes[k, first_level + z] for z in range(levels)]
                for part in parts:
                    t = 4 * l + part
                    for o, table in enumerate((even, odds)):
                        value = table[t, k] * steps[i, o, t, k : k + 1, :]
                        for z in range(levels):
                            term = value * scale[z]
                            acc[part, z, o] = term if k == 0 else acc[part, z, o] + term
            for part in parts:
                place = turn.at[4 * step + part]
                for z in range(levels):
                    place[pl.ds(z, 8, stride=4), :] = acc[part, z, 0] + acc[part, z, 1]
                    place[pl.ds(32 + z, 8, stride=4), :] = acc[part, z, 0] - acc[part, z, 1]
        for part in range(4):
            for q in range(rows // 16):
                octet = i if q < 2 else mirror
                near = pl.ds(pl.multiple_of(32 * octet + 16 * (q % 2), 16), 16)
                value = spec[near, part * LANES : (part + 1) * LANES]
                value = value + turn[4 * step + part, 16 * q : 16 * q + 16, :]
                high, low = halves(value)
                place = pl.multiple_of((2 * l + part // 2) * rows + 16 * q, 16)
                half = pl.ds((part % 2) * LANES, LANES)
                hi[pl.ds(place, 16), half] = high
                lo[pl.ds(place, 16), half] = low
    first = mm3((hi[:rows, :], lo[:rows, :]), (eh[...], el[...]))
    rest = mm3((hi[rows:, :], lo[rows:, :]), (fh[...], fl[...]))
    for q in range(rows // 16):
        at = slice(16 * q, 16 * q + 16)
        real = (first[at, :LANES], first[at, LANES:])
        comps = []
        for n in range(7):
            at = slice(n * rows + 16 * q, n * rows + 16 * q + 16)
            value = (rest[at, :LANES], rest[at, LANES:])
            comps.append(cmul(value, twiddle[n : n + 1, :], -twiddle[8 + n : 9 + n, :]))
        cells = real16_back(real, comps)
        here = slice(4 * (q % 2), 4 * (q % 2) + 4)
        for a in range(16):
            cols = slice(a * LANES, (a + 1) * LANES)
            ready[side, q // 2, here, :, cols] = cells[a].reshape(4, levels, LANES)
    for o in range(2):
        leave(i, o).start()

    @pl.when(i == last)
    def _():
        for step in (i - 1, i):
            for o in range(2):
                leave(step, o).wait()


def inverse_x(specs, ends, modes, tables, consts):
    levels = 4
    rows = specs[0].shape[0] // levels
    return pl.pallas_call(
        inverse_x_kernel,
        grid=(rows // YB,),
        in_specs=[VMEM] * 5 + [pl.BlockSpec(memory_space=pltpu.SMEM)] + [VMEM] * 8,
        out_specs=pl.BlockSpec(memory_space=pl.ANY),
        out_shape=jax.ShapeDtypeStruct((rows, levels, N), F32),
        scratch_shapes=[pltpu.VMEM((8 * levels * YB, 256), BF16)] * 2
        + [pltpu.VMEM((16, NZ, 8, LANES), F32)] * 2
        + [pltpu.VMEM((16, 4 * YB, LANES), F32)]
        + [pltpu.VMEM((2, 2, 8, levels, N), F32), pltpu.SemaphoreType.DMA((2, 2))],
        compiler_params=grant(16),
        name="inverse_x",
    )(*specs, ends, modes, *tables, *consts)


def modes_kernel(x0, x1, x2, x3, wh, wl, _, f):
    lev = lax.axis_index("lev")
    w = (wh[lev], wl[lev])
    for h in range(f.shape[0]):
        cols = pl.ds(h * 256, 256)
        for o in range(x0.shape[0] // 32):
            block = [x[32 * o : 32 * o + 32, cols] for x in (x0, x1, x2, x3)]
            value = mm3(w, halves(jnp.concatenate(block, 0)))
            f[h, 8 * o : 8 * o + 8] = value.reshape(8, NZ, 256)


def level_modes_of(xs, wh, wl, after):
    pairs, width = xs[0].shape
    return pl.pallas_call(
        modes_kernel,
        in_specs=[VMEM] * 7,
        out_specs=VMEM,
        out_shape=jax.ShapeDtypeStruct((width // 256, pairs // 4, NZ, 256), F32),
        compiler_params=grant(8),
        name="mode_values",
    )(*xs, wh, wl, after)


def level_kernel(
    x0, x1, x2, x3, upper, w2h, w2l, w4h, w4l, lam, eig, out0, out1, out2, out3, ends, f, work
):
    lev = lax.axis_index("lev")
    octets = x0.shape[0] // 32
    half = 8 * octets
    rows = 2 * half
    w2 = (w2h[lev], w2l[lev])
    w4 = (w4h[lev], w4l[lev])
    for h in range(x0.shape[1] // 256):
        cols = pl.ds(h * 256, 256)
        e = eig[pl.ds(lev * 2 + h, 1), :]
        r, gain = decay(lam[:, 0:1], e)
        for o in range(octets):
            block = [x[32 * o : 32 * o + 32, cols] for x in (x0, x1, x2, x3)]
            value = mm3(w2, halves(jnp.concatenate(block, 0)))
            f[8 * o : 8 * o + 8] = value.reshape(8, NZ, 256)

        def source(y):
            return f[y] if y < half else upper[h, y - half]

        up = jnp.zeros((NZ, 256), F32)
        down = jnp.zeros((NZ, 256), F32)
        for y in range(rows):
            up = r * up
            work[y] = up
            up = up + source(y)
        for y in reversed(range(rows)):
            down = source(y) + r * down
            work[y] = (work[y] + down) * gain
        place = pl.ds(h * NZ, NZ)
        ends[place, 0, :] = up[:, :LANES]
        ends[place, 1, :] = up[:, LANES:]
        ends[place, 2, :] = down[:, :LANES]
        ends[place, 3, :] = down[:, LANES:]
        for o in range(rows // 8):
            block = work[8 * o : 8 * o + 8].reshape(LANES, 256)
            value = mm3(w4, halves(block))
            for step, out in enumerate((out0, out1, out2, out3)):
                out[32 * o : 32 * o + 32, cols] = value[32 * step : 32 * step + 32]


def level_solve(xs, upper, weights, lam, eig):
    pairs, width = xs[0].shape
    rows = pairs // 2
    return pl.pallas_call(
        level_kernel,
        in_specs=[VMEM] * 11,
        out_specs=[VMEM] * 5,
        out_shape=[jax.ShapeDtypeStruct((4 * rows, width), F32)] * 4
        + [jax.ShapeDtypeStruct((2 * NZ, 4, LANES), F32)],
        scratch_shapes=[
            pltpu.VMEM((rows // 2, NZ, 256), F32),
            pltpu.VMEM((rows, NZ, 256), F32),
        ],
        compiler_params=grant(12),
        name="level_solve",
    )(*xs, upper, *weights, lam, eig)


def carry_kernel(ends, lam, eig, out):
    sections = ends.shape[0]
    j = lax.axis_index("rows")
    k = lax.rem(j, NZ)
    h = lax.div(j, NZ)
    e = eig[pl.ds(lax.axis_index("lev") * 2 + h, 1), :]
    r, _ = decay(lam[pl.ds(k, 1), 0:1], e)
    for _ in range(6):
        r = r * r
    row = lax.broadcasted_iota(jnp.int32, (4, LANES), 0)
    ratio = jnp.where(lax.rem(row, 2) == 0, r[:, :LANES], r[:, LANES:])
    whole = ratio
    for _ in range(5):
        whole = whole * whole
    scale = 1.0 / (1.0 - whole)
    up = jnp.zeros((4, LANES), F32)
    down = jnp.zeros((4, LANES), F32)
    for s in range(sections):
        up = ends[s] + ratio * up
        down = ends[sections - 1 - s] + ratio * down
    up = up * scale
    down = down * scale
    first = row < 2
    ups = []
    for s in range(sections):
        ups.append(up)
        up = ends[s] + ratio * up
    for s in reversed(range(sections)):
        value = jnp.where(first, ups[s], down)
        for section in range(4):
            out[s, section] = value
        down = ends[s] + ratio * down


def carries(ends, lam, eig):
    return pl.pallas_call(
        carry_kernel,
        in_specs=[VMEM] * 3,
        out_specs=VMEM,
        out_shape=jax.ShapeDtypeStruct((ends.shape[0], 4) + ends.shape[1:], F32),
        compiler_params=grant(4),
        name="section_carries",
    )(ends, lam, eig)


def shift(value, step):
    return lax.ppermute(value, "lev", [(i, (i + step) % 4) for i in range(4)])


def body(source, solid, couplings):
    full, edge, twiddle, eig, spread = host_tables()
    fh, fl = split_host(full)
    eh, el = split_host(edge)
    fth, ftl = split_host(full.T)
    eth, etl = split_host(edge.T)
    lam, modes, w2h, w2l, w4h, w4l = eigen(couplings)
    xs = []
    for half in (1, 0):
        parts = forward_x(source, solid, (spread, twiddle, fh, fl, eh, el), half)
        xs.append([parts[0]] + [shift(parts[step], -step) for step in (1, 2, 3)])
    tables = decay_tables(lam, eig, source.shape[0] // 8)
    upper = level_modes_of(xs[0], w2h, w2l, tables[0])
    *parts, ends = level_solve(xs[1], upper, (w2h, w2l, w4h, w4l), lam, eig)
    specs = [parts[0]] + [shift(parts[step], step) for step in (1, 2, 3)]
    ends = lax.all_to_all(ends, "rows", 0, 0, tiled=True)
    ends = carries(ends, lam, eig).reshape(128, 4, LANES)
    ends = lax.all_to_all(ends, ("rows", "lev"), 0, 0, tiled=True).reshape(2, NZ, 4, 4, LANES)
    return inverse_x(specs, ends, modes, tables, (twiddle, fth, ftl, eth, etl))


def solution(mesh):
    return jax.shard_map(
        body,
        mesh=mesh,
        in_specs=(P("rows", "lev", None), P("rows", "lev", None), P()),
        out_specs=P("rows", "lev", None),
        check_vma=False,
    )
```

```python
import math

import jax
import jax.numpy as jnp
import ml_dtypes
import numpy as np
from jax import lax
from jax.experimental import pallas as pl
from jax.experimental.pallas import tpu as pltpu
from jax.sharding import PartitionSpec as P

F32 = jnp.float32
BF16 = jnp.bfloat16
BY = 8
BX = 64
N = 2048
LANES = 128
NZ = 16
TURN = 2.0 * math.pi
RESIDUES = (1, 5, 9, 13, 2, 10, 4)
SWEEPS = 12
TILES = 4


VMEM = pl.BlockSpec(memory_space=pltpu.VMEM)


def grant(mebibytes):
    return pltpu.CompilerParams(vmem_limit_bytes=mebibytes << 20)


def split_host(table):
    table = np.asarray(table, np.float32)
    high = table.astype(ml_dtypes.bfloat16)
    low = (table - high.astype(np.float32)).astype(ml_dtypes.bfloat16)
    return high, low


def host_tables():
    b = np.arange(LANES)
    m = np.arange(LANES)
    angle = TURN * np.mod(np.outer(b, m), LANES) / LANES
    scale = math.sqrt(2.0 / N)
    cos, sin = scale * np.cos(angle), scale * np.sin(angle)
    full = np.block([[cos, -sin], [sin, cos]])
    edge = np.zeros((2 * LANES, 2 * LANES))
    freq0 = np.concatenate([np.arange(65), np.arange(1, 64)])
    angle0 = TURN * np.mod(np.outer(b, freq0), LANES) / LANES
    part = np.where(np.arange(LANES)[None, :] < 65, np.cos(angle0), -np.sin(angle0)) * scale
    part[:, 0] *= math.sqrt(0.5)
    part[:, 64] *= math.sqrt(0.5)
    edge[:LANES, :LANES] = part
    freq8 = 16 * np.arange(64) + 8
    angle8 = TURN * np.mod(np.outer(b, freq8), N) / N
    edge[LANES:, LANES:] = scale * np.concatenate([np.cos(angle8), -np.sin(angle8)], 1)
    q = np.array(RESIDUES)
    twist = TURN * np.outer(q, b) / N
    twiddle = np.zeros((16, LANES), np.float32)
    twiddle[:7] = np.cos(twist)
    twiddle[8:15] = np.sin(twist)
    freqs = [np.concatenate([16 * freq0, freq8, freq8])]
    for residue in RESIDUES:
        freqs.append(np.tile(16 * m + residue, 2))
    freqs = np.concatenate(freqs)
    eigen = (4.0 * np.sin(np.pi * freqs / N) ** 2).astype(np.float32).reshape(8, 256)
    spread = (np.arange(32)[:, None] == np.arange(N)[None, :] // BX).astype(ml_dtypes.bfloat16)
    return full, edge, twiddle, eigen, spread


def halves(value):
    high = value.astype(BF16)
    return high, (value - high.astype(F32)).astype(BF16)


def mm(left, right):
    return jnp.dot(left, right, preferred_element_type=F32)


def mm3(left, right):
    return mm(left[0], right[0]) + (mm(left[1], right[0]) + mm(left[0], right[1]))


def cmul(value, cos, sin):
    re, im = value
    return re * cos + im * sin, im * cos - re * sin


def cadd(left, right):
    return left[0] + right[0], left[1] + right[1]


def csub(left, right):
    return left[0] - right[0], left[1] - right[1]


def phase(steps):
    return math.cos(TURN * steps / 16), math.sin(TURN * steps / 16)


def real16(v):
    s = [v[a] + v[a + 8] for a in range(8)]
    d = [v[a] - v[a + 8] for a in range(8)]
    u = [(d[0], -d[4])]
    for a in range(1, 4):
        u.append(cmul((d[a], -d[a + 4]), *phase(a)))
    p02, m02 = cadd(u[0], u[2]), csub(u[0], u[2])
    p13, m13 = cadd(u[1], u[3]), csub(u[1], u[3])
    y1, y9 = cadd(p02, p13), csub(p02, p13)
    y5 = (m02[0] + m13[1], m02[1] - m13[0])
    y13 = (m02[0] - m13[1], m02[1] + m13[0])
    t = [s[a] + s[a + 4] for a in range(4)]
    e = [s[a] - s[a + 4] for a in range(4)]
    z1 = cmul((e[1], -e[3]), *phase(2))
    z0 = (e[0], -e[2])
    y2, y10 = cadd(z0, z1), csub(z0, z1)
    a0, a1 = t[0] + t[2], t[1] + t[3]
    y4 = (t[0] - t[2], t[3] - t[1])
    return (a0 + a1, a0 - a1), (y1, y5, y9, y13, y2, y10, y4)


def real16_back(real, comps):
    g1, g5, g9, g13, g2, g10, g4 = comps
    a0, a1 = real[0] + real[1], real[0] - real[1]
    t = [a0 + g4[0], a1 - g4[1], a0 - g4[0], a1 + g4[1]]
    z0 = cadd(g2, g10)
    cos, sin = phase(2)
    z1 = cmul(csub(g2, g10), cos, -sin)
    e = [z0[0], z1[0], -z0[1], -z1[1]]
    s = [t[a] + e[a] for a in range(4)] + [t[a] - e[a] for a in range(4)]
    p19, m19 = cadd(g1, g9), csub(g1, g9)
    p513, m513 = cadd(g5, g13), csub(g5, g13)
    u = [cadd(p19, p513), None, csub(p19, p513), None]
    u[1] = (m19[0] - m513[1], m19[1] + m513[0])
    u[3] = (m19[0] + m513[1], m19[1] - m513[0])
    d = [None] * 8
    for a in range(4):
        cos, sin = phase(a)
        z = u[a] if a == 0 else cmul(u[a], cos, -sin)
        d[a], d[a + 4] = z[0], -z[1]
    return [s[a] + d[a] for a in range(8)] + [s[a] - d[a] for a in range(8)]


YB = 16


def forward_x_kernel(
    src, solid, spread, twiddle, fh, fl, eh, el, out0, out1, out2, out3, *scratch
):
    hi, lo, hi0, lo0 = [scratch[2 * n : 2 * n + 2] for n in range(4)]
    outs = (out0, out1, out2, out3)
    firsts = []
    lev = lax.axis_index("lev")
    levels = src.shape[1]
    rows = levels * YB
    open_cells = (1 - solid[...]).astype(F32).astype(BF16)
    twice = [open_cells[i] for i in range(YB // BY) for _ in range(2)]
    masks = mm(jnp.concatenate(twice, 0), spread[...])
    for part in range(levels):
        near = slice(4 * part, 4 * part + 4)
        mask_at = 8 * (part // 2)
        cells = []
        for a in range(16):
            cols = slice(a * LANES, (a + 1) * LANES)
            piece = src[near, :, cols].reshape(2, 8, LANES)
            cells.append((piece * masks[None, mask_at : mask_at + 8, cols]).reshape(16, LANES))
        real, comps = real16(cells)
        group, at = part // 2, 16 * (part % 2)
        for half in range(2):
            cols = slice(half * LANES, (half + 1) * LANES)
            hi0[group][at : at + 16, cols], lo0[group][at : at + 16, cols] = halves(real[half])
        for i in range(1, 8):
            block = cmul(comps[i - 1], twiddle[i - 1 : i, :], twiddle[7 + i : 8 + i, :])
            slot = 2 * ((lev - i // 2) & 3) + i % 2
            place = pl.ds(pl.multiple_of(slot * 32 + at, 16), 16)
            for half in range(2):
                cols = slice(half * LANES, (half + 1) * LANES)
                hi[group][place, cols], lo[group][place, cols] = halves(block[half])
        if part % 2 == 0:
            continue
        band = pl.ds(pl.multiple_of(pl.program_id(0) * rows + 32 * group, 32), 32)
        rest = mm3((hi[group][...], lo[group][...]), (fh[...], fl[...]))
        for slot in range(8):
            cols = slice(slot % 2 * 256, slot % 2 * 256 + 256)
            outs[slot // 2][band, cols] = rest[slot * 32 : slot * 32 + 32]
        firsts.append((band, mm3((hi0[group][...], lo0[group][...]), (eh[...], el[...]))))
    for step in range(4):

        @pl.when(lev == step)
        def _(step=step):
            for band, first in firsts:
                outs[step][band, 0:256] = first


def forward_x(source, solid, consts, half):
    rows, levels, cells = source.shape
    steps = rows // YB // 2
    first = half * steps
    return pl.pallas_call(
        forward_x_kernel,
        grid=(steps,),
        in_specs=[
            pl.BlockSpec((YB, levels, cells), lambda i: (i + first, 0, 0)),
            pl.BlockSpec((YB // BY, levels, cells // BX), lambda i: (i + first, 0, 0)),
        ]
        + [pl.BlockSpec(value.shape, lambda i: (0, 0)) for value in consts],
        out_specs=[VMEM] * 4,
        out_shape=[jax.ShapeDtypeStruct((rows * levels // 2, 512), F32)] * 4,
        scratch_shapes=[pltpu.VMEM((4 * levels * YB, 256), BF16)] * 4
        + [pltpu.VMEM((levels * YB // 2, 256), BF16)] * 4,
        compiler_params=grant(12),
        name=f"forward_x_{half}",
    )(*[pltpu.with_memory_space_constraint(value, pltpu.HBM) for value in (source, solid, *consts)])


def rsqrt(value):
    root = lax.rsqrt(value)
    return root * (1.5 - 0.5 * value * root * root)


def eigen_kernel(coup, lam, modes, w2h, w2l, w4h, w4l):
    sub = lax.broadcasted_iota(jnp.int32, (8, LANES), 0)
    lane = lax.broadcasted_iota(jnp.int32, (8, LANES), 1) & (NZ - 1)
    low = lane < 8
    g = [jnp.zeros((8, LANES), F32), jnp.zeros((8, LANES), F32)]
    link = jnp.zeros((8, LANES), F32)
    for k in range(NZ):
        pivot = coup[k] + coup[k + 1] - link * link
        inverse = rsqrt(pivot)
        here = lane == (k // 2 + 8 * (k % 2))
        g[k // 8] = jnp.where(here & (sub == k % 8), pivot * inverse, g[k // 8])
        link = -coup[k + 1] * inverse
        if k < NZ - 1:
            below = (k + 1) // 8
            g[below] = jnp.where(here & (sub == (k + 1) % 8), link, g[below])
    partners = [pltpu.roll(value, 8, 1) for value in g]

    def total(first, second):
        value = first + second
        for shift in (4, 2, 1):
            value = value + pltpu.roll(value, shift, 0)
        return value

    def right(value):
        return pltpu.roll(value, 1, 1)

    def left(value):
        return pltpu.roll(value, LANES - 1, 1)

    def step(_, carry):
        g0, g1, p0, p1, worst = carry
        own = total(g0 * g0, g1 * g1)
        other = total(p0 * p0, p1 * p1)
        a = total(g0 * p0, g1 * p1)
        d = other - own
        w = d * d + 4.0 * a * a
        h = rsqrt(w)
        x = 0.5 + 0.5 * jnp.abs(d) * h
        y = rsqrt(x)
        positive = (d > 0.0) | ((d == 0.0) & low)
        turn = a * h * y
        still = w == 0.0
        c = jnp.where(still, 1.0, x * y)
        turn = jnp.where(still, 0.0, jnp.where(positive, turn, -turn))
        worst = jnp.maximum(worst, jnp.where(still, 0.0, a * a / (own * other)))
        out = []
        for value, partner in ((g0, p0), (g1, p1)):
            mine = c * value - turn * partner
            theirs = c * partner + turn * value
            rising = right(jnp.where(lane == 0, theirs, mine))
            new = jnp.where(low, rising, jnp.where(lane == 15, theirs, left(mine)))
            new = jnp.where(lane == 0, mine, new)
            falling = right(jnp.where(lane == 8, mine, theirs))
            new_partner = jnp.where(low, jnp.where(lane == 7, mine, left(theirs)), falling)
            new_partner = jnp.where(lane == 8, theirs, new_partner)
            out.append((new, new_partner))
        return out[0][0], out[1][0], out[0][1], out[1][1], worst

    def sweep(carry):
        count, _, *state = carry
        state = lax.fori_loop(0, 15, step, (*state, jnp.zeros((8, LANES), F32)))
        return (count + 1, jnp.max(state[4]), *state[:4])

    def unfinished(carry):
        return (carry[0] < SWEEPS) & (carry[1] > 1e-7)

    state = (jnp.int32(0), jnp.float32(1.0), g[0], g[1], partners[0], partners[1])
    _, _, g0, g1, _, _ = lax.while_loop(unfinished, sweep, state)
    square = total(g0 * g0, g1 * g1)
    inverse = rsqrt(square)
    vectors = jnp.concatenate([g0 * inverse, g1 * inverse], 0)
    lam[...] = jnp.concatenate([square] * NZ, 0).T[:NZ]
    modes[...] = jnp.concatenate([vectors] * 8, 0).T[:NZ]
    row = lax.broadcasted_iota(jnp.int32, (LANES, LANES), 0)
    col = lax.broadcasted_iota(jnp.int32, (LANES, LANES), 1)
    for section in range(4):
        group = []
        for s in range(4):
            at = (4 * section + 4 * s) % NZ
            group += [vectors[at : at + 4]] * 8
        w4 = jnp.where(row % 32 // 4 == col // NZ, jnp.concatenate(group, 0), 0.0)
        w4h[section], w4l[section] = halves(w4)
        w2h[section], w2l[section] = halves(w4.T)


def eigen(couplings):
    table = jax.ShapeDtypeStruct((NZ, LANES), F32)
    matrix = jax.ShapeDtypeStruct((4, LANES, LANES), BF16)
    return pl.pallas_call(
        eigen_kernel,
        in_specs=[pl.BlockSpec(memory_space=pltpu.SMEM)],
        out_specs=[VMEM] * 6,
        out_shape=[table, table, matrix, matrix, matrix, matrix],
        compiler_params=grant(4),
        name="level_modes",
    )(couplings)


def decay(lam, e):
    half = 0.5 * (lam + e)
    root = jnp.sqrt(half * (2.0 + half))
    return 1.0 / (1.0 + half + root), 0.5 / root


def decay_kernel(lam, eig, rise, fall, steps, shelf):
    b = lax.broadcasted_iota(jnp.int32, (8, LANES), 0)
    odd, half, upper = [(b & bit) != 0 for bit in (1, 2, 4)]

    def choose(mask, factor):
        return jnp.where(mask, factor, 1.0)

    for t in range(16):
        e = eig[t // 2 : t // 2 + 1, (t % 2) * LANES : (t % 2 + 1) * LANES]
        r, gain = decay(lam[:, 0:1], e)
        r2 = r * r
        r4 = r2 * r2
        for n, value in enumerate((r, r2, r4, gain * r)):
            shelf[t, n, :NZ] = value
        ladder = [jnp.ones_like(r)]
        for _ in range(2 * steps.shape[0] - 1):
            ladder.append(ladder[-1] * (r4 * r4))
        for i in range(steps.shape[0]):
            near, far = ladder[i], ladder[-1 - i]
            steps[i, 0, t] = 0.5 * (near + far)
            steps[i, 1, t] = 0.5 * (near - far)
        for k in range(NZ):
            row = pl.ds(k, 8, stride=0)
            r1, r2, r4, scale = [shelf[t, n, row, :] for n in range(4)]
            more = scale * r1
            rise[t, k] = jnp.where(odd, more, scale) * (choose(half, r2) * choose(upper, r4))
            fall[t, k] = jnp.where(odd, scale, more) * (choose(~half, r2) * choose(~upper, r4))


def decay_tables(lam, eig, octets):
    return pl.pallas_call(
        decay_kernel,
        in_specs=[VMEM] * 2,
        out_specs=[VMEM] * 3,
        out_shape=[jax.ShapeDtypeStruct((16, NZ, 8, LANES), F32)] * 2
        + [jax.ShapeDtypeStruct((octets // 2, 2, 16, NZ, LANES), F32)],
        scratch_shapes=[pltpu.VMEM((16, 4, NZ + 8, LANES), F32)],
        compiler_params=grant(8),
        name="decay_tables",
    )(lam, eig)


def inverse_x_kernel(
    spec0, spec1, spec2, spec3, ends, modes, rise, fall, steps, twiddle, fh, fl, eh, el,
    out, hi, lo, even, odds, turn, ready, sems,
):
    levels = out.shape[1]
    rows = levels * YB
    lev = lax.axis_index("lev")
    i = pl.program_id(0)
    last = pl.num_programs(0) - 1
    mirror = 2 * last + 1 - i
    side = i & 1

    def leave(step, o):
        octet = step if o == 0 else 2 * last + 1 - step
        return pltpu.make_async_copy(
            ready.at[step & 1, o], out.at[pl.ds(octet * 8, 8)], sems.at[step & 1, o]
        )

    @pl.when(i >= 2)
    def _():
        for o in range(2):
            leave(i - 2, o).wait()

    @pl.when(i == 0)
    def _():
        for t in range(16):
            l, h, p = t // 4, (t // 2) % 2, t % 2
            for k in range(NZ):
                up = rise[t, k] * ends[h, k, l, p : p + 1, :]
                down = fall[t, k] * ends[h, k, l, 2 + p : 3 + p, :]
                even[t, k] = up + down
                odds[t, k] = up - down

    first_level = lev * levels
    for step, spec in enumerate((spec0, spec1, spec2, spec3)):
        l = (lev - step) & 3
        for group in range(4 // TILES):
            parts = range(group * TILES, (group + 1) * TILES)
            acc = {}
            for k in range(NZ):
                scale = [modes[k, first_level + z] for z in range(levels)]
                for part in parts:
                    t = 4 * l + part
                    for o, table in enumerate((even, odds)):
                        value = table[t, k] * steps[i, o, t, k : k + 1, :]
                        for z in range(levels):
                            term = value * scale[z]
                            acc[part, z, o] = term if k == 0 else acc[part, z, o] + term
            for part in parts:
                place = turn.at[4 * step + part]
                for z in range(levels):
                    place[pl.ds(z, 8, stride=4), :] = acc[part, z, 0] + acc[part, z, 1]
                    place[pl.ds(32 + z, 8, stride=4), :] = acc[part, z, 0] - acc[part, z, 1]
        for part in range(4):
            for q in range(rows // 16):
                octet = i if q < 2 else mirror
                near = pl.ds(pl.multiple_of(32 * octet + 16 * (q % 2), 16), 16)
                value = spec[near, part * LANES : (part + 1) * LANES]
                value = value + turn[4 * step + part, 16 * q : 16 * q + 16, :]
                high, low = halves(value)
                place = pl.multiple_of((2 * l + part // 2) * rows + 16 * q, 16)
                half = pl.ds((part % 2) * LANES, LANES)
                hi[pl.ds(place, 16), half] = high
                lo[pl.ds(place, 16), half] = low
    first = mm3((hi[:rows, :], lo[:rows, :]), (eh[...], el[...]))
    rest = mm3((hi[rows:, :], lo[rows:, :]), (fh[...], fl[...]))
    for q in range(rows // 16):
        at = slice(16 * q, 16 * q + 16)
        real = (first[at, :LANES], first[at, LANES:])
        comps = []
        for n in range(7):
            at = slice(n * rows + 16 * q, n * rows + 16 * q + 16)
            value = (rest[at, :LANES], rest[at, LANES:])
            comps.append(cmul(value, twiddle[n : n + 1, :], -twiddle[8 + n : 9 + n, :]))
        cells = real16_back(real, comps)
        here = slice(4 * (q % 2), 4 * (q % 2) + 4)
        for a in range(16):
            cols = slice(a * LANES, (a + 1) * LANES)
            ready[side, q // 2, here, :, cols] = cells[a].reshape(4, levels, LANES)
    for o in range(2):
        leave(i, o).start()

    @pl.when(i == last)
    def _():
        for step in (i - 1, i):
            for o in range(2):
                leave(step, o).wait()


def inverse_x(specs, ends, modes, tables, consts):
    levels = 4
    rows = specs[0].shape[0] // levels
    return pl.pallas_call(
        inverse_x_kernel,
        grid=(rows // YB,),
        in_specs=[VMEM] * 5 + [pl.BlockSpec(memory_space=pltpu.SMEM)] + [VMEM] * 8,
        out_specs=pl.BlockSpec(memory_space=pl.ANY),
        out_shape=jax.ShapeDtypeStruct((rows, levels, N), F32),
        scratch_shapes=[pltpu.VMEM((8 * levels * YB, 256), BF16)] * 2
        + [pltpu.VMEM((16, NZ, 8, LANES), F32)] * 2
        + [pltpu.VMEM((16, 4 * YB, LANES), F32)]
        + [pltpu.VMEM((2, 2, 8, levels, N), F32), pltpu.SemaphoreType.DMA((2, 2))],
        compiler_params=grant(16),
        name="inverse_x",
    )(*specs, ends, modes, *tables, *consts)


def modes_kernel(x0, x1, x2, x3, wh, wl, _, f):
    lev = lax.axis_index("lev")
    w = (wh[lev], wl[lev])
    for h in range(f.shape[0]):
        cols = pl.ds(h * 256, 256)
        for o in range(x0.shape[0] // 32):
            block = [x[32 * o : 32 * o + 32, cols] for x in (x0, x1, x2, x3)]
            value = mm3(w, halves(jnp.concatenate(block, 0)))
            f[h, 8 * o : 8 * o + 8] = value.reshape(8, NZ, 256)


def level_modes_of(xs, wh, wl, after):
    pairs, width = xs[0].shape
    return pl.pallas_call(
        modes_kernel,
        in_specs=[VMEM] * 7,
        out_specs=VMEM,
        out_shape=jax.ShapeDtypeStruct((width // 256, pairs // 4, NZ, 256), F32),
        compiler_params=grant(8),
        name="mode_values",
    )(*xs, wh, wl, after)


def level_kernel(
    x0, x1, x2, x3, upper, w2h, w2l, w4h, w4l, lam, eig, out0, out1, out2, out3, ends, f, work
):
    lev = lax.axis_index("lev")
    octets = x0.shape[0] // 32
    half = 8 * octets
    rows = 2 * half
    w2 = (w2h[lev], w2l[lev])
    w4 = (w4h[lev], w4l[lev])
    for h in range(x0.shape[1] // 256):
        cols = pl.ds(h * 256, 256)
        e = eig[pl.ds(lev * 2 + h, 1), :]
        r, gain = decay(lam[:, 0:1], e)
        for o in range(octets):
            block = [x[32 * o : 32 * o + 32, cols] for x in (x0, x1, x2, x3)]
            value = mm3(w2, halves(jnp.concatenate(block, 0)))
            f[8 * o : 8 * o + 8] = value.reshape(8, NZ, 256)

        def source(y):
            return f[y] if y < half else upper[h, y - half]

        up = jnp.zeros((NZ, 256), F32)
        down = jnp.zeros((NZ, 256), F32)
        for y in range(rows):
            up = r * up
            work[y] = up
            up = up + source(y)
        for y in reversed(range(rows)):
            down = source(y) + r * down
            work[y] = (work[y] + down) * gain
        place = pl.ds(h * NZ, NZ)
        ends[place, 0, :] = up[:, :LANES]
        ends[place, 1, :] = up[:, LANES:]
        ends[place, 2, :] = down[:, :LANES]
        ends[place, 3, :] = down[:, LANES:]
        for o in range(rows // 8):
            block = work[8 * o : 8 * o + 8].reshape(LANES, 256)
            value = mm3(w4, halves(block))
            for step, out in enumerate((out0, out1, out2, out3)):
                out[32 * o : 32 * o + 32, cols] = value[32 * step : 32 * step + 32]


def level_solve(xs, upper, weights, lam, eig):
    pairs, width = xs[0].shape
    rows = pairs // 2
    return pl.pallas_call(
        level_kernel,
        in_specs=[VMEM] * 11,
        out_specs=[VMEM] * 5,
        out_shape=[jax.ShapeDtypeStruct((4 * rows, width), F32)] * 4
        + [jax.ShapeDtypeStruct((2 * NZ, 4, LANES), F32)],
        scratch_shapes=[
            pltpu.VMEM((rows // 2, NZ, 256), F32),
            pltpu.VMEM((rows, NZ, 256), F32),
        ],
        compiler_params=grant(12),
        name="level_solve",
    )(*xs, upper, *weights, lam, eig)


def carry_kernel(ends, lam, eig, out):
    sections = ends.shape[0]
    j = lax.axis_index("rows")
    k = lax.rem(j, NZ)
    h = lax.div(j, NZ)
    e = eig[pl.ds(lax.axis_index("lev") * 2 + h, 1), :]
    r, _ = decay(lam[pl.ds(k, 1), 0:1], e)
    for _ in range(6):
        r = r * r
    row = lax.broadcasted_iota(jnp.int32, (4, LANES), 0)
    ratio = jnp.where(lax.rem(row, 2) == 0, r[:, :LANES], r[:, LANES:])
    whole = ratio
    for _ in range(5):
        whole = whole * whole
    scale = 1.0 / (1.0 - whole)
    up = jnp.zeros((4, LANES), F32)
    down = jnp.zeros((4, LANES), F32)
    for s in range(sections):
        up = ends[s] + ratio * up
        down = ends[sections - 1 - s] + ratio * down
    up = up * scale
    down = down * scale
    first = row < 2
    ups = []
    for s in range(sections):
        ups.append(up)
        up = ends[s] + ratio * up
    for s in reversed(range(sections)):
        value = jnp.where(first, ups[s], down)
        for section in range(4):
            out[s, section] = value
        down = ends[s] + ratio * down


def carries(ends, lam, eig):
    return pl.pallas_call(
        carry_kernel,
        in_specs=[VMEM] * 3,
        out_specs=VMEM,
        out_shape=jax.ShapeDtypeStruct((ends.shape[0], 4) + ends.shape[1:], F32),
        compiler_params=grant(4),
        name="section_carries",
    )(ends, lam, eig)


def shift(value, step):
    return lax.ppermute(value, "lev", [(i, (i + step) % 4) for i in range(4)])


def body(source, solid, couplings):
    full, edge, twiddle, eig, spread = host_tables()
    fh, fl = split_host(full)
    eh, el = split_host(edge)
    fth, ftl = split_host(full.T)
    eth, etl = split_host(edge.T)
    lam, modes, w2h, w2l, w4h, w4l = eigen(couplings)
    xs = []
    for half in (1, 0):
        parts = forward_x(source, solid, (spread, twiddle, fh, fl, eh, el), half)
        far = shift(parts[2], -2)
        xs.append([parts[0], shift(parts[1], -1), far, shift(parts[3], -3)])
    tables = decay_tables(lam, eig, source.shape[0] // 8)
    upper = level_modes_of(xs[0], w2h, w2l, tables[0])
    *parts, ends = level_solve(xs[1], upper, (w2h, w2l, w4h, w4l), lam, eig)
    specs = [parts[0]] + [shift(parts[step], step) for step in (1, 2, 3)]
    ends = lax.all_to_all(ends, "rows", 0, 0, tiled=True)
    ends = carries(ends, lam, eig).reshape(128, 4, LANES)
    ends = lax.all_to_all(ends, ("rows", "lev"), 0, 0, tiled=True).reshape(2, NZ, 4, 4, LANES)
    return inverse_x(specs, ends, modes, tables, (twiddle, fth, ftl, eth, etl))


def solution(mesh):
    return jax.shard_map(
        body,
        mesh=mesh,
        in_specs=(P("rows", "lev", None), P("rows", "lev", None), P()),
        out_specs=P("rows", "lev", None),
        check_vma=False,
    )
```
